32 devices in a mesh: dp: 4 (over y, x), seq: 8 (over z, core).
Axes of the slice: x: 2, y: 2, z: 4, core: 2. Of those that a mesh axis runs over, the one named last changes fastest.
Arguments:
- student_x: bfloat16 [4096, 4096], P(('dp', 'seq')), parts along dimension 0, may hold values from -60 to 60
- student_z: bfloat16 [4096, 4096], P(('dp', 'seq')), parts along dimension 0, may hold values from -6 to 6
- student_b: bfloat16 [4096, 1024], P(('dp', 'seq')), parts along dimension 0, may hold values from -0.5 to 0.5
- student_c: bfloat16 [4096, 1024], P(('dp', 'seq')), parts along dimension 0, may hold values from -6 to 6
- step_size: float32 [64, 4096], P(None, ('dp', 'seq')), parts along dimension 1, may hold values from 0 to 1
- decay_rate: float32 [64], replicated, may hold values from 0.5 to 2
- norm_gain: float32 [4096], replicated, may hold values from 0.5 to 1.5
- teacher_q: bfloat16 [4096, 4096], P(('dp', 'seq')), parts along dimension 0, may hold values from -140 to 140
- teacher_k: bfloat16 [4096, 1024], P(('dp', 'seq')), parts along dimension 0, may hold values from -7 to 7
- teacher_v: bfloat16 [4096, 1024], P(('dp', 'seq')), parts along dimension 0, may hold values from -6 to 6
Outputs:
- student_out: bfloat16 [4096, 4096], P(('dp', 'seq')), parts along dimension 0
- teacher_out: bfloat16 [4096, 4096], P(('dp', 'seq')), parts along dimension 0
The draws below stay inside these ranges and needn't reach their ends.
There are 4 independent parts, one for each index of `dp`. The reference program is written for one: setup_inputs(seed, part) draws one part's arguments, and reference() takes and returns one part's arrays. A program takes and returns all parts, laid end to end along the dimension named above; an argument that names none is the same for every part. Nothing has to cross between parts.
All inputs are finite; a program needn't handle non-finite values.
Results may differ from the reference program's by a relative error of at most 0.0075.
Values may be sent and summed in bfloat16 or wider, within the bound.
A program may use at most 256 MiB of HBM per device.

```python
import math
import jax
import jax.numpy as jnp
from jax import lax

LEARNER_COUNT = 64
HEAD_DIM = 64
STATE = 128
GROUPS = 8
Q_HEADS = 32
KV_HEADS = 8
HEAD_SIZE = 128
BLOCK = 128
TOK_DEV = 128
EXAMPLE_SPAN = 1024


def draw_student_x(key, part):
    key_base = jax.random.fold_in(key, 3)
    key_cols = jax.random.fold_in(key, 4)
    key_rows = jax.random.fold_in(key, 5)
    width = LEARNER_COUNT * HEAD_DIM
    starting_figure = jnp.clip(jax.random.normal(key_base, (EXAMPLE_SPAN, width), jnp.float32), -6.0, 6.0)
    columns = jnp.exp(jax.random.uniform(key_cols, (1, width), jnp.float32, 0.0, math.log(10.0)))
    rows = jnp.exp(jax.random.uniform(key_rows, (EXAMPLE_SPAN, 1), jnp.float32, 0.0, math.log(10.0)))
    return (starting_figure * columns * rows / 10.0).astype(jnp.bfloat16)


def draw_step_size(key, part):
    key_kind = jax.random.fold_in(key, 21)
    key_fast = jax.random.fold_in(key, 22)
    key_slow = jax.random.fold_in(key, 23)
    key_device = jax.random.fold_in(key, 24)
    key_rough = jax.random.fold_in(key, 25)
    lookup_tile_span = jax.random.fold_in(key, 26)
    key_amount = jax.random.fold_in(key, 27)
    fast_share = 0.5
    is_fast = jax.random.bernoulli(key_kind, fast_share, (LEARNER_COUNT, 1))
    fast_rate = jnp.exp(jax.random.uniform(key_fast, (LEARNER_COUNT, 1), jnp.float32, math.log(0.02), math.log(0.05)))
    slow_rate = jnp.exp(jax.random.uniform(key_slow, (LEARNER_COUNT, 1), jnp.float32, math.log(0.1), math.log(0.5))) / EXAMPLE_SPAN
    starting_figure = jnp.where(is_fast, fast_rate, slow_rate)
    segments = EXAMPLE_SPAN // TOK_DEV
    processor_factor = jnp.exp(jax.random.uniform(key_device, (LEARNER_COUNT, segments, 1), jnp.float32, math.log(0.5), math.log(2.0)))
    processor_factor = jnp.broadcast_to(processor_factor, (LEARNER_COUNT, segments, TOK_DEV)).reshape(LEARNER_COUNT, EXAMPLE_SPAN)
    approximate_guess = jax.random.uniform(key_rough, (LEARNER_COUNT, EXAMPLE_SPAN), jnp.float32, 0.5, 1.5)
    tile_groupings = jax.random.bernoulli(lookup_tile_span, 4.0 / EXAMPLE_SPAN, (LEARNER_COUNT, EXAMPLE_SPAN)).astype(jnp.float32)
    position_total = jax.random.uniform(key_amount, (LEARNER_COUNT, EXAMPLE_SPAN), jnp.float32, 0.25, 0.6)
    return starting_figure * processor_factor * approximate_guess + tile_groupings * position_total


def teacher_pair(key):
    key_query = jax.random.fold_in(key, 11)
    key_keys = jax.random.fold_in(key, 12)
    keys_flat = jnp.clip(jax.random.normal(key_keys, (EXAMPLE_SPAN, KV_HEADS * HEAD_SIZE), jnp.float32), -6.0, 6.0)
    queries = jnp.clip(jax.random.normal(key_query, (EXAMPLE_SPAN, Q_HEADS * HEAD_SIZE), jnp.float32), -6.0, 6.0)
    return (queries, keys_flat)


def draw_teacher_q(key, part):
    return teacher_pair(key)[0].astype(jnp.bfloat16)


def draw_teacher_k(key, part):
    return teacher_pair(key)[1].astype(jnp.bfloat16)


def level_of(rng, shape, pieces, smallest, top_value):
    def one(axis_at, parts):
        steps = jax.random.uniform(jax.random.fold_in(jax.random.fold_in(rng, 6), axis_at), (parts,), jnp.float32, smallest / len(pieces), top_value / len(pieces))
        return jnp.repeat(jnp.exp(steps), shape[axis_at] // parts).reshape((-1,) + (1,) * (len(shape) - axis_at - 1))

    gain = one(*pieces[0])
    for cut in pieces[1:]:
        gain = gain * one(*cut)
    return gain


def normal_values(stream_key, shape, scale, most, cuts=(), kind=jnp.bfloat16):
    entries = scale * jax.random.normal(stream_key, shape, jnp.float32)
    if cuts:
        entries = entries * level_of(stream_key, shape, cuts, -0.22, 0.18)
    return jnp.clip(entries, -most, most).astype(kind)


def setup_inputs(seed: int = 0, part: int = 0) -> dict:
    seeds = jax.random.split(jax.random.key(seed), 11)
    own_keys = jax.random.split(jax.random.fold_in(seeds[10], part), 11)
    student_x = draw_student_x(jax.random.fold_in(jax.random.fold_in(seeds[10], part), 71), part)
    student_z = normal_values(own_keys[1], (EXAMPLE_SPAN, LEARNER_COUNT * HEAD_DIM), 1.0, 6.0, ((0, 8),))
    student_b = normal_values(own_keys[2], (EXAMPLE_SPAN, GROUPS * STATE), STATE ** -0.5, 0.5, ((0, 8),))
    student_c = normal_values(own_keys[3], (EXAMPLE_SPAN, GROUPS * STATE), 1.0, 6.0, ((0, 8),))
    step_size = draw_step_size(jax.random.fold_in(jax.random.fold_in(seeds[10], part), 71), part)
    decay_rate = jnp.clip(jnp.exp(jax.random.uniform(seeds[5], (LEARNER_COUNT,), jnp.float32, math.log(0.5), math.log(2.0))), 0.5, 2.0)
    norm_gain = jnp.clip(1.0 + 0.1 * jax.random.normal(seeds[6], (LEARNER_COUNT * HEAD_DIM,), jnp.float32), 0.5, 1.5)
    teacher_q = draw_teacher_q(jax.random.fold_in(jax.random.fold_in(seeds[10], part), 71), part)
    teacher_k = draw_teacher_k(jax.random.fold_in(jax.random.fold_in(seeds[10], part), 71), part)
    teacher_v = normal_values(own_keys[9], (EXAMPLE_SPAN, KV_HEADS * HEAD_SIZE), 1.0, 6.0, ((0, 8),))
    return dict(student_x=student_x, student_z=student_z, student_b=student_b, student_c=student_c, step_size=step_size, decay_rate=decay_rate, norm_gain=norm_gain, teacher_q=teacher_q, teacher_k=teacher_k, teacher_v=teacher_v)


epsilon_norm = 1e-05
masked_score = -1e+30
HIGHEST = lax.Precision.HIGHEST

def block_pass(carry_state, block_inputs, decay_rate):
    x_block, b_block, c_block, step_block = block_inputs
    block_rows = x_block.shape[0]
    per_group = LEARNER_COUNT // GROUPS
    log_decay = -step_block * decay_rate[:, None]
    running = jnp.cumsum(log_decay, axis=1)
    b_three = b_block.reshape(block_rows, GROUPS, STATE).astype(jnp.float32)
    c_three = c_block.reshape(block_rows, GROUPS, STATE).astype(jnp.float32)
    x_four = x_block.reshape(block_rows, GROUPS, per_group, HEAD_DIM).astype(jnp.float32)
    products = jnp.einsum('tgn,sgn->gts', c_three, b_three, precision=HIGHEST)
    lower_mask = jnp.arange(block_rows)[:, None] >= jnp.arange(block_rows)[None, :]
    spread = running[:, :, None] - running[:, None, :]
    factor = jnp.exp(jnp.where(lower_mask[None], spread, masked_score))
    weights = (products[:, None] * factor.reshape(GROUPS, per_group, block_rows, block_rows)).astype(jnp.bfloat16)
    local_out = jnp.einsum('gkts,sgkp->tgkp', weights.astype(jnp.float32), x_four, precision=HIGHEST)
    state_four = carry_state.reshape(GROUPS, per_group, HEAD_DIM, STATE)
    carried = jnp.einsum('tgn,gkpn->tgkp', c_three, state_four, precision=HIGHEST)
    carried = carried * jnp.exp(running).T.reshape(block_rows, GROUPS, per_group, 1)
    tail_decay = jnp.exp(running[:, -1:] - running)
    scaled = x_four * tail_decay.T.reshape(block_rows, GROUPS, per_group, 1)
    fresh_state = jnp.einsum('sgkp,sgn->gkpn', scaled, b_three, precision=HIGHEST)
    new_state = jnp.exp(running[:, -1]).reshape(GROUPS, per_group, 1, 1) * state_four + fresh_state
    combined = (local_out + carried).reshape(block_rows, LEARNER_COUNT * HEAD_DIM)
    return (new_state.reshape(LEARNER_COUNT, HEAD_DIM, STATE), combined)

def student(student_x, student_z, student_b, student_c, step_size, decay_rate, norm_gain):
    block_count = EXAMPLE_SPAN // BLOCK
    blocks_in = (student_x.reshape(block_count, BLOCK, LEARNER_COUNT * HEAD_DIM), student_b.reshape(block_count, BLOCK, GROUPS * STATE), student_c.reshape(block_count, BLOCK, GROUPS * STATE), step_size.reshape(LEARNER_COUNT, block_count, BLOCK).transpose(1, 0, 2))

    def advance(carry_state, block_inputs):
        return block_pass(carry_state, block_inputs, decay_rate)
    zero_state = jnp.zeros((LEARNER_COUNT, HEAD_DIM, STATE), jnp.float32)
    _, block_outs = lax.scan(advance, zero_state, blocks_in)
    ssm_out = block_outs.reshape(EXAMPLE_SPAN, LEARNER_COUNT, HEAD_DIM)
    gated_out = ssm_out * jax.nn.silu(student_z.astype(jnp.float32)).reshape(EXAMPLE_SPAN, LEARNER_COUNT, HEAD_DIM)
    mean_square = lax.optimization_barrier(jnp.mean(gated_out * gated_out, axis=2, keepdims=True))
    normed = gated_out * lax.rsqrt(mean_square + epsilon_norm) * norm_gain.reshape(1, LEARNER_COUNT, HEAD_DIM)
    return normed.reshape(EXAMPLE_SPAN, LEARNER_COUNT * HEAD_DIM).astype(jnp.bfloat16)

def teacher(teacher_q, teacher_k, teacher_v):
    ratio = Q_HEADS // KV_HEADS
    query_rows = min(128, EXAMPLE_SPAN)
    block_count = EXAMPLE_SPAN // query_rows
    score_scale = 1.0 / HEAD_SIZE ** 0.5
    query_blocks = teacher_q.reshape(block_count, query_rows, KV_HEADS, ratio, HEAD_SIZE)
    keys_three = teacher_k.reshape(EXAMPLE_SPAN, KV_HEADS, HEAD_SIZE).astype(jnp.float32)
    values_three = teacher_v.reshape(EXAMPLE_SPAN, KV_HEADS, HEAD_SIZE).astype(jnp.float32)
    key_pos = jnp.arange(EXAMPLE_SPAN)

    def attend_rows(block_args):
        block_index, query_block = block_args
        scores = jnp.einsum('qgkd,sgd->qgks', query_block.astype(jnp.float32), keys_three, precision=HIGHEST) * score_scale
        query_pos = block_index * query_rows + jnp.arange(query_rows)
        visible = (key_pos[None, :] <= query_pos[:, None])[:, None, None, :]
        masked = jnp.where(visible, scores, masked_score)
        row_max = lax.optimization_barrier(jnp.max(masked, axis=3, keepdims=True))
        probabilities = jnp.where(visible, jnp.exp(masked - row_max), 0.0)
        row_total = lax.optimization_barrier(jnp.sum(probabilities, axis=3))
        low = probabilities.astype(jnp.bfloat16).astype(jnp.float32)
        weighted = jnp.einsum('qgks,sgd->qgkd', low, values_three, precision=HIGHEST)
        return (weighted / row_total[..., None]).astype(jnp.bfloat16)
    outputs = lax.map(attend_rows, (jnp.arange(block_count, dtype=jnp.int32), query_blocks))
    return outputs.reshape(EXAMPLE_SPAN, Q_HEADS * HEAD_SIZE)

def reference(student_x, student_z, student_b, student_c, step_size, decay_rate, norm_gain, teacher_q, teacher_k, teacher_v):
    student_out = student(student_x, student_z, student_b, student_c, step_size, decay_rate, norm_gain)
    teacher_out = teacher(teacher_q, teacher_k, teacher_v)
    return (student_out, teacher_out)
```

```python
import functools
import math

import jax
import jax.numpy as jnp
from jax import lax
from jax.experimental import pallas as pl
from jax.experimental.pallas import tpu as pltpu
from jax.sharding import PartitionSpec as P

GROUPS = 8
HEAD_SIZE = 128
BLOCK = 128
HALVES = 2

epsilon_norm = 1e-05
masked_score = -1e30
F32 = jnp.float32
BF16 = jnp.bfloat16
MESH = pl.DeviceIdType.MESH


def dot(a, b, ca=1, cb=0):
    return lax.dot_general(a, b, (((ca,), (cb,)), ((), ())), preferred_element_type=F32)


def kernel(
    n,
    x_hbm, z_hbm, b_hbm, c_hbm, step_hbm, rate_ref, gain_ref, q_hbm, k_hbm, v_hbm,
    so_ref, to_ref,
    x_ref, z_ref, b_ref, c_ref, step_ref, q_ref, kv_ref,
    cum_ref, csib_ref, ssm_ref, reach_ref, stl_ref, lout_ref, lsib_ref,
    raw_ref, st_ref, send_ref, out_ref,
    qt_ref, qtail_ref, acc_ref, max_ref, sum_ref, part_ref, stat_ref, tacc_ref,
    in_sem, kv_in, dn_send, dn_recv, sib_send, sib_recv, q_send, q_recv,
    r_send, r_recv, t_send, t_recv, s_send, s_recv, m_send, m_recv, l_send, l_recv,
    c_send, c_recv,
):
    me = lax.axis_index("seq")
    core = lax.rem(me, 2)
    chip = me // 2
    chips = n // 2
    sibling = me + 1 - 2 * core
    up = me - 2
    down = me + 2
    has_up = chip > 0
    has_down = chip < chips - 1
    is_tail = chip == chips - 1
    is_helper = chip == chips - 2
    relays = chip < chips - 2
    gets_keys = jnp.logical_and(has_up, has_down)

    tokens, width = x_ref.shape
    heads = step_ref.shape[0]
    per_group = heads // GROUPS
    head_width = width // heads
    gw = width // GROUPS
    half_width = gw // HALVES
    state_dim = b_ref.shape[1] // GROUPS
    kv_count = kv_ref.shape[0]
    qw = q_ref.shape[1] // kv_count
    ratio = qw // HEAD_SIZE
    lanes = 128
    pack = lanes // head_width
    pairs = per_group // pack
    half_pairs = pairs // HALVES
    scale = math.log2(math.e) / math.sqrt(HEAD_SIZE)

    def span(g, size):
        return pl.ds(pl.multiple_of(g * size, 128), size)

    def to_seq(device):
        return dict(device_id={"seq": device}, device_id_type=MESH)

    key_loads = []
    for g in range(kv_count):
        for i, source in enumerate((k_hbm, v_hbm)):
            key_loads.append(
                pltpu.make_async_copy(
                    source.at[:, g * HEAD_SIZE : (g + 1) * HEAD_SIZE],
                    kv_ref.at[g, core, chip, i],
                    kv_in.at[g, i],
                )
            )
    loads = [
        pltpu.make_async_copy(src, dst, in_sem.at[i])
        for i, (src, dst) in enumerate(
            (
                (step_hbm, step_ref), (q_hbm, q_ref),
                (b_hbm, b_ref), (c_hbm, c_ref), (x_hbm, x_ref), (z_hbm, z_ref),
            )
        )
    ]

    barrier = pltpu.get_barrier_semaphore()
    pl.semaphore_signal(barrier, inc=1, **to_seq(sibling))

    @pl.when(has_up)
    def _():
        pl.semaphore_signal(barrier, inc=1, **to_seq(up))

    @pl.when(has_down)
    def _():
        pl.semaphore_signal(barrier, inc=1, **to_seq(down))

    loads[0].start()
    for load in key_loads:
        load.start()
    for load in loads[1:]:
        load.start()

    def key_down(g, j):
        return pltpu.make_async_remote_copy(
            src_ref=kv_ref.at[g, core, j], dst_ref=kv_ref.at[g, core, j],
            send_sem=dn_send.at[g, j], recv_sem=dn_recv.at[g, j], **to_seq(down),
        )

    def key_side(g, j, parity):
        return pltpu.make_async_remote_copy(
            src_ref=kv_ref.at[g, parity, j], dst_ref=kv_ref.at[g, parity, j],
            send_sem=sib_send.at[g, j], recv_sem=sib_recv.at[g, j], **to_seq(sibling),
        )

    def query_up(g):
        return pltpu.make_async_remote_copy(
            src_ref=qt_ref.at[g], dst_ref=qtail_ref.at[g],
            send_sem=q_send.at[g], recv_sem=q_recv.at[g], **to_seq(up),
        )

    def part_down(g):
        return pltpu.make_async_remote_copy(
            src_ref=part_ref.at[g], dst_ref=part_ref.at[g],
            send_sem=r_send.at[g], recv_sem=r_recv.at[g], **to_seq(down),
        )

    def stat_down(g):
        return pltpu.make_async_remote_copy(
            src_ref=stat_ref.at[g], dst_ref=stat_ref.at[g],
            send_sem=t_send.at[g], recv_sem=t_recv.at[g], **to_seq(down),
        )

    def state_down(g):
        return pltpu.make_async_remote_copy(
            src_ref=out_ref.at[g], dst_ref=raw_ref.at[g],
            send_sem=s_send.at[g], recv_sem=s_recv.at[g], **to_seq(down),
        )

    def state_side(g, half):
        return pltpu.make_async_remote_copy(
            src_ref=send_ref.at[g], dst_ref=st_ref.at[g, half],
            send_sem=m_send.at[g], recv_sem=m_recv.at[g], **to_seq(sibling),
        )

    def local_side(g):
        return pltpu.make_async_remote_copy(
            src_ref=lout_ref.at[g], dst_ref=lsib_ref.at[g],
            send_sem=l_send.at[g], recv_sem=l_recv.at[g], **to_seq(sibling),
        )

    cum_side = pltpu.make_async_remote_copy(
        src_ref=cum_ref, dst_ref=csib_ref,
        send_sem=c_send.at[0], recv_sem=c_recv.at[0], **to_seq(sibling),
    )

    loads[0].wait()
    eye = lax.broadcasted_iota(jnp.int32, (heads, heads), 0) == lax.broadcasted_iota(
        jnp.int32, (heads, heads), 1
    )
    rate = jnp.sum(jnp.where(eye, rate_ref[...], 0.0), axis=1, keepdims=True)
    running = -step_ref[...] * rate
    position = lax.broadcasted_iota(jnp.int32, (heads, tokens), 1)
    shift = 1
    while shift < tokens:
        running = running + jnp.where(position >= shift, pltpu.roll(running, shift, 1), 0.0)
        shift *= 2
    cum_ref[...] = running

    for load in key_loads:
        load.wait()

    partners = 1 + has_up.astype(jnp.int32) + has_down.astype(jnp.int32)
    pl.semaphore_wait(barrier, partners)

    @pl.when(relays)
    def _():
        key_down(0, chip).start()

    cum_side.start()

    @pl.loop(0, kv_count)
    def _(g):
        key_side(g, chip, core).start()

    loads[1].wait()

    def transpose_queries(g):
        for h in range(ratio):
            piece = q_ref[:, pl.ds(pl.multiple_of(g * qw + h * HEAD_SIZE, 128), HEAD_SIZE)]
            qt_ref[g, :, h * HEAD_SIZE : (h + 1) * HEAD_SIZE] = piece.T

    @pl.loop(0, kv_count)
    def _(g):
        transpose_queries(g)

        @pl.when(is_tail)
        def _():
            query_up(g).start()

    @pl.when(jnp.logical_not(has_up))
    def _():
        raw_ref[...] = jnp.zeros_like(raw_ref)

    for load in loads[2:]:
        load.wait()

    key_at = lax.broadcasted_iota(jnp.int32, (tokens, tokens), 0)
    query_at = lax.broadcasted_iota(jnp.int32, (tokens, tokens), 1)
    lower = query_at <= key_at
    half = lax.broadcasted_iota(jnp.int32, (tokens, lanes), 1) // head_width
    row_half = lax.broadcasted_iota(jnp.int32, (1, lanes), 1) // head_width
    visible = lax.broadcasted_iota(jnp.int32, (2 * tokens, tokens), 0) <= (
        lax.broadcasted_iota(jnp.int32, (2 * tokens, tokens), 1) + core * tokens
    )

    def columns_of(g, p):
        return pl.ds(pl.multiple_of(g * gw + p * lanes, 128), lanes)

    def student_local(g):
        cum = cum_ref[pl.ds(pl.multiple_of(g * per_group, 8), per_group), :]
        cum_t = cum.T
        tail = jnp.exp(cum[:, tokens - 1 : tokens] - cum)
        b = b_ref[:, span(g, state_dim)]
        b_t = b.T.astype(F32)
        products = dot(c_ref[:, span(g, state_dim)], b, 1, 1)
        for p in range(pairs):
            x = x_ref[:, columns_of(g, p)].astype(F32)
            mixes = []
            adds = []
            sources = []
            reach = None
            for j in range(pack):
                h = p * pack + j
                column = jnp.broadcast_to(cum_t[:, h : h + 1], (tokens, lanes))
                difference = jnp.where(lower, column - cum[h : h + 1, :], masked_score)
                mixes.append((products * jnp.exp(difference)).astype(BF16))
                adds.append((b_t * tail[h : h + 1, :]).astype(BF16))
                sources.append(jnp.where(half == j, x, 0.0).astype(BF16))
                reach = column if j == 0 else jnp.where(half == j, column, reach)
            z = z_ref[:, columns_of(g, p)].astype(F32)
            gate = z / (1.0 + jnp.exp(-z))
            at = slice(p * lanes, (p + 1) * lanes)
            source = jnp.concatenate(sources, axis=0)
            ssm_ref[g, :, at] = gate * dot(jnp.concatenate(mixes, axis=1), source)
            reach_ref[g, :, at] = gate * jnp.exp(reach)
            stl_ref[g, :, at] = dot(jnp.concatenate(adds, axis=1), source)
        lout_ref[g] = stl_ref[g, :, span(1 - core, half_width)].astype(BF16)
        local_side(g).start()

    def chain(g):
        local_side(g).wait_recv()

        @pl.when(has_up)
        def _():
            state_down(g).wait_recv()

        rows = pl.ds(pl.multiple_of(g * per_group, 8), per_group)
        total_own = jnp.exp(cum_ref[rows, tokens - 1 : tokens])
        total_sib = jnp.exp(csib_ref[rows, tokens - 1 : tokens])

        def decay_of(total, p):
            decay = total[p * pack : p * pack + 1, :]
            for j in range(1, pack):
                decay = jnp.where(row_half == j, total[p * pack + j : p * pack + j + 1, :], decay)
            return decay

        for part in range(HALVES):

            @pl.when(core == part)
            def _():
                for i in range(half_pairs):
                    p = part * half_pairs + i
                    at = slice(i * lanes, (i + 1) * lanes)
                    own = (decay_of(total_own, p), stl_ref[g, :, p * lanes : (p + 1) * lanes])
                    other = (decay_of(total_sib, p), lsib_ref[g, :, at].astype(F32))
                    first, second = (own, other) if part == 0 else (other, own)
                    raw = raw_ref[g, :, at]
                    middle = raw.astype(F32) * first[0] + first[1]
                    out_ref[g, :, at] = (middle * second[0] + second[1]).astype(BF16)
                    middle = middle.astype(BF16)
                    st_ref[g, part, :, at] = raw if part == 0 else middle
                    send_ref[g, :, at] = middle if part == 0 else raw

        @pl.when(has_down)
        def _():
            state_down(g).start()

        state_side(g, core).start()

    mean_of = jnp.where(
        lax.broadcasted_iota(jnp.int32, (lanes, lanes), 0) // head_width
        == lax.broadcasted_iota(jnp.int32, (lanes, lanes), 1) // head_width,
        1.0 / head_width,
        0.0,
    ).astype(BF16)

    def student_finish(g):
        state_side(g, 1 - core).wait_recv()
        c = c_ref[:, span(g, state_dim)]
        for part in range(HALVES):
            carried = dot(c, st_ref[g, part])
            for i in range(half_pairs):
                p = part * half_pairs + i
                at = slice(p * lanes, (p + 1) * lanes)
                gated = ssm_ref[g, :, at] + reach_ref[g, :, at] * carried[:, i * lanes : (i + 1) * lanes]
                mean = dot((gated * gated).astype(BF16), mean_of)
                so_ref[:, columns_of(g, p)] = (
                    gated * lax.rsqrt(mean + epsilon_norm) * gain_ref[:, columns_of(g, p)]
                ).astype(BF16)

    def head_at(h):
        return slice(h * HEAD_SIZE, (h + 1) * HEAD_SIZE)

    def pass_over(keys, values, queries, mask=None):
        scores = dot(keys, queries)
        if mask is not None:
            scores = jnp.where(mask, scores, masked_score)
        top = jnp.max(scores, axis=0, keepdims=True)
        weight = jnp.exp2((scores - top) * scale)
        return top, jnp.sum(weight, axis=0, keepdims=True), dot(values, weight.astype(BF16), 0, 0)

    def join(first, second):
        top = jnp.maximum(first[0], second[0])
        one = jnp.exp2((first[0] - top) * scale)
        two = jnp.exp2((second[0] - top) * scale)
        return top, first[1] * one + second[1] * two, first[2] * one + second[2] * two

    def rows_of(g, kind, start, count):
        taken = kv_ref[g, :, pl.ds(start, count), kind]
        return taken.reshape(2 * count * tokens, HEAD_SIZE)

    def attend_own(g):
        key_side(g, chip, 1 - core).wait_recv()
        keys = rows_of(g, 0, chip, 1)
        values = rows_of(g, 1, chip, 1)
        for h in range(ratio):
            at = head_at(h)
            max_ref[g, :, at], sum_ref[g, :, at], acc_ref[g, :, at] = pass_over(
                keys, values, qt_ref[g, :, at], visible
            )

    def attend_earlier(g):
        @pl.loop(0, chip)
        def _(j):
            keys = rows_of(g, 0, j, 1)
            values = rows_of(g, 1, j, 1)
            for h in range(ratio):
                at = head_at(h)
                held = (max_ref[g, :, at], sum_ref[g, :, at], acc_ref[g, :, at])
                max_ref[g, :, at], sum_ref[g, :, at], acc_ref[g, :, at] = join(
                    held, pass_over(keys, values, qt_ref[g, :, at])
                )

    chunk = max(k for k in range(1, 4) if (chips - 1) % k == 0)
    chunks = (chips - 1) // chunk

    def attend_tail(g):
        def keep(at, result):
            top, total, acc = result
            stat_ref[g, 0:1, at] = top
            stat_ref[g, 1:2, at] = total
            part_ref[g, :, at] = (acc * (1.0 / total)).astype(BF16)

        keys = rows_of(g, 0, 0, chunk)
        values = rows_of(g, 1, 0, chunk)
        for h in range(ratio):
            at = head_at(h)
            result = pass_over(keys, values, qtail_ref[g, :, at])
            if chunks == 1:
                keep(at, result)
            else:
                stat_ref[g, 0:1, at], stat_ref[g, 1:2, at], tacc_ref[:, at] = result
        if chunks > 1:

            @pl.loop(1, chunks)
            def _(k):
                keys = rows_of(g, 0, k * chunk, chunk)
                values = rows_of(g, 1, k * chunk, chunk)
                for h in range(ratio):
                    at = head_at(h)
                    held = (stat_ref[g, 0:1, at], stat_ref[g, 1:2, at], tacc_ref[:, at])
                    stat_ref[g, 0:1, at], stat_ref[g, 1:2, at], tacc_ref[:, at] = join(
                        held, pass_over(keys, values, qtail_ref[g, :, at])
                    )

            for h in range(ratio):
                at = head_at(h)
                keep(at, (stat_ref[g, 0:1, at], stat_ref[g, 1:2, at], tacc_ref[:, at]))
        part_down(g).start()
        stat_down(g).start()

    def write_teacher(g, h, result):
        to_ref[:, pl.ds(pl.multiple_of(g * qw + h * HEAD_SIZE, 128), HEAD_SIZE)] = result.T.astype(BF16)

    def finish_teacher(g):
        for h in range(ratio):
            at = head_at(h)
            write_teacher(g, h, acc_ref[g, :, at] * (1.0 / sum_ref[g, :, at]))

    def merge_teacher(g):
        part_down(g).wait_recv()
        stat_down(g).wait_recv()
        for h in range(ratio):
            at = head_at(h)
            top = jnp.maximum(max_ref[g, :, at], stat_ref[g, 0:1, at])
            one = jnp.exp2((max_ref[g, :, at] - top) * scale)
            two = jnp.exp2((stat_ref[g, 0:1, at] - top) * scale) * stat_ref[g, 1:2, at]
            inverse = 1.0 / (sum_ref[g, :, at] * one + two)
            write_teacher(
                g, h,
                acc_ref[g, :, at] * (one * inverse) + part_ref[g, :, at].astype(F32) * (two * inverse),
            )

    cum_side.wait_recv()

    @pl.loop(0, GROUPS + 2)
    def _(r):
        live = r < GROUPS

        @pl.when(jnp.logical_and(relays, r + 1 < GROUPS))
        def _():
            key_down(r + 1, chip).start()

        @pl.when(live)
        def _():
            student_local(r)
            attend_own(r)

        @pl.when(jnp.logical_and(live, gets_keys))
        def _():
            @pl.loop(0, chip)
            def _(i):
                j = chip - 1 - i
                key_down(r, j).wait_recv()

                @pl.when(relays)
                def _():
                    key_down(r, j).start()

                key_side(r, j, core).start()

            @pl.loop(0, chip)
            def _(i):
                key_side(r, chip - 1 - i, 1 - core).wait_recv()

        @pl.when(jnp.logical_and(live, is_helper))
        def _():
            query_up(r).wait_recv()
            attend_tail(r)

        @pl.when(r >= 2)
        def _():
            student_finish(r - 2)

        behind = jnp.logical_and(r >= 1, r <= GROUPS)

        @pl.when(jnp.logical_and(behind, is_tail))
        def _():
            merge_teacher(r - 1)

        @pl.when(behind)
        def _():
            chain(r - 1)

        @pl.when(jnp.logical_and(live, has_down))
        def _():
            attend_earlier(r)
            finish_teacher(r)

    cum_side.wait_send()

    @pl.loop(0, GROUPS)
    def _(g):
        local_side(g).wait_send()
        state_side(g, core).wait_send()
        key_side(g, chip, core).wait_send()

        @pl.when(has_down)
        def _():
            state_down(g).wait_send()

        @pl.when(relays)
        def _():
            key_down(g, chip).wait_send()

        @pl.when(gets_keys)
        def _():
            @pl.loop(0, chip)
            def _(j):
                key_side(g, j, core).wait_send()

                @pl.when(relays)
                def _():
                    key_down(g, j).wait_send()

        @pl.when(is_helper)
        def _():
            part_down(g).wait_send()
            stat_down(g).wait_send()

        @pl.when(is_tail)
        def _():
            query_up(g).wait_send()


def store(s_ref, t_ref, s_out, t_out, sem):
    copies = [
        pltpu.make_async_copy(s_ref, s_out, sem.at[0]),
        pltpu.make_async_copy(t_ref, t_out, sem.at[1]),
    ]
    for copy in copies:
        copy.start()
    for copy in copies:
        copy.wait()


def on_device(
    student_x, student_z, student_b, student_c, step_size, decay_rate, norm_gain,
    teacher_q, teacher_k, teacher_v,
):
    n = lax.axis_size("seq")
    tokens, width = student_x.shape
    assert tokens == BLOCK and n % 2 == 0 and n >= 4
    gw = width // GROUPS
    state_dim = student_b.shape[1] // GROUPS
    kv_count = teacher_k.shape[1] // HEAD_SIZE
    assert kv_count == GROUPS
    qw = teacher_q.shape[1] // kv_count
    hbm = pl.BlockSpec(memory_space=pl.ANY)
    vmem = pl.BlockSpec(memory_space=pltpu.VMEM)
    dma = pltpu.SemaphoreType.DMA
    states = pltpu.VMEM((GROUPS, state_dim, gw // HALVES), BF16)
    queries = pltpu.VMEM((kv_count, HEAD_SIZE, qw), BF16)
    results = pl.pallas_call(
        functools.partial(kernel, n),
        out_shape=(
            pltpu.VMEM(student_x.shape, BF16),
            pltpu.VMEM(teacher_q.shape, BF16),
        ),
        in_specs=[hbm, hbm, hbm, hbm, hbm, vmem, vmem, hbm, hbm, hbm],
        out_specs=(vmem, vmem),
        scratch_shapes=[
            pltpu.VMEM(student_x.shape, BF16),
            pltpu.VMEM(student_z.shape, BF16),
            pltpu.VMEM(student_b.shape, BF16),
            pltpu.VMEM(student_c.shape, BF16),
            pltpu.VMEM(step_size.shape, F32),
            pltpu.VMEM(teacher_q.shape, BF16),
            pltpu.VMEM((kv_count, 2, n // 2, 2, tokens, HEAD_SIZE), BF16),
            pltpu.VMEM(step_size.shape, F32),
            pltpu.VMEM(step_size.shape, F32),
            pltpu.VMEM((GROUPS, tokens, gw), F32),
            pltpu.VMEM((GROUPS, tokens, gw), F32),
            pltpu.VMEM((GROUPS, state_dim, gw), F32),
            states,
            states,
            states,
            pltpu.VMEM((GROUPS, HALVES, state_dim, gw // HALVES), BF16),
            states,
            states,
            queries,
            queries,
            pltpu.VMEM((kv_count, HEAD_SIZE, qw), F32),
            pltpu.VMEM((kv_count, 1, qw), F32),
            pltpu.VMEM((kv_count, 1, qw), F32),
            queries,
            pltpu.VMEM((kv_count, 2, qw), F32),
            pltpu.VMEM((HEAD_SIZE, qw), F32),
            dma((6,)),
            dma((kv_count, 2)),
            dma((kv_count, n // 2)),
            dma((kv_count, n // 2)),
            dma((kv_count, n // 2)),
            dma((kv_count, n // 2)),
        ]
        + [dma((GROUPS,))] * 12
        + [dma((1,))] * 2,
        compiler_params=pltpu.CompilerParams(
            collective_id=0, has_side_effects=True, vmem_limit_bytes=56 * 1024 * 1024
        ),
    )(
        student_x, student_z, student_b, student_c, step_size, decay_rate[None, :],
        norm_gain[None, :], teacher_q, teacher_k, teacher_v,
    )
    results = [pltpu.with_memory_space_constraint(r, pltpu.VMEM) for r in results]
    return pl.pallas_call(
        store,
        out_shape=(
            jax.ShapeDtypeStruct(student_x.shape, BF16),
            jax.ShapeDtypeStruct(teacher_q.shape, BF16),
        ),
        in_specs=[vmem, vmem],
        out_specs=(hbm, hbm),
        scratch_shapes=[dma((2,))],
    )(*results)


def solution(mesh):
    return jax.shard_map(
        on_device,
        mesh=mesh,
        in_specs=(
            P(("dp", "seq"), None),
            P(("dp", "seq"), None),
            P(("dp", "seq"), None),
            P(("dp", "seq"), None),
            P(None, ("dp", "seq")),
            P(),
            P(),
            P(("dp", "seq"), None),
            P(("dp", "seq"), None),
            P(("dp", "seq"), None),
        ),
        out_specs=(P(("dp", "seq"), None), P(("dp", "seq"), None)),
        check_vma=False,
    )
```

```python
import functools
import math

import jax
import jax.numpy as jnp
from jax import lax
from jax.experimental import pallas as pl
from jax.experimental.pallas import tpu as pltpu
from jax.sharding import PartitionSpec as P

GROUPS = 8
HEAD_SIZE = 128
BLOCK = 128
HALVES = 2
LEAD = 2
LAG = 2
OWN_LAG = 4
SKIPPED = 1

epsilon_norm = 1e-05
masked_score = -1e30
F32 = jnp.float32
BF16 = jnp.bfloat16
MESH = pl.DeviceIdType.MESH


def dot(a, b, ca=1, cb=0):
    return lax.dot_general(a, b, (((ca,), (cb,)), ((), ())), preferred_element_type=F32)


def kernel(
    n,
    x_hbm, z_hbm, b_hbm, c_hbm, step_hbm, rate_ref, gain_ref, q_hbm, k_hbm, v_hbm,
    so_ref, to_ref,
    x_ref, z_ref, b_ref, c_ref, step_ref, q_ref, kv_ref,
    cum_ref, csib_ref, ssm_ref, reach_ref, stl_ref, lout_ref, lsib_ref,
    raw_ref, st_ref, send_ref, out_ref,
    qt_ref, qtail_ref, acc_ref, max_ref, sum_ref, part_ref, stat_ref, tacc_ref,
    in_sem, kv_in, dn_send, dn_recv, sib_send, sib_recv, q_send, q_recv,
    r_send, r_recv, t_send, t_recv, s_send, s_recv, m_send, m_recv, l_send, l_recv,
    c_send, c_recv, lazy_send,
):
    me = lax.axis_index("seq")
    core = lax.rem(me, 2)
    chip = me // 2
    chips = n // 2
    sibling = me + 1 - 2 * core
    up = me - 2
    down = me + 2
    has_up = chip > 0
    has_down = chip < chips - 1
    is_tail = chip == chips - 1
    is_helper = chip == chips - 2
    feeds = chip < chips - 2
    relays = jnp.logical_and(has_up, feeds)
    skips = SKIPPED if chips == 4 else 0
    helper = 2 * (chips - 2) + core
    lag = jnp.where(feeds, 0, LAG)

    tokens, width = x_ref.shape
    heads = step_ref.shape[0]
    per_group = heads // GROUPS
    head_width = width // heads
    gw = width // GROUPS
    half_width = gw // HALVES
    state_dim = b_ref.shape[1] // GROUPS
    kv_count = kv_ref.shape[0]
    qw = q_ref.shape[1] // kv_count
    ratio = qw // HEAD_SIZE
    lanes = 128
    pack = lanes // head_width
    pairs = per_group // pack
    half_pairs = pairs // HALVES
    scale = math.log2(math.e) / math.sqrt(HEAD_SIZE)

    def span(g, size):
        return pl.ds(pl.multiple_of(g * size, 128), size)

    def to_seq(device):
        return dict(device_id={"seq": device}, device_id_type=MESH)

    key_loads = []
    for g in range(kv_count):
        for i, source in enumerate((k_hbm, v_hbm)):
            key_loads.append(
                pltpu.make_async_copy(
                    source.at[:, g * HEAD_SIZE : (g + 1) * HEAD_SIZE],
                    kv_ref.at[g, core, chip, i],
                    kv_in.at[g, i],
                )
            )
    loads = [
        pltpu.make_async_copy(src, dst, in_sem.at[i])
        for i, (src, dst) in enumerate(
            (
                (step_hbm, step_ref), (q_hbm, q_ref),
                (b_hbm, b_ref), (c_hbm, c_ref), (x_hbm, x_ref), (z_hbm, z_ref),
            )
        )
    ]
    skip_pairs = ((0, helper), (chips - 2, core)) if skips else ()

    barrier = pltpu.get_barrier_semaphore()
    pl.semaphore_signal(barrier, inc=1, **to_seq(sibling))

    @pl.when(has_up)
    def _():
        pl.semaphore_signal(barrier, inc=1, **to_seq(up))

    @pl.when(has_down)
    def _():
        pl.semaphore_signal(barrier, inc=1, **to_seq(down))

    for source, target in skip_pairs:

        @pl.when(chip == source)
        def _():
            pl.semaphore_signal(barrier, inc=1, **to_seq(target))

    loads[0].start()
    loads[1].start()
    for load in key_loads:
        load.start()
    for load in loads[2:]:
        load.start()

    def key_down(g, j):
        return pltpu.make_async_remote_copy(
            src_ref=kv_ref.at[g, core, j], dst_ref=kv_ref.at[g, core, j],
            send_sem=dn_send.at[g, j], recv_sem=dn_recv.at[g, j], **to_seq(down),
        )

    def key_skip(g, j):
        return pltpu.make_async_remote_copy(
            src_ref=kv_ref.at[g, core, j], dst_ref=kv_ref.at[g, core, j],
            send_sem=dn_send.at[g, j], recv_sem=dn_recv.at[g, j], **to_seq(helper),
        )

    def key_lazy(g, j):
        return pltpu.make_async_remote_copy(
            src_ref=kv_ref.at[g, core, j], dst_ref=kv_ref.at[g, core, j],
            send_sem=lazy_send.at[g], recv_sem=dn_recv.at[g, j], **to_seq(down),
        )

    def key_side(g, j, parity):
        return pltpu.make_async_remote_copy(
            src_ref=kv_ref.at[g, parity, j], dst_ref=kv_ref.at[g, parity, j],
            send_sem=sib_send.at[g, j], recv_sem=sib_recv.at[g, j], **to_seq(sibling),
        )

    def query_up(g):
        return pltpu.make_async_remote_copy(
            src_ref=qt_ref.at[g], dst_ref=qtail_ref.at[g],
            send_sem=q_send.at[g], recv_sem=q_recv.at[g], **to_seq(up),
        )

    def part_down(g):
        return pltpu.make_async_remote_copy(
            src_ref=part_ref.at[g], dst_ref=part_ref.at[g],
            send_sem=r_send.at[g], recv_sem=r_recv.at[g], **to_seq(down),
        )

    def stat_down(g):
        return pltpu.make_async_remote_copy(
            src_ref=stat_ref.at[g], dst_ref=stat_ref.at[g],
            send_sem=t_send.at[g], recv_sem=t_recv.at[g], **to_seq(down),
        )

    def state_down(g):
        return pltpu.make_async_remote_copy(
            src_ref=out_ref.at[g], dst_ref=raw_ref.at[g],
            send_sem=s_send.at[g], recv_sem=s_recv.at[g], **to_seq(down),
        )

    def state_side(g, half):
        return pltpu.make_async_remote_copy(
            src_ref=send_ref.at[g], dst_ref=st_ref.at[g, half],
            send_sem=m_send.at[g], recv_sem=m_recv.at[g], **to_seq(sibling),
        )

    def local_side(g):
        return pltpu.make_async_remote_copy(
            src_ref=lout_ref.at[g], dst_ref=lsib_ref.at[g],
            send_sem=l_send.at[g], recv_sem=l_recv.at[g], **to_seq(sibling),
        )

    cum_side = pltpu.make_async_remote_copy(
        src_ref=cum_ref, dst_ref=csib_ref,
        send_sem=c_send.at[0], recv_sem=c_recv.at[0], **to_seq(sibling),
    )

    loads[0].wait()
    eye = lax.broadcasted_iota(jnp.int32, (heads, heads), 0) == lax.broadcasted_iota(
        jnp.int32, (heads, heads), 1
    )
    rate = jnp.sum(jnp.where(eye, rate_ref[...], 0.0), axis=1, keepdims=True)
    running = -step_ref[...] * rate
    position = lax.broadcasted_iota(jnp.int32, (heads, tokens), 1)
    shift = 1
    while shift < tokens:
        running = running + jnp.where(position >= shift, pltpu.roll(running, shift, 1), 0.0)
        shift *= 2
    cum_ref[...] = running

    loads[1].wait()

    @pl.loop(0, kv_count)
    def _(g):
        for h in range(ratio):
            piece = q_ref[:, pl.ds(pl.multiple_of(g * qw + h * HEAD_SIZE, 128), HEAD_SIZE)]
            qt_ref[g, :, h * HEAD_SIZE : (h + 1) * HEAD_SIZE] = piece.T

    for load in key_loads:
        load.wait()

    partners = 1 + has_up.astype(jnp.int32) + has_down.astype(jnp.int32)
    for source, _ in skip_pairs:
        partners = partners + (chip == source).astype(jnp.int32)
    pl.semaphore_wait(barrier, partners)

    @pl.when(feeds)
    def _():
        for g in range(LEAD):
            if g < skips:

                @pl.when(chip == 0)
                def _():
                    key_skip(g, chip).start()

                @pl.when(has_up)
                def _():
                    key_down(g, chip).start()
            else:
                key_down(g, chip).start()

    @pl.when(is_tail)
    def _():
        @pl.loop(0, kv_count)
        def _(g):
            query_up(g).start()

    @pl.loop(0, kv_count)
    def _(g):
        key_side(g, chip, core).start()

    cum_side.start()

    @pl.when(jnp.logical_not(has_up))
    def _():
        raw_ref[...] = jnp.zeros_like(raw_ref)

    for load in loads[2:]:
        load.wait()

    key_at = lax.broadcasted_iota(jnp.int32, (tokens, tokens), 0)
    query_at = lax.broadcasted_iota(jnp.int32, (tokens, tokens), 1)
    lower = query_at <= key_at
    half = lax.broadcasted_iota(jnp.int32, (tokens, lanes), 1) // head_width
    row_half = lax.broadcasted_iota(jnp.int32, (1, lanes), 1) // head_width
    visible = lax.broadcasted_iota(jnp.int32, (2 * tokens, tokens), 0) <= (
        lax.broadcasted_iota(jnp.int32, (2 * tokens, tokens), 1) + core * tokens
    )

    def mask_last(scores):
        rows = scores.shape[0] // 2
        parts = []
        for parity in range(2):
            seen = visible[parity * tokens : (parity + 1) * tokens]
            part = scores[parity * rows : (parity + 1) * rows]
            parts += [part[: rows - tokens]] if rows > tokens else []
            parts.append(jnp.where(seen, part[rows - tokens :], masked_score))
        return jnp.concatenate(parts, axis=0)

    def columns_of(g, p):
        return pl.ds(pl.multiple_of(g * gw + p * lanes, 128), lanes)

    def student_local(g):
        cum = cum_ref[pl.ds(pl.multiple_of(g * per_group, 8), per_group), :]
        cum_t = cum.T
        tail = jnp.exp(cum[:, tokens - 1 : tokens] - cum)
        b = b_ref[:, span(g, state_dim)]
        b_t = b.T.astype(F32)
        products = dot(c_ref[:, span(g, state_dim)], b, 1, 1)
        for p in range(pairs):
            x = x_ref[:, columns_of(g, p)].astype(F32)
            mixes = []
            adds = []
            sources = []
            reach = None
            for j in range(pack):
                h = p * pack + j
                column = jnp.broadcast_to(cum_t[:, h : h + 1], (tokens, lanes))
                difference = jnp.where(lower, column - cum[h : h + 1, :], masked_score)
                mixes.append((products * jnp.exp(difference)).astype(BF16))
                adds.append((b_t * tail[h : h + 1, :]).astype(BF16))
                sources.append(jnp.where(half == j, x, 0.0).astype(BF16))
                reach = column if j == 0 else jnp.where(half == j, column, reach)
            z = z_ref[:, columns_of(g, p)].astype(F32)
            gate = z / (1.0 + jnp.exp(-z))
            at = slice(p * lanes, (p + 1) * lanes)
            source = jnp.concatenate(sources, axis=0)
            ssm_ref[g, :, at] = gate * dot(jnp.concatenate(mixes, axis=1), source)
            reach_ref[g, :, at] = gate * jnp.exp(reach)
            stl_ref[g, :, at] = dot(jnp.concatenate(adds, axis=1), source)
        lout_ref[g] = stl_ref[g, :, span(1 - core, half_width)].astype(BF16)
        local_side(g).start()

    def chain(g):
        local_side(g).wait_recv()

        @pl.when(has_up)
        def _():
            state_down(g).wait_recv()

        rows = pl.ds(pl.multiple_of(g * per_group, 8), per_group)
        total_own = jnp.exp(cum_ref[rows, tokens - 1 : tokens])
        total_sib = jnp.exp(csib_ref[rows, tokens - 1 : tokens])

        def decay_of(total, p):
            decay = total[p * pack : p * pack + 1, :]
            for j in range(1, pack):
                decay = jnp.where(row_half == j, total[p * pack + j : p * pack + j + 1, :], decay)
            return decay

        for part in range(HALVES):

            @pl.when(core == part)
            def _():
                for i in range(half_pairs):
                    p = part * half_pairs + i
                    at = slice(i * lanes, (i + 1) * lanes)
                    own = (decay_of(total_own, p), stl_ref[g, :, p * lanes : (p + 1) * lanes])
                    other = (decay_of(total_sib, p), lsib_ref[g, :, at].astype(F32))
                    first, second = (own, other) if part == 0 else (other, own)
                    raw = raw_ref[g, :, at]
                    middle = raw.astype(F32) * first[0] + first[1]
                    out_ref[g, :, at] = (middle * second[0] + second[1]).astype(BF16)
                    middle = middle.astype(BF16)
                    st_ref[g, part, :, at] = raw if part == 0 else middle
                    send_ref[g, :, at] = middle if part == 0 else raw

        @pl.when(has_down)
        def _():
            state_down(g).start()

        state_side(g, core).start()

    mean_of = jnp.where(
        lax.broadcasted_iota(jnp.int32, (lanes, lanes), 0) // head_width
        == lax.broadcasted_iota(jnp.int32, (lanes, lanes), 1) // head_width,
        1.0 / head_width,
        0.0,
    ).astype(BF16)

    def student_finish(g):
        state_side(g, 1 - core).wait_recv()
        c = c_ref[:, span(g, state_dim)]
        for part in range(HALVES):
            carried = dot(c, st_ref[g, part])
            for i in range(half_pairs):
                p = part * half_pairs + i
                at = slice(p * lanes, (p + 1) * lanes)
                gated = ssm_ref[g, :, at] + reach_ref[g, :, at] * carried[:, i * lanes : (i + 1) * lanes]
                mean = dot((gated * gated).astype(BF16), mean_of)
                so_ref[:, columns_of(g, p)] = (
                    gated * lax.rsqrt(mean + epsilon_norm) * gain_ref[:, columns_of(g, p)]
                ).astype(BF16)

    def head_at(h):
        return slice(h * HEAD_SIZE, (h + 1) * HEAD_SIZE)

    def pass_over(keys, values, queries, mask=None):
        scores = dot(keys, queries)
        if mask is not None:
            scores = mask(scores)
        top = jnp.max(scores, axis=0, keepdims=True)
        weight = jnp.exp2((scores - top) * scale)
        return top, jnp.sum(weight, axis=0, keepdims=True), dot(values, weight.astype(BF16), 0, 0)

    def join(first, second):
        top = jnp.maximum(first[0], second[0])
        one = jnp.exp2((first[0] - top) * scale)
        two = jnp.exp2((second[0] - top) * scale)
        return top, first[1] * one + second[1] * two, first[2] * one + second[2] * two

    def rows_of(g, kind, start, count):
        taken = kv_ref[g, :, pl.ds(start, count), kind]
        return taken.reshape(2 * count * tokens, HEAD_SIZE)

    def attend_own(g):
        keys = rows_of(g, 0, chip, 1)
        values = rows_of(g, 1, chip, 1)
        for h in range(ratio):
            at = head_at(h)
            max_ref[g, :, at], sum_ref[g, :, at], acc_ref[g, :, at] = pass_over(
                keys, values, qt_ref[g, :, at], mask_last
            )

    def attend_earlier(g):
        @pl.loop(0, chip)
        def _(j):
            keys = rows_of(g, 0, j, 1)
            values = rows_of(g, 1, j, 1)
            for h in range(ratio):
                at = head_at(h)
                held = (max_ref[g, :, at], sum_ref[g, :, at], acc_ref[g, :, at])
                max_ref[g, :, at], sum_ref[g, :, at], acc_ref[g, :, at] = join(
                    held, pass_over(keys, values, qt_ref[g, :, at])
                )

    chunk = max(k for k in range(1, 4) if (chips - 1) % k == 0)
    chunks = (chips - 1) // chunk

    def attend_tail(g):
        def keep(h, at, result):
            top, total, acc = result
            stat_ref[g, 0:1, at] = top
            stat_ref[g, 1:2, at] = total
            part_ref[g, h] = (acc * (1.0 / total)).astype(BF16)

        keys = rows_of(g, 0, 0, chunk)
        values = rows_of(g, 1, 0, chunk)
        for h in range(ratio):
            at = head_at(h)
            result = pass_over(keys, values, qtail_ref[g, :, at])
            if chunks == 1:
                keep(h, at, result)
            else:
                stat_ref[g, 0:1, at], stat_ref[g, 1:2, at], tacc_ref[:, at] = result
        if chunks > 1:

            @pl.loop(1, chunks)
            def _(k):
                keys = rows_of(g, 0, k * chunk, chunk)
                values = rows_of(g, 1, k * chunk, chunk)
                for h in range(ratio):
                    at = head_at(h)
                    held = (stat_ref[g, 0:1, at], stat_ref[g, 1:2, at], tacc_ref[:, at])
                    stat_ref[g, 0:1, at], stat_ref[g, 1:2, at], tacc_ref[:, at] = join(
                        held, pass_over(keys, values, qtail_ref[g, :, at])
                    )

            for h in range(ratio):
                at = head_at(h)
                keep(h, at, (stat_ref[g, 0:1, at], stat_ref[g, 1:2, at], tacc_ref[:, at]))
        part_down(g).start()
        stat_down(g).start()

    def attend_all(g):
        if chunks > 1:
            attend_own(g)
            attend_earlier(g)
            finish_teacher(g)
        else:
            keys = rows_of(g, 0, 0, chunk)
            values = rows_of(g, 1, 0, chunk)
            for h in range(ratio):
                _, total, acc = pass_over(keys, values, qt_ref[g, :, head_at(h)], mask_last)
                write_teacher(g, h, acc * (1.0 / total))

    def write_teacher(g, h, result):
        to_ref[:, pl.ds(pl.multiple_of(g * qw + h * HEAD_SIZE, 128), HEAD_SIZE)] = result.T.astype(BF16)

    def finish_teacher(g):
        for h in range(ratio):
            at = head_at(h)
            write_teacher(g, h, acc_ref[g, :, at] * (1.0 / sum_ref[g, :, at]))

    def merge_teacher(g):
        part_down(g).wait_recv()
        stat_down(g).wait_recv()
        for h in range(ratio):
            at = head_at(h)
            top = jnp.maximum(max_ref[g, :, at], stat_ref[g, 0:1, at])
            one = jnp.exp2((max_ref[g, :, at] - top) * scale)
            two = jnp.exp2((stat_ref[g, 0:1, at] - top) * scale) * stat_ref[g, 1:2, at]
            inverse = 1.0 / (sum_ref[g, :, at] * one + two)
            write_teacher(
                g, h,
                acc_ref[g, :, at] * (one * inverse) + part_ref[g, h].astype(F32) * (two * inverse),
            )

    def take_keys(g, onward):
        @pl.loop(0, chip)
        def _(i):
            j = chip - 1 - i
            key_down(g, j).wait_recv()
            if onward:
                key_down(g, j).start()
            key_side(g, j, core).start()

    def attend_rest(g):
        @pl.loop(0, chip)
        def _(i):
            key_side(g, chip - 1 - i, 1 - core).wait_recv()

        attend_earlier(g)
        finish_teacher(g)

    cum_side.wait_recv()
    final = GROUPS - 1

    student_local(0)

    @pl.loop(0, GROUPS + 1)
    def _(r):
        live = r < GROUPS

        @pl.when(relays)
        def _():
            @pl.loop(jnp.where(r == 0, skips, r + 1), jnp.minimum(r + 2, GROUPS))
            def _(g):
                take_keys(g, True)

        @pl.when(jnp.logical_and(live, is_helper))
        def _():
            take_keys(r, False)

        @pl.when(r < final)
        def _():
            student_local(r + 1)

        @pl.loop(jnp.maximum(r - lag - 1, 0), jnp.where(live, jnp.maximum(r - lag, 0), GROUPS))
        def _(g):
            student_finish(g)

        @pl.when(jnp.logical_and(is_tail, r >= 1))
        def _():
            merge_teacher(r - 1)

        @pl.loop(
            jnp.where(live, jnp.maximum(r - lag, 0), GROUPS),
            jnp.where(r < final, jnp.maximum(r - lag + 1, 0), GROUPS),
        )
        def _(g):
            chain(g)

        @pl.when(jnp.logical_and(feeds, r + LEAD < GROUPS))
        def _():
            key_down(r + LEAD, chip).start()

        @pl.when(live)
        def _():
            key_side(r, chip, 1 - core).wait_recv()

            @pl.when(is_helper)
            def _():
                @pl.loop(0, chip)
                def _(i):
                    key_side(r, chip - 1 - i, 1 - core).wait_recv()

                query_up(r).wait_recv()
                attend_tail(r)

            @pl.when(jnp.logical_not(is_helper))
            def _():
                attend_own(r)

            @pl.when(jnp.logical_not(has_up))
            def _():
                @pl.when(jnp.logical_not(is_helper))
                def _():
                    finish_teacher(r)

        @pl.when(is_helper)
        def _():
            @pl.loop(jnp.where(live, jnp.maximum(r - OWN_LAG, 0), GROUPS - OWN_LAG), jnp.where(live, jnp.maximum(r - OWN_LAG + 1, 0), GROUPS))
            def _(g):
                attend_all(g)

    if skips:

        @pl.when(chip == 0)
        def _():
            for g in range(skips):
                key_lazy(g, chip).start()

    @pl.when(relays)
    def _():
        for g in range(skips):
            take_keys(g, False)

        @pl.loop(0, GROUPS)
        def _(g):
            attend_rest(g)

    cum_side.wait_send()
    if skips:

        @pl.when(chip == 0)
        def _():
            for g in range(skips):
                key_lazy(g, chip).wait_send()

    @pl.loop(0, GROUPS)
    def _(g):
        local_side(g).wait_send()
        state_side(g, core).wait_send()
        key_side(g, chip, core).wait_send()

        @pl.when(has_down)
        def _():
            state_down(g).wait_send()

        @pl.when(feeds)
        def _():
            key_down(g, chip).wait_send()

        @pl.when(jnp.logical_and(has_up, has_down))
        def _():
            @pl.loop(0, chip)
            def _(j):
                key_side(g, j, core).wait_send()

        @pl.when(jnp.logical_and(relays, g >= skips))
        def _():
            @pl.loop(0, chip)
            def _(j):
                key_down(g, j).wait_send()

        @pl.when(is_helper)
        def _():
            part_down(g).wait_send()
            stat_down(g).wait_send()

        @pl.when(is_tail)
        def _():
            query_up(g).wait_send()


def store(s_ref, t_ref, s_out, t_out, sem):
    copies = [
        pltpu.make_async_copy(s_ref, s_out, sem.at[0]),
        pltpu.make_async_copy(t_ref, t_out, sem.at[1]),
    ]
    for copy in copies:
        copy.start()
    for copy in copies:
        copy.wait()


def on_device(
    student_x, student_z, student_b, student_c, step_size, decay_rate, norm_gain,
    teacher_q, teacher_k, teacher_v,
):
    n = lax.axis_size("seq")
    tokens, width = student_x.shape
    assert tokens == BLOCK and n % 2 == 0 and n >= 4
    gw = width // GROUPS
    state_dim = student_b.shape[1] // GROUPS
    kv_count = teacher_k.shape[1] // HEAD_SIZE
    assert kv_count == GROUPS
    qw = teacher_q.shape[1] // kv_count
    hbm = pl.BlockSpec(memory_space=pl.ANY)
    vmem = pl.BlockSpec(memory_space=pltpu.VMEM)
    dma = pltpu.SemaphoreType.DMA
    states = pltpu.VMEM((GROUPS, state_dim, gw // HALVES), BF16)
    queries = pltpu.VMEM((kv_count, HEAD_SIZE, qw), BF16)
    results = pl.pallas_call(
        functools.partial(kernel, n),
        out_shape=(
            pltpu.VMEM(student_x.shape, BF16),
            pltpu.VMEM(teacher_q.shape, BF16),
        ),
        in_specs=[hbm, hbm, hbm, hbm, hbm, vmem, vmem, hbm, hbm, hbm],
        out_specs=(vmem, vmem),
        scratch_shapes=[
            pltpu.VMEM(student_x.shape, BF16),
            pltpu.VMEM(student_z.shape, BF16),
            pltpu.VMEM(student_b.shape, BF16),
            pltpu.VMEM(student_c.shape, BF16),
            pltpu.VMEM(step_size.shape, F32),
            pltpu.VMEM(teacher_q.shape, BF16),
            pltpu.VMEM((kv_count, 2, n // 2, 2, tokens, HEAD_SIZE), BF16),
            pltpu.VMEM(step_size.shape, F32),
            pltpu.VMEM(step_size.shape, F32),
            pltpu.VMEM((GROUPS, tokens, gw), F32),
            pltpu.VMEM((GROUPS, tokens, gw), F32),
            pltpu.VMEM((GROUPS, state_dim, gw), F32),
            states,
            states,
            states,
            pltpu.VMEM((GROUPS, HALVES, state_dim, gw // HALVES), BF16),
            states,
            states,
            queries,
            queries,
            pltpu.VMEM((kv_count, HEAD_SIZE, qw), F32),
            pltpu.VMEM((kv_count, 1, qw), F32),
            pltpu.VMEM((kv_count, 1, qw), F32),
            pltpu.VMEM((kv_count, qw // HEAD_SIZE, HEAD_SIZE, HEAD_SIZE), BF16),
            pltpu.VMEM((kv_count, 2, qw), F32),
            pltpu.VMEM((HEAD_SIZE, qw), F32),
            dma((6,)),
            dma((kv_count, 2)),
            dma((kv_count, n // 2)),
            dma((kv_count, n // 2)),
            dma((kv_count, n // 2)),
            dma((kv_count, n // 2)),
        ]
        + [dma((GROUPS,))] * 12
        + [dma((1,))] * 2
        + [dma((GROUPS,))],
        compiler_params=pltpu.CompilerParams(
            collective_id=0, has_side_effects=True, vmem_limit_bytes=56 * 1024 * 1024
        ),
    )(
        student_x, student_z, student_b, student_c, step_size, decay_rate[None, :],
        norm_gain[None, :], teacher_q, teacher_k, teacher_v,
    )
    results = [pltpu.with_memory_space_constraint(r, pltpu.VMEM) for r in results]
    return pl.pallas_call(
        store,
        out_shape=(
            jax.ShapeDtypeStruct(student_x.shape, BF16),
            jax.ShapeDtypeStruct(teacher_q.shape, BF16),
        ),
        in_specs=[vmem, vmem],
        out_specs=(hbm, hbm),
        scratch_shapes=[dma((2,))],
    )(*results)


def solution(mesh):
    return jax.shard_map(
        on_device,
        mesh=mesh,
        in_specs=(
            P(("dp", "seq"), None),
            P(("dp", "seq"), None),
            P(("dp", "seq"), None),
            P(("dp", "seq"), None),
            P(None, ("dp", "seq")),
            P(),
            P(),
            P(("dp", "seq"), None),
            P(("dp", "seq"), None),
            P(("dp", "seq"), None),
        ),
        out_specs=(P(("dp", "seq"), None), P(("dp", "seq"), None)),
        check_vma=False,
    )
```

```python
import functools
import math

import jax
import jax.numpy as jnp
from jax import lax
from jax.experimental import pallas as pl
from jax.experimental.pallas import tpu as pltpu
from jax.sharding import PartitionSpec as P

GROUPS = 8
HEAD_SIZE = 128
BLOCK = 128
HALVES = 2
LEAD = 2
LAG = 2
OWN_LAG = 4
SKIPPED = 1

epsilon_norm = 1e-05
masked_score = -1e30
F32 = jnp.float32
BF16 = jnp.bfloat16
MESH = pl.DeviceIdType.MESH


def dot(a, b, ca=1, cb=0):
    return lax.dot_general(a, b, (((ca,), (cb,)), ((), ())), preferred_element_type=F32)


def kernel(
    n,
    x_hbm, z_hbm, b_hbm, c_hbm, step_hbm, rate_hbm, gain_hbm, q_hbm, k_hbm, v_hbm,
    so_ref, to_ref,
    x_ref, z_ref, b_ref, c_ref, step_ref, rate_ref, gain_ref, q_ref, kv_ref,
    cum_ref, csib_ref, ssm_ref, reach_ref, stl_ref, lout_ref, lsib_ref,
    raw_ref, st_ref, send_ref, out_ref,
    qt_ref, qtail_ref, acc_ref, max_ref, sum_ref, part_ref, stat_ref, tacc_ref,
    in_sem, send_sem, relay_send, spread_send, keys_recv, spread_recv, back_recv, stat_recv,
    state_recv, start_recv, local_recv, once_recv,
):
    me = lax.axis_index("seq")
    core = lax.rem(me, 2)
    chip = me // 2
    chips = n // 2
    sibling = me + 1 - 2 * core
    up = me - 2
    down = me + 2
    has_up = chip > 0
    has_down = chip < chips - 1
    is_tail = chip == chips - 1
    is_helper = chip == chips - 2
    feeds = chip < chips - 2
    relays = jnp.logical_and(has_up, feeds)
    skips = SKIPPED if chips == 4 else 0
    helper = 2 * (chips - 2) + core
    lag = jnp.where(feeds, 0, LAG)

    tokens, width = x_ref.shape
    heads = step_ref.shape[0]
    per_group = heads // GROUPS
    head_width = width // heads
    gw = width // GROUPS
    half_width = gw // HALVES
    state_dim = b_ref.shape[1] // GROUPS
    kv_count = kv_ref.shape[0]
    qw = q_ref.shape[1] // kv_count
    ratio = qw // HEAD_SIZE
    lanes = 128
    pack = lanes // head_width
    pairs = per_group // pack
    half_pairs = pairs // HALVES
    scale = math.log2(math.e) / math.sqrt(HEAD_SIZE)

    def span(g, size):
        return pl.ds(pl.multiple_of(g * size, 128), size)

    def to_seq(device):
        return dict(device_id={"seq": device}, device_id_type=MESH)

    key_loads = []
    for g in range(kv_count):
        for i, source in enumerate((k_hbm, v_hbm)):
            key_loads.append(
                pltpu.make_async_copy(
                    source.at[:, g * HEAD_SIZE : (g + 1) * HEAD_SIZE],
                    kv_ref.at[g, core, chip, i],
                    in_sem.at[0],
                )
            )
    own_keys = kv_ref.at[:, core, chip]
    all_keys = pltpu.make_async_copy(own_keys, own_keys, in_sem.at[0])
    loads = [
        pltpu.make_async_copy(src, dst, in_sem.at[i + 1])
        for i, (src, dst) in enumerate(
            (
                (step_hbm, step_ref), (rate_hbm, rate_ref), (q_hbm, q_ref),
                (b_hbm, b_ref), (c_hbm, c_ref), (x_hbm, x_ref), (z_hbm, z_ref), (gain_hbm, gain_ref),
            )
        )
    ]
    skip_pairs = ((0, helper), (chips - 2, core)) if skips else ()

    barrier = pltpu.get_barrier_semaphore()
    pl.semaphore_signal(barrier, inc=1, **to_seq(sibling))

    @pl.when(has_up)
    def _():
        pl.semaphore_signal(barrier, inc=1, **to_seq(up))

    @pl.when(has_down)
    def _():
        pl.semaphore_signal(barrier, inc=1, **to_seq(down))

    for source, target in skip_pairs:

        @pl.when(chip == source)
        def _():
            pl.semaphore_signal(barrier, inc=1, **to_seq(target))

    loads[0].start()
    loads[1].start()
    for load in key_loads:
        load.start()
    for load in loads[2:]:
        load.start()

    def remote(source, target, sent, got, device):
        return pltpu.make_async_remote_copy(
            src_ref=source, dst_ref=target, send_sem=sent, recv_sem=got, **to_seq(device)
        )

    def key_own(g, device):
        block = kv_ref.at[g, core, chip]
        return remote(block, block, send_sem.at[0], keys_recv.at[g, chip], device)

    def key_relay(g, j):
        block = kv_ref.at[g, core, j]
        return remote(block, block, relay_send.at[j], keys_recv.at[g, j], down)

    def key_lazy(g):
        block = kv_ref.at[g, core, chip]
        return remote(block, block, send_sem.at[1], keys_recv.at[g, chip], down)

    def key_side(parity):
        block = kv_ref.at[:, parity, chip]
        return remote(block, block, send_sem.at[2], once_recv.at[0], sibling)

    def key_spread(g, j, parity):
        block = kv_ref.at[g, parity, j]
        return remote(block, block, spread_send.at[j], spread_recv.at[g, j], sibling)

    def key_spread_all(g, parity):
        blocks = kv_ref.at[g, parity, 0 : chips - 2]
        return remote(blocks, blocks, spread_send.at[0], spread_recv.at[g, 0], sibling)

    def cum_side():
        return remote(cum_ref, csib_ref, send_sem.at[3], once_recv.at[1], sibling)

    def query_up(g):
        return remote(qt_ref.at[g], qtail_ref.at[g], send_sem.at[4], back_recv.at[g], up)

    def part_down(g):
        return remote(part_ref.at[g], part_ref.at[g], send_sem.at[4], back_recv.at[g], down)

    def stat_down(g):
        return remote(stat_ref.at[g], stat_ref.at[g], send_sem.at[5], stat_recv.at[g], down)

    def state_down(g):
        return remote(out_ref.at[g], raw_ref.at[g], send_sem.at[6], state_recv.at[g], down)

    def state_side(g, half):
        return remote(send_ref.at[g], st_ref.at[g, half], send_sem.at[7], start_recv.at[g], sibling)

    def local_side(g):
        return remote(lout_ref.at[g], lsib_ref.at[g], send_sem.at[8], local_recv.at[g], sibling)

    def sent(block, semaphore, device):
        remote(block, block, semaphore, once_recv.at[0], device).wait_send()

    loads[0].wait()
    loads[1].wait()
    eye = lax.broadcasted_iota(jnp.int32, (heads, heads), 0) == lax.broadcasted_iota(
        jnp.int32, (heads, heads), 1
    )
    rate = jnp.sum(jnp.where(eye, rate_ref[...], 0.0), axis=1, keepdims=True)
    running = -step_ref[...] * rate
    position = lax.broadcasted_iota(jnp.int32, (heads, tokens), 1)
    shift = 1
    while shift < tokens:
        running = running + jnp.where(position >= shift, pltpu.roll(running, shift, 1), 0.0)
        shift *= 2
    cum_ref[...] = running

    loads[2].wait()

    @pl.loop(0, kv_count)
    def _(g):
        for h in range(ratio):
            piece = q_ref[:, pl.ds(pl.multiple_of(g * qw + h * HEAD_SIZE, 128), HEAD_SIZE)]
            qt_ref[g, :, h * HEAD_SIZE : (h + 1) * HEAD_SIZE] = piece.T

    all_keys.wait()
    partners = 1 + has_up.astype(jnp.int32) + has_down.astype(jnp.int32)
    for source, _ in skip_pairs:
        partners = partners + (chip == source).astype(jnp.int32)
    pl.semaphore_wait(barrier, partners)

    @pl.when(feeds)
    def _():
        for g in range(LEAD):
            if g < skips:

                @pl.when(chip == 0)
                def _():
                    key_own(g, helper).start()

                @pl.when(has_up)
                def _():
                    key_own(g, down).start()
            else:
                key_own(g, down).start()

    @pl.when(is_tail)
    def _():
        @pl.loop(0, kv_count)
        def _(g):
            query_up(g).start()

    key_side(core).start()
    cum_side().start()

    @pl.when(jnp.logical_not(has_up))
    def _():
        raw_ref[...] = jnp.zeros_like(raw_ref)

    for load in loads[3:]:
        load.wait()

    key_at = lax.broadcasted_iota(jnp.int32, (tokens, tokens), 0)
    query_at = lax.broadcasted_iota(jnp.int32, (tokens, tokens), 1)
    lower = query_at <= key_at
    half = lax.broadcasted_iota(jnp.int32, (tokens, lanes), 1) // head_width
    row_half = lax.broadcasted_iota(jnp.int32, (1, lanes), 1) // head_width
    visible = lax.broadcasted_iota(jnp.int32, (2 * tokens, tokens), 0) <= (
        lax.broadcasted_iota(jnp.int32, (2 * tokens, tokens), 1) + core * tokens
    )

    def mask_last(scores):
        rows = scores.shape[0] // 2
        parts = []
        for parity in range(2):
            seen = visible[parity * tokens : (parity + 1) * tokens]
            part = scores[parity * rows : (parity + 1) * rows]
            parts += [part[: rows - tokens]] if rows > tokens else []
            parts.append(jnp.where(seen, part[rows - tokens :], masked_score))
        return jnp.concatenate(parts, axis=0)

    def columns_of(g, p):
        return pl.ds(pl.multiple_of(g * gw + p * lanes, 128), lanes)

    def student_local(g):
        cum = cum_ref[pl.ds(pl.multiple_of(g * per_group, 8), per_group), :]
        cum_t = cum.T
        tail = jnp.exp(cum[:, tokens - 1 : tokens] - cum)
        b = b_ref[:, span(g, state_dim)]
        b_t = b.T.astype(F32)
        products = dot(c_ref[:, span(g, state_dim)], b, 1, 1)
        for p in range(pairs):
            x = x_ref[:, columns_of(g, p)].astype(F32)
            mixes = []
            adds = []
            sources = []
            reach = None
            for j in range(pack):
                h = p * pack + j
                column = jnp.broadcast_to(cum_t[:, h : h + 1], (tokens, lanes))
                difference = jnp.where(lower, column - cum[h : h + 1, :], masked_score)
                mixes.append((products * jnp.exp(difference)).astype(BF16))
                adds.append((b_t * tail[h : h + 1, :]).astype(BF16))
                sources.append(jnp.where(half == j, x, 0.0).astype(BF16))
                reach = column if j == 0 else jnp.where(half == j, column, reach)
            z = z_ref[:, columns_of(g, p)].astype(F32)
            gate = z / (1.0 + jnp.exp(-z))
            at = slice(p * lanes, (p + 1) * lanes)
            source = jnp.concatenate(sources, axis=0)
            ssm_ref[g, :, at] = gate * dot(jnp.concatenate(mixes, axis=1), source)
            reach_ref[g, :, at] = gate * jnp.exp(reach)
            stl_ref[g, :, at] = dot(jnp.concatenate(adds, axis=1), source)
        lout_ref[g] = stl_ref[g, :, span(1 - core, half_width)].astype(BF16)
        local_side(g).start()

    def chain(g):
        local_side(g).wait_recv()

        @pl.when(has_up)
        def _():
            state_down(g).wait_recv()

        rows = pl.ds(pl.multiple_of(g * per_group, 8), per_group)
        total_own = jnp.exp(cum_ref[rows, tokens - 1 : tokens])
        total_sib = jnp.exp(csib_ref[rows, tokens - 1 : tokens])

        def decay_of(total, p):
            decay = total[p * pack : p * pack + 1, :]
            for j in range(1, pack):
                decay = jnp.where(row_half == j, total[p * pack + j : p * pack + j + 1, :], decay)
            return decay

        for part in range(HALVES):

            @pl.when(core == part)
            def _():
                for i in range(half_pairs):
                    p = part * half_pairs + i
                    at = slice(i * lanes, (i + 1) * lanes)
                    own = (decay_of(total_own, p), stl_ref[g, :, p * lanes : (p + 1) * lanes])
                    other = (decay_of(total_sib, p), lsib_ref[g, :, at].astype(F32))
                    first, second = (own, other) if part == 0 else (other, own)
                    raw = raw_ref[g, :, at]
                    middle = raw.astype(F32) * first[0] + first[1]
                    out_ref[g, :, at] = (middle * second[0] + second[1]).astype(BF16)
                    middle = middle.astype(BF16)
                    st_ref[g, part, :, at] = raw if part == 0 else middle
                    send_ref[g, :, at] = middle if part == 0 else raw

        @pl.when(has_down)
        def _():
            state_down(g).start()

        state_side(g, core).start()

    mean_of = jnp.where(
        lax.broadcasted_iota(jnp.int32, (lanes, lanes), 0) // head_width
        == lax.broadcasted_iota(jnp.int32, (lanes, lanes), 1) // head_width,
        1.0 / head_width,
        0.0,
    ).astype(BF16)

    def student_finish(g):
        state_side(g, 1 - core).wait_recv()
        c = c_ref[:, span(g, state_dim)]
        for part in range(HALVES):
            carried = dot(c, st_ref[g, part])
            for i in range(half_pairs):
                p = part * half_pairs + i
                at = slice(p * lanes, (p + 1) * lanes)
                gated = ssm_ref[g, :, at] + reach_ref[g, :, at] * carried[:, i * lanes : (i + 1) * lanes]
                mean = dot((gated * gated).astype(BF16), mean_of)
                so_ref[:, columns_of(g, p)] = (
                    gated * lax.rsqrt(mean + epsilon_norm) * gain_ref[:, columns_of(g, p)]
                ).astype(BF16)

    def head_at(h):
        return slice(h * HEAD_SIZE, (h + 1) * HEAD_SIZE)

    def pass_over(keys, values, queries, mask=None):
        scores = dot(keys, queries)
        if mask is not None:
            scores = mask(scores)
        top = jnp.max(scores, axis=0, keepdims=True)
        weight = jnp.exp2((scores - top) * scale)
        return top, jnp.sum(weight, axis=0, keepdims=True), dot(values, weight.astype(BF16), 0, 0)

    def join(first, second):
        top = jnp.maximum(first[0], second[0])
        one = jnp.exp2((first[0] - top) * scale)
        two = jnp.exp2((second[0] - top) * scale)
        return top, first[1] * one + second[1] * two, first[2] * one + second[2] * two

    def rows_of(g, kind, start, count):
        taken = kv_ref[g, :, pl.ds(start, count), kind]
        return taken.reshape(2 * count * tokens, HEAD_SIZE)

    def attend_own(g):
        keys = rows_of(g, 0, chip, 1)
        values = rows_of(g, 1, chip, 1)
        for h in range(ratio):
            at = head_at(h)
            max_ref[g, :, at], sum_ref[g, :, at], acc_ref[g, :, at] = pass_over(
                keys, values, qt_ref[g, :, at], mask_last
            )

    def attend_earlier(g):
        @pl.loop(0, chip)
        def _(j):
            keys = rows_of(g, 0, j, 1)
            values = rows_of(g, 1, j, 1)
            for h in range(ratio):
                at = head_at(h)
                held = (max_ref[g, :, at], sum_ref[g, :, at], acc_ref[g, :, at])
                max_ref[g, :, at], sum_ref[g, :, at], acc_ref[g, :, at] = join(
                    held, pass_over(keys, values, qt_ref[g, :, at])
                )

    chunk = max(k for k in range(1, 4) if (chips - 1) % k == 0)
    chunks = (chips - 1) // chunk

    def attend_tail(g):
        def keep(h, at, result):
            top, total, acc = result
            stat_ref[g, 0:1, at] = top
            stat_ref[g, 1:2, at] = total
            part_ref[g, h] = (acc * (1.0 / total)).astype(BF16)

        keys = rows_of(g, 0, 0, chunk)
        values = rows_of(g, 1, 0, chunk)
        for h in range(ratio):
            at = head_at(h)
            result = pass_over(keys, values, qtail_ref[g, :, at])
            if chunks == 1:
                keep(h, at, result)
            else:
                stat_ref[g, 0:1, at], stat_ref[g, 1:2, at], tacc_ref[:, at] = result
        if chunks > 1:

            @pl.loop(1, chunks)
            def _(k):
                keys = rows_of(g, 0, k * chunk, chunk)
                values = rows_of(g, 1, k * chunk, chunk)
                for h in range(ratio):
                    at = head_at(h)
                    held = (stat_ref[g, 0:1, at], stat_ref[g, 1:2, at], tacc_ref[:, at])
                    stat_ref[g, 0:1, at], stat_ref[g, 1:2, at], tacc_ref[:, at] = join(
                        held, pass_over(keys, values, qtail_ref[g, :, at])
                    )

            for h in range(ratio):
                at = head_at(h)
                keep(h, at, (stat_ref[g, 0:1, at], stat_ref[g, 1:2, at], tacc_ref[:, at]))
        part_down(g).start()
        stat_down(g).start()

    def attend_all(g):
        if chunks > 1:
            attend_own(g)
            attend_earlier(g)
            finish_teacher(g)
        else:
            keys = rows_of(g, 0, 0, chunk)
            values = rows_of(g, 1, 0, chunk)
            for h in range(ratio):
                _, total, acc = pass_over(keys, values, qt_ref[g, :, head_at(h)], mask_last)
                write_teacher(g, h, acc * (1.0 / total))

    def write_teacher(g, h, result):
        to_ref[:, pl.ds(pl.multiple_of(g * qw + h * HEAD_SIZE, 128), HEAD_SIZE)] = result.T.astype(BF16)

    def finish_teacher(g):
        for h in range(ratio):
            at = head_at(h)
            write_teacher(g, h, acc_ref[g, :, at] * (1.0 / sum_ref[g, :, at]))

    def merge_teacher(g):
        part_down(g).wait_recv()
        stat_down(g).wait_recv()
        for h in range(ratio):
            at = head_at(h)
            top = jnp.maximum(max_ref[g, :, at], stat_ref[g, 0:1, at])
            one = jnp.exp2((max_ref[g, :, at] - top) * scale)
            two = jnp.exp2((stat_ref[g, 0:1, at] - top) * scale) * stat_ref[g, 1:2, at]
            inverse = 1.0 / (sum_ref[g, :, at] * one + two)
            write_teacher(
                g, h,
                acc_ref[g, :, at] * (one * inverse) + part_ref[g, h].astype(F32) * (two * inverse),
            )

    def take_keys(g, onward):
        @pl.loop(0, chip)
        def _(i):
            j = chip - 1 - i
            key_relay(g, j).wait_recv()
            if onward:
                key_relay(g, j).start()
            key_spread(g, j, core).start()

    def attend_rest(g):
        @pl.loop(0, chip)
        def _(i):
            key_spread(g, chip - 1 - i, 1 - core).wait_recv()

        attend_earlier(g)
        finish_teacher(g)

    cum_side().wait_recv()
    key_side(1 - core).wait_recv()
    final = GROUPS - 1

    student_local(0)

    @pl.loop(0, GROUPS + 1)
    def _(r):
        live = r < GROUPS

        @pl.when(relays)
        def _():
            @pl.loop(jnp.where(r == 0, skips, r + 1), jnp.minimum(r + 2, GROUPS))
            def _(g):
                take_keys(g, True)

        @pl.when(jnp.logical_and(live, is_helper))
        def _():
            @pl.loop(0, chip)
            def _(i):
                key_relay(r, chip - 1 - i).wait_recv()

            if chips > 2:
                key_spread_all(r, core).start()

        @pl.when(r < final)
        def _():
            student_local(r + 1)

        @pl.loop(jnp.maximum(r - lag - 1, 0), jnp.where(live, jnp.maximum(r - lag, 0), GROUPS))
        def _(g):
            student_finish(g)

        @pl.when(jnp.logical_and(is_tail, r >= 1))
        def _():
            merge_teacher(r - 1)

        @pl.loop(
            jnp.where(live, jnp.maximum(r - lag, 0), GROUPS),
            jnp.where(r < final, jnp.maximum(r - lag + 1, 0), GROUPS),
        )
        def _(g):
            chain(g)

        @pl.when(jnp.logical_and(feeds, r + LEAD < GROUPS))
        def _():
            key_own(r + LEAD, down).start()

        @pl.when(live)
        def _():
            @pl.when(is_helper)
            def _():
                if chips > 2:
                    key_spread_all(r, 1 - core).wait_recv()
                query_up(r).wait_recv()
                attend_tail(r)

            @pl.when(jnp.logical_not(is_helper))
            def _():
                attend_own(r)

            @pl.when(jnp.logical_not(has_up))
            def _():
                @pl.when(jnp.logical_not(is_helper))
                def _():
                    finish_teacher(r)

        @pl.when(is_helper)
        def _():
            @pl.loop(jnp.where(live, jnp.maximum(r - OWN_LAG, 0), GROUPS - OWN_LAG), jnp.where(live, jnp.maximum(r - OWN_LAG + 1, 0), GROUPS))
            def _(g):
                attend_all(g)

    if skips:

        @pl.when(chip == 0)
        def _():
            for g in range(skips):
                key_lazy(g).start()

    @pl.when(relays)
    def _():
        for g in range(skips):
            take_keys(g, False)

        @pl.loop(0, GROUPS)
        def _(g):
            attend_rest(g)

    sent(kv_ref.at[:, core, chip], send_sem.at[2], sibling)
    sent(cum_ref, send_sem.at[3], sibling)
    sent(send_ref, send_sem.at[7], sibling)
    sent(lout_ref, send_sem.at[8], sibling)

    @pl.when(has_down)
    def _():
        sent(out_ref, send_sem.at[6], down)

    @pl.when(feeds)
    def _():
        sent(kv_ref.at[:, core, chip], send_sem.at[0], down)

    if skips:

        @pl.when(chip == 0)
        def _():
            sent(kv_ref.at[0:skips, core, chip], send_sem.at[1], down)

    @pl.when(relays)
    def _():
        @pl.loop(0, chip)
        def _(j):
            sent(kv_ref.at[skips:, core, j], relay_send.at[j], down)
            sent(kv_ref.at[:, core, j], spread_send.at[j], sibling)

    @pl.when(is_helper)
    def _():
        if chips > 2:
            sent(kv_ref.at[:, core, 0 : chips - 2], spread_send.at[0], sibling)
        sent(part_ref, send_sem.at[4], down)
        sent(stat_ref, send_sem.at[5], down)

    @pl.when(is_tail)
    def _():
        sent(qt_ref, send_sem.at[4], up)


def store(s_ref, t_ref, s_out, t_out, sem):
    copies = [
        pltpu.make_async_copy(s_ref, s_out, sem.at[0]),
        pltpu.make_async_copy(t_ref, t_out, sem.at[1]),
    ]
    for copy in copies:
        copy.start()
    for copy in copies:
        copy.wait()


def on_device(
    student_x, student_z, student_b, student_c, step_size, decay_rate, norm_gain,
    teacher_q, teacher_k, teacher_v,
):
    n = lax.axis_size("seq")
    tokens, width = student_x.shape
    heads = step_size.shape[0]
    assert tokens == BLOCK and n % 2 == 0 and n >= 4
    gw = width // GROUPS
    state_dim = student_b.shape[1] // GROUPS
    kv_count = teacher_k.shape[1] // HEAD_SIZE
    assert kv_count == GROUPS
    qw = teacher_q.shape[1] // kv_count
    hbm = pl.BlockSpec(memory_space=pl.ANY)
    vmem = pl.BlockSpec(memory_space=pltpu.VMEM)
    dma = pltpu.SemaphoreType.DMA
    states = pltpu.VMEM((GROUPS, state_dim, gw // HALVES), BF16)
    queries = pltpu.VMEM((kv_count, HEAD_SIZE, qw), BF16)
    results = pl.pallas_call(
        functools.partial(kernel, n),
        out_shape=(
            pltpu.VMEM(student_x.shape, BF16),
            pltpu.VMEM(teacher_q.shape, BF16),
        ),
        in_specs=[hbm] * 10,
        out_specs=(vmem, vmem),
        scratch_shapes=[
            pltpu.VMEM(student_x.shape, BF16),
            pltpu.VMEM(student_z.shape, BF16),
            pltpu.VMEM(student_b.shape, BF16),
            pltpu.VMEM(student_c.shape, BF16),
            pltpu.VMEM(step_size.shape, F32),
            pltpu.VMEM((1, heads), F32),
            pltpu.VMEM((1, width), F32),
            pltpu.VMEM(teacher_q.shape, BF16),
            pltpu.VMEM((kv_count, 2, n // 2, 2, tokens, HEAD_SIZE), BF16),
            pltpu.VMEM(step_size.shape, F32),
            pltpu.VMEM(step_size.shape, F32),
            pltpu.VMEM((GROUPS, tokens, gw), F32),
            pltpu.VMEM((GROUPS, tokens, gw), F32),
            pltpu.VMEM((GROUPS, state_dim, gw), F32),
            states,
            states,
            states,
            pltpu.VMEM((GROUPS, HALVES, state_dim, gw // HALVES), BF16),
            states,
            states,
            queries,
            queries,
            pltpu.VMEM((kv_count, HEAD_SIZE, qw), F32),
            pltpu.VMEM((kv_count, 1, qw), F32),
            pltpu.VMEM((kv_count, 1, qw), F32),
            pltpu.VMEM((kv_count, qw // HEAD_SIZE, HEAD_SIZE, HEAD_SIZE), BF16),
            pltpu.VMEM((kv_count, 2, qw), F32),
            pltpu.VMEM((HEAD_SIZE, qw), F32),
            dma((9,)),
            dma((9,)),
            dma((max(n // 2 - 3, 1),)),
            dma((max(n // 2 - 3, 1),)),
            dma((kv_count, max(n // 2 - 2, 1))),
            dma((kv_count, max(n // 2 - 3, 1))),
        ]
        + [dma((GROUPS,))] * 5
        + [dma((2,))],
        compiler_params=pltpu.CompilerParams(
            collective_id=0, has_side_effects=True, vmem_limit_bytes=56 * 1024 * 1024
        ),
    )(
        student_x, student_z, student_b, student_c, step_size, decay_rate[None, :],
        norm_gain[None, :], teacher_q, teacher_k, teacher_v,
    )
    results = [pltpu.with_memory_space_constraint(r, pltpu.VMEM) for r in results]
    return pl.pallas_call(
        store,
        out_shape=(
            jax.ShapeDtypeStruct(student_x.shape, BF16),
            jax.ShapeDtypeStruct(teacher_q.shape, BF16),
        ),
        in_specs=[vmem, vmem],
        out_specs=(hbm, hbm),
        scratch_shapes=[dma((2,))],
    )(*results)


def solution(mesh):
    return jax.shard_map(
        on_device,
        mesh=mesh,
        in_specs=(
            P(("dp", "seq"), None),
            P(("dp", "seq"), None),
            P(("dp", "seq"), None),
            P(("dp", "seq"), None),
            P(None, ("dp", "seq")),
            P(),
            P(),
            P(("dp", "seq"), None),
            P(("dp", "seq"), None),
            P(("dp", "seq"), None),
        ),
        out_specs=(P(("dp", "seq"), None), P(("dp", "seq"), None)),
        check_vma=False,
    )
```

```python
import functools
import math

import jax
import jax.numpy as jnp
from jax import lax
from jax.experimental import pallas as pl
from jax.experimental.pallas import tpu as pltpu
from jax.sharding import PartitionSpec as P

GROUPS = 8
HEAD_SIZE = 128
BLOCK = 128
HALVES = 2
LEAD = 2
LAG = 1
OWN_LAG = 4
PIECES = 3
SKIPPED = 1

epsilon_norm = 1e-05
masked_score = -1e30
F32 = jnp.float32
BF16 = jnp.bfloat16
MESH = pl.DeviceIdType.MESH


def dot(a, b, ca=1, cb=0):
    return lax.dot_general(a, b, (((ca,), (cb,)), ((), ())), preferred_element_type=F32)


def rows_for(heads):
    return -(-heads * PIECES // 16) * 16


def kernel(
    n,
    x_hbm, z_hbm, b_hbm, c_hbm, step_hbm, rate_hbm, gain_hbm, q_hbm, k_hbm, v_hbm,
    so_ref, to_ref,
    x_ref, z_ref, b_ref, c_ref, step_ref, rate_ref, gain_ref, q_ref, kv_ref,
    cum_ref, csib_ref, ssm_ref, reach_ref, stl_ref, lout_ref, lsib_ref,
    raw_ref, st_ref, send_ref, out_ref,
    qt_ref, qtail_ref, acc_ref, max_ref, sum_ref, part_ref, stat_ref, tacc_ref,
    in_sem, send_sem, relay_send, spread_send, keys_recv, spread_recv, back_recv,
    state_recv, start_recv, local_recv, once_recv,
):
    me = lax.axis_index("seq")
    core = lax.rem(me, 2)
    chip = me // 2
    chips = n // 2
    sibling = me + 1 - 2 * core
    up = me - 2
    down = me + 2
    has_up = chip > 0
    has_down = chip < chips - 1
    is_tail = chip == chips - 1
    is_helper = chip == chips - 2
    feeds = chip < chips - 2
    relays = jnp.logical_and(has_up, feeds)
    skips = SKIPPED if chips == 4 else 0
    helper = 2 * (chips - 2) + core
    lag = jnp.where(feeds, 0, LAG)

    tokens, width = x_ref.shape
    heads = step_ref.shape[0]
    per_group = heads // GROUPS
    head_width = width // heads
    gw = width // GROUPS
    half_width = gw // HALVES
    state_dim = b_ref.shape[1] // GROUPS
    kv_count = kv_ref.shape[0]
    qw = q_ref.shape[1] // kv_count
    ratio = qw // HEAD_SIZE
    lanes = 128
    pack = lanes // head_width
    pairs = per_group // pack
    half_pairs = pairs // HALVES
    scale = math.log2(math.e) / math.sqrt(HEAD_SIZE)

    def span(g, size):
        return pl.ds(pl.multiple_of(g * size, 128), size)

    def to_seq(device):
        return dict(device_id={"seq": device}, device_id_type=MESH)

    key_loads = []
    for g in range(kv_count):
        for i, source in enumerate((k_hbm, v_hbm)):
            key_loads.append(
                pltpu.make_async_copy(
                    source.at[:, g * HEAD_SIZE : (g + 1) * HEAD_SIZE],
                    kv_ref.at[g, core, chip, i],
                    in_sem.at[0],
                )
            )
    own_keys = kv_ref.at[:, core, chip]
    all_keys = pltpu.make_async_copy(own_keys, own_keys, in_sem.at[0])
    loads = [
        pltpu.make_async_copy(src, dst, in_sem.at[i + 1])
        for i, (src, dst) in enumerate(
            (
                (step_hbm, step_ref), (rate_hbm, rate_ref), (q_hbm, q_ref),
                (b_hbm, b_ref), (c_hbm, c_ref), (x_hbm, x_ref), (z_hbm, z_ref), (gain_hbm, gain_ref),
            )
        )
    ]
    skip_pairs = ((0, helper), (chips - 2, core)) if skips else ()

    barrier = pltpu.get_barrier_semaphore()
    pl.semaphore_signal(barrier, inc=1, **to_seq(sibling))

    @pl.when(has_up)
    def _():
        pl.semaphore_signal(barrier, inc=1, **to_seq(up))

    @pl.when(has_down)
    def _():
        pl.semaphore_signal(barrier, inc=1, **to_seq(down))

    for source, target in skip_pairs:

        @pl.when(chip == source)
        def _():
            pl.semaphore_signal(barrier, inc=1, **to_seq(target))

    loads[0].start()
    loads[1].start()
    for load in key_loads:
        load.start()
    for load in loads[2:]:
        load.start()

    def remote(source, target, sent, got, device):
        return pltpu.make_async_remote_copy(
            src_ref=source, dst_ref=target, send_sem=sent, recv_sem=got, **to_seq(device)
        )

    def key_own(g, device):
        block = kv_ref.at[g, core, chip]
        return remote(block, block, send_sem.at[0], keys_recv.at[g, chip], device)

    def key_relay(g, j):
        block = kv_ref.at[g, core, j]
        return remote(block, block, relay_send.at[j], keys_recv.at[g, j], down)

    def key_lazy(g):
        block = kv_ref.at[g, core, chip]
        return remote(block, block, send_sem.at[1], keys_recv.at[g, chip], down)

    def key_side(parity):
        block = kv_ref.at[:, parity, chip]
        return remote(block, block, send_sem.at[2], once_recv.at[0], sibling)

    def key_spread(g, j, parity):
        block = kv_ref.at[g, parity, j]
        return remote(block, block, spread_send.at[j], spread_recv.at[g, j], sibling)

    def key_spread_all(g, parity):
        blocks = kv_ref.at[g, parity, 0 : chips - 2]
        return remote(blocks, blocks, spread_send.at[0], spread_recv.at[g, 0], sibling)

    def cum_side():
        return remote(cum_ref, csib_ref, send_sem.at[3], once_recv.at[1], sibling)

    def query_up(g):
        return remote(qt_ref.at[g], qtail_ref.at[g], send_sem.at[4], back_recv.at[g], up)

    def part_down(g, start, stop):
        block = part_ref.at[g, start:stop]
        return remote(block, block, send_sem.at[4], back_recv.at[g], down)

    def state_down(g):
        return remote(out_ref.at[g], raw_ref.at[g], send_sem.at[5], state_recv.at[g], down)

    def state_side(g, half):
        return remote(send_ref.at[g], st_ref.at[g, half], send_sem.at[6], start_recv.at[g], sibling)

    def local_side(g):
        return remote(lout_ref.at[g], lsib_ref.at[g], send_sem.at[7], local_recv.at[g], sibling)

    def sent(block, semaphore, device):
        remote(block, block, semaphore, once_recv.at[0], device).wait_send()

    loads[0].wait()
    loads[1].wait()
    eye = lax.broadcasted_iota(jnp.int32, (heads, heads), 0) == lax.broadcasted_iota(
        jnp.int32, (heads, heads), 1
    )
    rate = jnp.sum(jnp.where(eye, rate_ref[...], 0.0), axis=1, keepdims=True)
    running = -step_ref[...] * rate
    position = lax.broadcasted_iota(jnp.int32, (heads, tokens), 1)
    shift = 1
    while shift < tokens:
        running = running + jnp.where(position >= shift, pltpu.roll(running, shift, 1), 0.0)
        shift *= 2
    cum_ref[...] = running

    all_keys.wait()
    partners = 1 + has_up.astype(jnp.int32) + has_down.astype(jnp.int32)
    for source, _ in skip_pairs:
        partners = partners + (chip == source).astype(jnp.int32)
    pl.semaphore_wait(barrier, partners)

    @pl.when(feeds)
    def _():
        for g in range(LEAD):
            if g < skips:

                @pl.when(chip == 0)
                def _():
                    key_own(g, helper).start()

                @pl.when(has_up)
                def _():
                    key_own(g, down).start()
            else:
                key_own(g, down).start()

    key_side(core).start()
    cum_side().start()
    loads[2].wait()

    @pl.loop(0, kv_count)
    def _(g):
        for h in range(ratio):
            piece = q_ref[:, pl.ds(pl.multiple_of(g * qw + h * HEAD_SIZE, 128), HEAD_SIZE)]
            qt_ref[g, :, h * HEAD_SIZE : (h + 1) * HEAD_SIZE] = piece.T

        @pl.when(is_tail)
        def _():
            query_up(g).start()

    @pl.when(jnp.logical_not(has_up))
    def _():
        raw_ref[...] = jnp.zeros_like(raw_ref)

    for load in loads[3:]:
        load.wait()

    key_at = lax.broadcasted_iota(jnp.int32, (tokens, tokens), 0)
    query_at = lax.broadcasted_iota(jnp.int32, (tokens, tokens), 1)
    lower = query_at <= key_at
    half = lax.broadcasted_iota(jnp.int32, (tokens, lanes), 1) // head_width
    row_half = lax.broadcasted_iota(jnp.int32, (1, lanes), 1) // head_width
    visible = lax.broadcasted_iota(jnp.int32, (2 * tokens, tokens), 0) <= (
        lax.broadcasted_iota(jnp.int32, (2 * tokens, tokens), 1) + core * tokens
    )

    def mask_last(scores):
        rows = scores.shape[0] // 2
        parts = []
        for parity in range(2):
            seen = visible[parity * tokens : (parity + 1) * tokens]
            part = scores[parity * rows : (parity + 1) * rows]
            parts += [part[: rows - tokens]] if rows > tokens else []
            parts.append(jnp.where(seen, part[rows - tokens :], masked_score))
        return jnp.concatenate(parts, axis=0)

    def columns_of(g, p):
        return pl.ds(pl.multiple_of(g * gw + p * lanes, 128), lanes)

    def student_local(g):
        cum = cum_ref[pl.ds(pl.multiple_of(g * per_group, 8), per_group), :]
        cum_t = cum.T
        tail = jnp.exp(cum[:, tokens - 1 : tokens] - cum)
        b = b_ref[:, span(g, state_dim)]
        b_t = b.T.astype(F32)
        products = dot(c_ref[:, span(g, state_dim)], b, 1, 1)
        for p in range(pairs):
            x = x_ref[:, columns_of(g, p)].astype(F32)
            mixes = []
            adds = []
            sources = []
            reach = None
            for j in range(pack):
                h = p * pack + j
                column = jnp.broadcast_to(cum_t[:, h : h + 1], (tokens, lanes))
                difference = jnp.where(lower, column - cum[h : h + 1, :], masked_score)
                mixes.append((products * jnp.exp(difference)).astype(BF16))
                adds.append((b_t * tail[h : h + 1, :]).astype(BF16))
                sources.append(jnp.where(half == j, x, 0.0).astype(BF16))
                reach = column if j == 0 else jnp.where(half == j, column, reach)
            z = z_ref[:, columns_of(g, p)].astype(F32)
            gate = z / (1.0 + jnp.exp(-z))
            at = slice(p * lanes, (p + 1) * lanes)
            source = jnp.concatenate(sources, axis=0)
            ssm_ref[g, :, at] = gate * dot(jnp.concatenate(mixes, axis=1), source)
            reach_ref[g, :, at] = gate * jnp.exp(reach)
            stl_ref[g, :, at] = dot(jnp.concatenate(adds, axis=1), source)
        lout_ref[g] = stl_ref[g, :, span(1 - core, half_width)].astype(BF16)
        local_side(g).start()

    def chain(g):
        local_side(g).wait_recv()

        @pl.when(has_up)
        def _():
            state_down(g).wait_recv()

        rows = pl.ds(pl.multiple_of(g * per_group, 8), per_group)
        total_own = jnp.exp(cum_ref[rows, tokens - 1 : tokens])
        total_sib = jnp.exp(csib_ref[rows, tokens - 1 : tokens])

        def decay_of(total, p):
            decay = total[p * pack : p * pack + 1, :]
            for j in range(1, pack):
                decay = jnp.where(row_half == j, total[p * pack + j : p * pack + j + 1, :], decay)
            return decay

        for part in range(HALVES):

            @pl.when(core == part)
            def _():
                for i in range(half_pairs):
                    p = part * half_pairs + i
                    at = slice(i * lanes, (i + 1) * lanes)
                    own = (decay_of(total_own, p), stl_ref[g, :, p * lanes : (p + 1) * lanes])
                    other = (decay_of(total_sib, p), lsib_ref[g, :, at].astype(F32))
                    first, second = (own, other) if part == 0 else (other, own)
                    raw = raw_ref[g, :, at]
                    middle = raw.astype(F32) * first[0] + first[1]
                    out_ref[g, :, at] = (middle * second[0] + second[1]).astype(BF16)
                    middle = middle.astype(BF16)
                    st_ref[g, part, :, at] = raw if part == 0 else middle
                    send_ref[g, :, at] = middle if part == 0 else raw

        @pl.when(has_down)
        def _():
            state_down(g).start()

        state_side(g, core).start()

    mean_of = jnp.where(
        lax.broadcasted_iota(jnp.int32, (lanes, lanes), 0) // head_width
        == lax.broadcasted_iota(jnp.int32, (lanes, lanes), 1) // head_width,
        1.0 / head_width,
        0.0,
    ).astype(BF16)

    def student_finish(g):
        state_side(g, 1 - core).wait_recv()
        c = c_ref[:, span(g, state_dim)]
        for part in range(HALVES):
            carried = dot(c, st_ref[g, part])
            for i in range(half_pairs):
                p = part * half_pairs + i
                at = slice(p * lanes, (p + 1) * lanes)
                gated = ssm_ref[g, :, at] + reach_ref[g, :, at] * carried[:, i * lanes : (i + 1) * lanes]
                mean = dot((gated * gated).astype(BF16), mean_of)
                so_ref[:, columns_of(g, p)] = (
                    gated * lax.rsqrt(mean + epsilon_norm) * gain_ref[:, columns_of(g, p)]
                ).astype(BF16)

    def head_at(h):
        return slice(h * HEAD_SIZE, (h + 1) * HEAD_SIZE)

    def pass_over(keys, values, queries, mask=None):
        scores = dot(keys, queries)
        if mask is not None:
            scores = mask(scores)
        top = jnp.max(scores, axis=0, keepdims=True)
        weight = jnp.exp2((scores - top) * scale)
        return top, jnp.sum(weight, axis=0, keepdims=True), dot(values, weight.astype(BF16), 0, 0)

    def join(first, second):
        top = jnp.maximum(first[0], second[0])
        one = jnp.exp2((first[0] - top) * scale)
        two = jnp.exp2((second[0] - top) * scale)
        return top, first[1] * one + second[1] * two, first[2] * one + second[2] * two

    def rows_of(g, kind, start, count):
        taken = kv_ref[g, :, pl.ds(start, count), kind]
        return taken.reshape(2 * count * tokens, HEAD_SIZE)

    def attend_own(g):
        keys = rows_of(g, 0, chip, 1)
        values = rows_of(g, 1, chip, 1)
        for h in range(ratio):
            at = head_at(h)
            max_ref[g, :, at], sum_ref[g, :, at], acc_ref[g, :, at] = pass_over(
                keys, values, qt_ref[g, :, at], mask_last
            )

    def attend_earlier(g):
        @pl.loop(0, chip)
        def _(j):
            keys = rows_of(g, 0, j, 1)
            values = rows_of(g, 1, j, 1)
            for h in range(ratio):
                at = head_at(h)
                held = (max_ref[g, :, at], sum_ref[g, :, at], acc_ref[g, :, at])
                max_ref[g, :, at], sum_ref[g, :, at], acc_ref[g, :, at] = join(
                    held, pass_over(keys, values, qt_ref[g, :, at])
                )

    chunk = max(k for k in range(1, 4) if (chips - 1) % k == 0)
    chunks = (chips - 1) // chunk
    log_rows = rows_for(ratio)

    def attend_tail(g, cuts):
        def keep(h, result):
            top, total, acc = result
            part_ref[g, h * HEAD_SIZE : (h + 1) * HEAD_SIZE] = (acc * (1.0 / total)).astype(BF16)
            rest = top * scale + jnp.log2(total)
            pieces = []
            for _ in range(PIECES):
                pieces.append(rest.astype(BF16))
                rest = rest - pieces[-1].astype(F32)
            return pieces

        def send(logs, heads_from, heads_to):
            if heads_to == ratio:
                rows = [piece for pieces in logs for piece in pieces]
                blank = jnp.zeros((log_rows - len(rows), HEAD_SIZE), BF16)
                part_ref[g, ratio * HEAD_SIZE :] = jnp.concatenate(rows + [blank], axis=0)
            part_down(g, heads_from * HEAD_SIZE, heads_to * HEAD_SIZE + (log_rows if heads_to == ratio else 0)).start()

        keys = rows_of(g, 0, 0, chunk)
        values = rows_of(g, 1, 0, chunk)
        logs = []
        for h in range(ratio):
            at = head_at(h)
            result = pass_over(keys, values, qtail_ref[g, :, at])
            if chunks == 1:
                logs.append(keep(h, result))
                if (h + 1) % (ratio // cuts) == 0:
                    send(logs, h + 1 - ratio // cuts, h + 1)
            else:
                stat_ref[0:1, at], stat_ref[1:2, at], tacc_ref[:, at] = result
        if chunks > 1:

            @pl.loop(1, chunks)
            def _(k):
                keys = rows_of(g, 0, k * chunk, chunk)
                values = rows_of(g, 1, k * chunk, chunk)
                for h in range(ratio):
                    at = head_at(h)
                    held = (stat_ref[0:1, at], stat_ref[1:2, at], tacc_ref[:, at])
                    stat_ref[0:1, at], stat_ref[1:2, at], tacc_ref[:, at] = join(
                        held, pass_over(keys, values, qtail_ref[g, :, at])
                    )

            for h in range(ratio):
                at = head_at(h)
                logs.append(keep(h, (stat_ref[0:1, at], stat_ref[1:2, at], tacc_ref[:, at])))
            send(logs, 0, ratio)

    def attend_all(g):
        if chunks > 1:
            attend_own(g)
            attend_earlier(g)
            finish_teacher(g)
        else:
            keys = rows_of(g, 0, 0, chunk)
            values = rows_of(g, 1, 0, chunk)
            for h in range(ratio):
                _, total, acc = pass_over(keys, values, qt_ref[g, :, head_at(h)], mask_last)
                write_teacher(g, h, acc * (1.0 / total))

    def write_teacher(g, h, result):
        to_ref[:, pl.ds(pl.multiple_of(g * qw + h * HEAD_SIZE, 128), HEAD_SIZE)] = result.T.astype(BF16)

    def finish_teacher(g):
        for h in range(ratio):
            at = head_at(h)
            write_teacher(g, h, acc_ref[g, :, at] * (1.0 / sum_ref[g, :, at]))

    def merge_teacher(g):
        part_down(g, 0, ratio * HEAD_SIZE + log_rows).wait_recv()
        logs = part_ref[g, ratio * HEAD_SIZE :].astype(F32)
        for h in range(ratio):
            at = head_at(h)
            total = sum_ref[g, :, at]
            near = max_ref[g, :, at] * scale + jnp.log2(total)
            far = logs[h * PIECES : h * PIECES + 1]
            for i in range(1, PIECES):
                far = far + logs[h * PIECES + i : h * PIECES + i + 1]
            top = jnp.maximum(near, far)
            one = jnp.exp2(near - top)
            two = jnp.exp2(far - top)
            inverse = 1.0 / (one + two)
            part = part_ref[g, h * HEAD_SIZE : (h + 1) * HEAD_SIZE].astype(F32)
            write_teacher(g, h, acc_ref[g, :, at] * (one * inverse / total) + part * (two * inverse))

    def take_keys(g, onward):
        @pl.loop(0, chip)
        def _(i):
            j = chip - 1 - i
            key_relay(g, j).wait_recv()
            if onward:
                key_relay(g, j).start()
            key_spread(g, j, core).start()

    def attend_rest(g):
        @pl.loop(0, chip)
        def _(i):
            key_spread(g, chip - 1 - i, 1 - core).wait_recv()

        attend_earlier(g)
        finish_teacher(g)

    cum_side().wait_recv()
    key_side(1 - core).wait_recv()
    final = GROUPS - 1

    student_local(0)

    @pl.loop(0, GROUPS + 1)
    def _(r):
        live = r < GROUPS

        @pl.when(relays)
        def _():
            @pl.loop(jnp.where(r == 0, skips, r + 1), jnp.minimum(r + 2, GROUPS))
            def _(g):
                take_keys(g, True)

        @pl.when(jnp.logical_and(live, is_helper))
        def _():
            @pl.loop(0, chip)
            def _(i):
                key_relay(r, chip - 1 - i).wait_recv()

            if chips > 2:
                key_spread_all(r, core).start()

        @pl.when(r < final)
        def _():
            student_local(r + 1)

        @pl.loop(jnp.maximum(r - lag - 1, 0), jnp.where(live, jnp.maximum(r - lag, 0), GROUPS))
        def _(g):
            student_finish(g)

        @pl.when(jnp.logical_and(is_tail, r >= 1))
        def _():
            merge_teacher(r - 1)

        @pl.loop(
            jnp.where(live, jnp.maximum(r - lag, 0), GROUPS),
            jnp.where(r < final, jnp.maximum(r - lag + 1, 0), GROUPS),
        )
        def _(g):
            chain(g)

        @pl.when(jnp.logical_and(feeds, r + LEAD < GROUPS))
        def _():
            key_own(r + LEAD, down).start()

        @pl.when(live)
        def _():
            @pl.when(is_helper)
            def _():
                if chips > 2:
                    key_spread_all(r, 1 - core).wait_recv()
                query_up(r).wait_recv()

                @pl.when(r == 0)
                def _():
                    attend_tail(r, 2)

                @pl.when(r > 0)
                def _():
                    attend_tail(r, 1)

            @pl.when(jnp.logical_not(is_helper))
            def _():
                attend_own(r)

            @pl.when(jnp.logical_not(has_up))
            def _():
                @pl.when(jnp.logical_not(is_helper))
                def _():
                    finish_teacher(r)

        @pl.when(is_helper)
        def _():
            @pl.loop(jnp.where(live, jnp.maximum(r - OWN_LAG, 0), GROUPS - OWN_LAG), jnp.where(live, jnp.maximum(r - OWN_LAG + 1, 0), GROUPS))
            def _(g):
                attend_all(g)

    if skips:

        @pl.when(chip == 0)
        def _():
            for g in range(skips):
                key_lazy(g).start()

    @pl.when(relays)
    def _():
        for g in range(skips):
            take_keys(g, False)

        @pl.loop(0, GROUPS)
        def _(g):
            attend_rest(g)

    sent(kv_ref.at[:, core, chip], send_sem.at[2], sibling)
    sent(cum_ref, send_sem.at[3], sibling)
    sent(send_ref, send_sem.at[6], sibling)
    sent(lout_ref, send_sem.at[7], sibling)

    @pl.when(has_down)
    def _():
        sent(out_ref, send_sem.at[5], down)

    @pl.when(feeds)
    def _():
        sent(kv_ref.at[:, core, chip], send_sem.at[0], down)

    if skips:

        @pl.when(chip == 0)
        def _():
            sent(kv_ref.at[0:skips, core, chip], send_sem.at[1], down)

    @pl.when(relays)
    def _():
        @pl.loop(0, chip)
        def _(j):
            sent(kv_ref.at[skips:, core, j], relay_send.at[j], down)
            sent(kv_ref.at[:, core, j], spread_send.at[j], sibling)

    @pl.when(is_helper)
    def _():
        if chips > 2:
            sent(kv_ref.at[:, core, 0 : chips - 2], spread_send.at[0], sibling)
        sent(part_ref, send_sem.at[4], down)

    @pl.when(is_tail)
    def _():
        sent(qt_ref, send_sem.at[4], up)


def store(s_ref, t_ref, s_out, t_out, sem):
    copies = [
        pltpu.make_async_copy(s_ref, s_out, sem.at[0]),
        pltpu.make_async_copy(t_ref, t_out, sem.at[1]),
    ]
    for copy in copies:
        copy.start()
    for copy in copies:
        copy.wait()


def on_device(
    student_x, student_z, student_b, student_c, step_size, decay_rate, norm_gain,
    teacher_q, teacher_k, teacher_v,
):
    n = lax.axis_size("seq")
    tokens, width = student_x.shape
    heads = step_size.shape[0]
    assert tokens == BLOCK and n % 2 == 0 and n >= 4
    gw = width // GROUPS
    state_dim = student_b.shape[1] // GROUPS
    kv_count = teacher_k.shape[1] // HEAD_SIZE
    assert kv_count == GROUPS
    qw = teacher_q.shape[1] // kv_count
    hbm = pl.BlockSpec(memory_space=pl.ANY)
    vmem = pl.BlockSpec(memory_space=pltpu.VMEM)
    dma = pltpu.SemaphoreType.DMA
    states = pltpu.VMEM((GROUPS, state_dim, gw // HALVES), BF16)
    queries = pltpu.VMEM((kv_count, HEAD_SIZE, qw), BF16)
    results = pl.pallas_call(
        functools.partial(kernel, n),
        out_shape=(
            pltpu.VMEM(student_x.shape, BF16),
            pltpu.VMEM(teacher_q.shape, BF16),
        ),
        in_specs=[hbm] * 10,
        out_specs=(vmem, vmem),
        scratch_shapes=[
            pltpu.VMEM(student_x.shape, BF16),
            pltpu.VMEM(student_z.shape, BF16),
            pltpu.VMEM(student_b.shape, BF16),
            pltpu.VMEM(student_c.shape, BF16),
            pltpu.VMEM(step_size.shape, F32),
            pltpu.VMEM((1, heads), F32),
            pltpu.VMEM((1, width), F32),
            pltpu.VMEM(teacher_q.shape, BF16),
            pltpu.VMEM((kv_count, 2, n // 2, 2, tokens, HEAD_SIZE), BF16),
            pltpu.VMEM(step_size.shape, F32),
            pltpu.VMEM(step_size.shape, F32),
            pltpu.VMEM((GROUPS, tokens, gw), F32),
            pltpu.VMEM((GROUPS, tokens, gw), F32),
            pltpu.VMEM((GROUPS, state_dim, gw), F32),
            states,
            states,
            states,
            pltpu.VMEM((GROUPS, HALVES, state_dim, gw // HALVES), BF16),
            states,
            states,
            queries,
            queries,
            pltpu.VMEM((kv_count, HEAD_SIZE, qw), F32),
            pltpu.VMEM((kv_count, 1, qw), F32),
            pltpu.VMEM((kv_count, 1, qw), F32),
            pltpu.VMEM((kv_count, qw + rows_for(qw // HEAD_SIZE), HEAD_SIZE), BF16),
            pltpu.VMEM((2, qw), F32),
            pltpu.VMEM((HEAD_SIZE, qw), F32),
            dma((9,)),
            dma((8,)),
            dma((max(n // 2 - 3, 1),)),
            dma((max(n // 2 - 3, 1),)),
            dma((kv_count, max(n // 2 - 2, 1))),
            dma((kv_count, max(n // 2 - 3, 1))),
        ]
        + [dma((GROUPS,))] * 4
        + [dma((2,))],
        compiler_params=pltpu.CompilerParams(
            collective_id=0, has_side_effects=True, vmem_limit_bytes=56 * 1024 * 1024
        ),
    )(
        student_x, student_z, student_b, student_c, step_size, decay_rate[None, :],
        norm_gain[None, :], teacher_q, teacher_k, teacher_v,
    )
    results = [pltpu.with_memory_space_constraint(r, pltpu.VMEM) for r in results]
    return pl.pallas_call(
        store,
        out_shape=(
            jax.ShapeDtypeStruct(student_x.shape, BF16),
            jax.ShapeDtypeStruct(teacher_q.shape, BF16),
        ),
        in_specs=[vmem, vmem],
        out_specs=(hbm, hbm),
        scratch_shapes=[dma((2,))],
    )(*results)


def solution(mesh):
    return jax.shard_map(
        on_device,
        mesh=mesh,
        in_specs=(
            P(("dp", "seq"), None),
            P(("dp", "seq"), None),
            P(("dp", "seq"), None),
            P(("dp", "seq"), None),
            P(None, ("dp", "seq")),
            P(),
            P(),
            P(("dp", "seq"), None),
            P(("dp", "seq"), None),
            P(("dp", "seq"), None),
        ),
        out_specs=(P(("dp", "seq"), None), P(("dp", "seq"), None)),
        check_vma=False,
    )
```

```python
import functools
import math

import jax
import jax.numpy as jnp
from jax import lax
from jax.experimental import pallas as pl
from jax.experimental.pallas import tpu as pltpu
from jax.sharding import PartitionSpec as P

GROUPS = 8
HEAD_SIZE = 128
BLOCK = 128
HALVES = 2
LEAD = 2
LAG = 1
OWN_LAG = 2
PIECES = 3
CUTS = 2
SKIPPED = 1

epsilon_norm = 1e-05
masked_score = -1e30
F32 = jnp.float32
BF16 = jnp.bfloat16
MESH = pl.DeviceIdType.MESH


def dot(a, b, ca=1, cb=0):
    return lax.dot_general(a, b, (((ca,), (cb,)), ((), ())), preferred_element_type=F32)


def rows_for(heads):
    return -(-heads * PIECES // 16) * 16


def kernel(
    n,
    x_hbm, z_hbm, b_hbm, c_hbm, step_hbm, rate_hbm, gain_hbm, q_hbm, k_hbm, v_hbm,
    so_ref, to_ref,
    x_ref, z_ref, b_ref, c_ref, step_ref, rate_ref, gain_ref, q_ref, kv_ref,
    cum_ref, csib_ref, ssm_ref, reach_ref, stl_ref, lout_ref, lsib_ref,
    raw_ref, st_ref, send_ref, out_ref,
    qt_ref, qtail_ref, acc_ref, max_ref, sum_ref, part_ref, stat_ref, tacc_ref,
    in_sem, send_sem, relay_send, spread_send, keys_recv, spread_recv, back_recv,
    state_recv, start_recv, local_recv, once_recv,
):
    me = lax.axis_index("seq")
    core = lax.rem(me, 2)
    chip = me // 2
    chips = n // 2
    sibling = me + 1 - 2 * core
    up = me - 2
    down = me + 2
    has_up = chip > 0
    has_down = chip < chips - 1
    is_tail = chip == chips - 1
    is_helper = chip == chips - 2
    feeds = chip < chips - 2
    relays = jnp.logical_and(has_up, feeds)
    skips = SKIPPED if chips == 4 else 0
    helper = 2 * (chips - 2) + core
    lag = jnp.where(feeds, 0, LAG)

    tokens, width = x_ref.shape
    heads = step_ref.shape[0]
    per_group = heads // GROUPS
    head_width = width // heads
    gw = width // GROUPS
    half_width = gw // HALVES
    state_dim = b_ref.shape[1] // GROUPS
    kv_count = kv_ref.shape[0]
    qw = q_ref.shape[1] // kv_count
    ratio = qw // HEAD_SIZE
    lanes = 128
    pack = lanes // head_width
    pairs = per_group // pack
    half_pairs = pairs // HALVES
    scale = math.log2(math.e) / math.sqrt(HEAD_SIZE)

    def span(g, size):
        return pl.ds(pl.multiple_of(g * size, 128), size)

    def to_seq(device):
        return dict(device_id={"seq": device}, device_id_type=MESH)

    key_loads = []
    for g in range(kv_count):
        for i, source in enumerate((k_hbm, v_hbm)):
            key_loads.append(
                pltpu.make_async_copy(
                    source.at[:, g * HEAD_SIZE : (g + 1) * HEAD_SIZE],
                    kv_ref.at[g, core, chip, i],
                    in_sem.at[0],
                )
            )
    own_keys = kv_ref.at[:, core, chip]
    all_keys = pltpu.make_async_copy(own_keys, own_keys, in_sem.at[0])
    loads = [
        pltpu.make_async_copy(src, dst, in_sem.at[i + 1])
        for i, (src, dst) in enumerate(
            (
                (step_hbm, step_ref), (rate_hbm, rate_ref), (q_hbm, q_ref),
                (b_hbm, b_ref), (c_hbm, c_ref), (x_hbm, x_ref), (z_hbm, z_ref), (gain_hbm, gain_ref),
            )
        )
    ]
    skip_pairs = ((0, helper), (chips - 2, core)) if skips else ()

    barrier = pltpu.get_barrier_semaphore()
    pl.semaphore_signal(barrier, inc=1, **to_seq(sibling))

    @pl.when(has_up)
    def _():
        pl.semaphore_signal(barrier, inc=1, **to_seq(up))

    @pl.when(has_down)
    def _():
        pl.semaphore_signal(barrier, inc=1, **to_seq(down))

    for source, target in skip_pairs:

        @pl.when(chip == source)
        def _():
            pl.semaphore_signal(barrier, inc=1, **to_seq(target))

    loads[0].start()
    loads[1].start()
    for load in key_loads:
        load.start()

    @pl.when(is_tail)
    def _():
        loads[2].start()

    for load in loads[3:]:
        load.start()

    @pl.when(jnp.logical_not(is_tail))
    def _():
        loads[2].start()

    def remote(source, target, sent, got, device):
        return pltpu.make_async_remote_copy(
            src_ref=source, dst_ref=target, send_sem=sent, recv_sem=got, **to_seq(device)
        )

    def key_own(g, device):
        block = kv_ref.at[g, core, chip]
        return remote(block, block, send_sem.at[0], keys_recv.at[g, chip], device)

    def key_relay(g, j):
        block = kv_ref.at[g, core, j]
        return remote(block, block, relay_send.at[j], keys_recv.at[g, j], down)

    def key_lazy(g):
        block = kv_ref.at[g, core, chip]
        return remote(block, block, send_sem.at[1], keys_recv.at[g, chip], down)

    def key_side(parity):
        block = kv_ref.at[:, parity, chip]
        return remote(block, block, send_sem.at[2], once_recv.at[0], sibling)

    def key_spread(g, j, parity):
        block = kv_ref.at[g, parity, j]
        return remote(block, block, spread_send.at[j], spread_recv.at[g, j], sibling)

    def key_spread_all(g, parity):
        blocks = kv_ref.at[g, parity, 0 : chips - 2]
        return remote(blocks, blocks, spread_send.at[0], spread_recv.at[g, 0], sibling)

    def cum_side():
        return remote(cum_ref, csib_ref, send_sem.at[3], once_recv.at[1], sibling)

    def query_up(g):
        return remote(qt_ref.at[g], qtail_ref.at[g], send_sem.at[4], back_recv.at[g], up)

    def part_down(g, start, stop):
        block = part_ref.at[g, start:stop]
        return remote(block, block, send_sem.at[4], back_recv.at[g], down)

    def state_down(g):
        return remote(out_ref.at[g], raw_ref.at[g], send_sem.at[5], state_recv.at[g], down)

    def state_side(g, half):
        return remote(send_ref.at[g], st_ref.at[g, half], send_sem.at[6], start_recv.at[g], sibling)

    def local_side(g):
        return remote(lout_ref.at[g], lsib_ref.at[g], send_sem.at[7], local_recv.at[g], sibling)

    def sent(block, semaphore, device):
        remote(block, block, semaphore, once_recv.at[0], device).wait_send()

    loads[0].wait()
    loads[1].wait()
    eye = lax.broadcasted_iota(jnp.int32, (heads, heads), 0) == lax.broadcasted_iota(
        jnp.int32, (heads, heads), 1
    )
    rate = jnp.sum(jnp.where(eye, rate_ref[...], 0.0), axis=1, keepdims=True)
    running = -step_ref[...] * rate
    position = lax.broadcasted_iota(jnp.int32, (heads, tokens), 1)
    shift = 1
    while shift < tokens:
        running = running + jnp.where(position >= shift, pltpu.roll(running, shift, 1), 0.0)
        shift *= 2
    cum_ref[...] = running

    all_keys.wait()
    partners = 1 + has_up.astype(jnp.int32) + has_down.astype(jnp.int32)
    for source, _ in skip_pairs:
        partners = partners + (chip == source).astype(jnp.int32)
    pl.semaphore_wait(barrier, partners)

    @pl.when(feeds)
    def _():
        for g in range(LEAD):
            if g < skips:

                @pl.when(chip == 0)
                def _():
                    key_own(g, helper).start()

                @pl.when(has_up)
                def _():
                    key_own(g, down).start()
            else:
                key_own(g, down).start()

    cum_side().start()
    key_side(core).start()

    def transpose_queries(g):
        for h in range(ratio):
            piece = q_ref[:, pl.ds(pl.multiple_of(g * qw + h * HEAD_SIZE, 128), HEAD_SIZE)]
            qt_ref[g, :, h * HEAD_SIZE : (h + 1) * HEAD_SIZE] = piece.T

    @pl.when(is_tail)
    def _():
        loads[2].wait()

        @pl.loop(0, kv_count)
        def _(g):
            transpose_queries(g)
            query_up(g).start()

    @pl.when(jnp.logical_not(has_up))
    def _():
        raw_ref[...] = jnp.zeros_like(raw_ref)

    for load in loads[3:7]:
        load.wait()

    key_at = lax.broadcasted_iota(jnp.int32, (tokens, tokens), 0)
    query_at = lax.broadcasted_iota(jnp.int32, (tokens, tokens), 1)
    lower = query_at <= key_at
    half = lax.broadcasted_iota(jnp.int32, (tokens, lanes), 1) // head_width
    row_half = lax.broadcasted_iota(jnp.int32, (1, lanes), 1) // head_width
    visible = lax.broadcasted_iota(jnp.int32, (2 * tokens, tokens), 0) <= (
        lax.broadcasted_iota(jnp.int32, (2 * tokens, tokens), 1) + core * tokens
    )

    def mask_last(scores):
        rows = scores.shape[0] // 2
        parts = []
        for parity in range(2):
            seen = visible[parity * tokens : (parity + 1) * tokens]
            part = scores[parity * rows : (parity + 1) * rows]
            parts += [part[: rows - tokens]] if rows > tokens else []
            parts.append(jnp.where(seen, part[rows - tokens :], masked_score))
        return jnp.concatenate(parts, axis=0)

    def columns_of(g, p):
        return pl.ds(pl.multiple_of(g * gw + p * lanes, 128), lanes)

    def student_local(g):
        cum = cum_ref[pl.ds(pl.multiple_of(g * per_group, 8), per_group), :]
        cum_t = cum.T
        tail = jnp.exp(cum[:, tokens - 1 : tokens] - cum)
        b = b_ref[:, span(g, state_dim)]
        b_t = b.T.astype(F32)
        products = dot(c_ref[:, span(g, state_dim)], b, 1, 1)
        for p in range(pairs):
            x = x_ref[:, columns_of(g, p)].astype(F32)
            mixes = []
            adds = []
            sources = []
            reach = None
            for j in range(pack):
                h = p * pack + j
                column = jnp.broadcast_to(cum_t[:, h : h + 1], (tokens, lanes))
                difference = jnp.where(lower, column - cum[h : h + 1, :], masked_score)
                mixes.append((products * jnp.exp(difference)).astype(BF16))
                adds.append((b_t * tail[h : h + 1, :]).astype(BF16))
                sources.append(jnp.where(half == j, x, 0.0).astype(BF16))
                reach = column if j == 0 else jnp.where(half == j, column, reach)
            z = z_ref[:, columns_of(g, p)].astype(F32)
            gate = z / (1.0 + jnp.exp(-z))
            at = slice(p * lanes, (p + 1) * lanes)
            source = jnp.concatenate(sources, axis=0)
            ssm_ref[g, :, at] = gate * dot(jnp.concatenate(mixes, axis=1), source)
            reach_ref[g, :, at] = gate * jnp.exp(reach)
            stl_ref[g, :, at] = dot(jnp.concatenate(adds, axis=1), source)
        lout_ref[g] = stl_ref[g, :, span(1 - core, half_width)].astype(BF16)
        local_side(g).start()

    def chain(g):
        local_side(g).wait_recv()

        @pl.when(has_up)
        def _():
            state_down(g).wait_recv()

        rows = pl.ds(pl.multiple_of(g * per_group, 8), per_group)
        total_own = jnp.exp(cum_ref[rows, tokens - 1 : tokens])
        total_sib = jnp.exp(csib_ref[rows, tokens - 1 : tokens])

        def decay_of(total, p):
            decay = total[p * pack : p * pack + 1, :]
            for j in range(1, pack):
                decay = jnp.where(row_half == j, total[p * pack + j : p * pack + j + 1, :], decay)
            return decay

        for part in range(HALVES):

            @pl.when(core == part)
            def _():
                for i in range(half_pairs):
                    p = part * half_pairs + i
                    at = slice(i * lanes, (i + 1) * lanes)
                    own = (decay_of(total_own, p), stl_ref[g, :, p * lanes : (p + 1) * lanes])
                    other = (decay_of(total_sib, p), lsib_ref[g, :, at].astype(F32))
                    first, second = (own, other) if part == 0 else (other, own)
                    raw = raw_ref[g, :, at]
                    middle = raw.astype(F32) * first[0] + first[1]
                    out_ref[g, :, at] = (middle * second[0] + second[1]).astype(BF16)
                    middle = middle.astype(BF16)
                    st_ref[g, part, :, at] = raw if part == 0 else middle
                    send_ref[g, :, at] = middle if part == 0 else raw

        @pl.when(has_down)
        def _():
            state_down(g).start()

        state_side(g, core).start()

    mean_of = jnp.where(
        lax.broadcasted_iota(jnp.int32, (lanes, lanes), 0) // head_width
        == lax.broadcasted_iota(jnp.int32, (lanes, lanes), 1) // head_width,
        1.0 / head_width,
        0.0,
    ).astype(BF16)

    def student_finish(g):
        state_side(g, 1 - core).wait_recv()
        c = c_ref[:, span(g, state_dim)]
        for part in range(HALVES):
            carried = dot(c, st_ref[g, part])
            for i in range(half_pairs):
                p = part * half_pairs + i
                at = slice(p * lanes, (p + 1) * lanes)
                gated = ssm_ref[g, :, at] + reach_ref[g, :, at] * carried[:, i * lanes : (i + 1) * lanes]
                mean = dot((gated * gated).astype(BF16), mean_of)
                so_ref[:, columns_of(g, p)] = (
                    gated * lax.rsqrt(mean + epsilon_norm) * gain_ref[:, columns_of(g, p)]
                ).astype(BF16)

    def head_at(h):
        return slice(h * HEAD_SIZE, (h + 1) * HEAD_SIZE)

    def pass_over(keys, values, queries, mask=None):
        scores = dot(keys, queries)
        if mask is not None:
            scores = mask(scores)
        top = jnp.max(scores, axis=0, keepdims=True)
        weight = jnp.exp2((scores - top) * scale)
        return top, jnp.sum(weight, axis=0, keepdims=True), dot(values, weight.astype(BF16), 0, 0)

    def join(first, second):
        top = jnp.maximum(first[0], second[0])
        one = jnp.exp2((first[0] - top) * scale)
        two = jnp.exp2((second[0] - top) * scale)
        return top, first[1] * one + second[1] * two, first[2] * one + second[2] * two

    def rows_of(g, kind, start, count):
        taken = kv_ref[g, :, pl.ds(start, count), kind]
        return taken.reshape(2 * count * tokens, HEAD_SIZE)

    def attend_own(g):
        keys = rows_of(g, 0, chip, 1)
        values = rows_of(g, 1, chip, 1)
        for h in range(ratio):
            at = head_at(h)
            max_ref[g, :, at], sum_ref[g, :, at], acc_ref[g, :, at] = pass_over(
                keys, values, qt_ref[g, :, at], mask_last
            )

    def attend_earlier(g):
        @pl.loop(0, chip)
        def _(j):
            keys = rows_of(g, 0, j, 1)
            values = rows_of(g, 1, j, 1)
            for h in range(ratio):
                at = head_at(h)
                held = (max_ref[g, :, at], sum_ref[g, :, at], acc_ref[g, :, at])
                max_ref[g, :, at], sum_ref[g, :, at], acc_ref[g, :, at] = join(
                    held, pass_over(keys, values, qt_ref[g, :, at])
                )

    chunk = max(k for k in range(1, 4) if (chips - 1) % k == 0)
    chunks = (chips - 1) // chunk
    log_rows = rows_for(ratio)

    def attend_tail(g):
        def keep(h, result):
            top, total, acc = result
            part_ref[g, h * HEAD_SIZE : (h + 1) * HEAD_SIZE] = (acc * (1.0 / total)).astype(BF16)
            rest = top * scale + jnp.log2(total)
            pieces = []
            for _ in range(PIECES):
                pieces.append(rest.astype(BF16))
                rest = rest - pieces[-1].astype(F32)
            return pieces

        def send(logs, heads_from, heads_to):
            if heads_to == ratio:
                rows = [piece for pieces in logs for piece in pieces]
                blank = jnp.zeros((log_rows - len(rows), HEAD_SIZE), BF16)
                part_ref[g, ratio * HEAD_SIZE :] = jnp.concatenate(rows + [blank], axis=0)
            part_down(g, heads_from * HEAD_SIZE, heads_to * HEAD_SIZE + (log_rows if heads_to == ratio else 0)).start()

        keys = rows_of(g, 0, 0, chunk)
        values = rows_of(g, 1, 0, chunk)
        logs = []
        for h in range(ratio):
            at = head_at(h)
            result = pass_over(keys, values, qtail_ref[g, :, at])
            if chunks == 1:
                logs.append(keep(h, result))
                if (h + 1) % (ratio // CUTS) == 0:
                    send(logs, h + 1 - ratio // CUTS, h + 1)
            else:
                stat_ref[0:1, at], stat_ref[1:2, at], tacc_ref[:, at] = result
        if chunks > 1:

            @pl.loop(1, chunks)
            def _(k):
                keys = rows_of(g, 0, k * chunk, chunk)
                values = rows_of(g, 1, k * chunk, chunk)
                for h in range(ratio):
                    at = head_at(h)
                    held = (stat_ref[0:1, at], stat_ref[1:2, at], tacc_ref[:, at])
                    stat_ref[0:1, at], stat_ref[1:2, at], tacc_ref[:, at] = join(
                        held, pass_over(keys, values, qtail_ref[g, :, at])
                    )

            for h in range(ratio):
                at = head_at(h)
                logs.append(keep(h, (stat_ref[0:1, at], stat_ref[1:2, at], tacc_ref[:, at])))
            send(logs, 0, ratio)

    def attend_all(g):
        if chunks > 1:
            attend_own(g)
            attend_earlier(g)
            finish_teacher(g)
        else:
            keys = rows_of(g, 0, 0, chunk)
            values = rows_of(g, 1, 0, chunk)
            for h in range(ratio):
                _, total, acc = pass_over(keys, values, qt_ref[g, :, head_at(h)], mask_last)
                write_teacher(g, h, acc * (1.0 / total))

    def write_teacher(g, h, result):
        to_ref[:, pl.ds(pl.multiple_of(g * qw + h * HEAD_SIZE, 128), HEAD_SIZE)] = result.T.astype(BF16)

    def finish_teacher(g):
        for h in range(ratio):
            at = head_at(h)
            write_teacher(g, h, acc_ref[g, :, at] * (1.0 / sum_ref[g, :, at]))

    def merge_teacher(g):
        part_down(g, 0, ratio * HEAD_SIZE + log_rows).wait_recv()
        logs = part_ref[g, ratio * HEAD_SIZE :].astype(F32)
        for h in range(ratio):
            at = head_at(h)
            total = sum_ref[g, :, at]
            near = max_ref[g, :, at] * scale + jnp.log2(total)
            far = logs[h * PIECES : h * PIECES + 1]
            for i in range(1, PIECES):
                far = far + logs[h * PIECES + i : h * PIECES + i + 1]
            top = jnp.maximum(near, far)
            one = jnp.exp2(near - top)
            two = jnp.exp2(far - top)
            inverse = 1.0 / (one + two)
            part = part_ref[g, h * HEAD_SIZE : (h + 1) * HEAD_SIZE].astype(F32)
            write_teacher(g, h, acc_ref[g, :, at] * (one * inverse / total) + part * (two * inverse))

    def take_keys(g, onward):
        @pl.loop(0, chip)
        def _(i):
            j = chip - 1 - i
            key_relay(g, j).wait_recv()
            if onward:
                key_relay(g, j).start()
            key_spread(g, j, core).start()

    def attend_rest(g):
        @pl.loop(0, chip)
        def _(i):
            key_spread(g, chip - 1 - i, 1 - core).wait_recv()

        attend_earlier(g)
        finish_teacher(g)

    final = GROUPS - 1

    student_local(0)
    cum_side().wait_recv()

    @pl.loop(0, GROUPS + 1)
    def _(r):
        live = r < GROUPS

        @pl.when(relays)
        def _():
            @pl.loop(jnp.where(r == 0, skips, r + 1), jnp.minimum(r + 2, GROUPS))
            def _(g):
                take_keys(g, True)

        @pl.when(jnp.logical_and(live, is_helper))
        def _():
            @pl.loop(0, chip)
            def _(i):
                key_relay(r, chip - 1 - i).wait_recv()

            if chips > 2:
                key_spread_all(r, core).start()

        @pl.when(r < final)
        def _():
            student_local(r + 1)

        @pl.loop(jnp.maximum(r - lag - 1, 0), jnp.where(live, jnp.maximum(r - lag, 0), GROUPS))
        def _(g):
            student_finish(g)

        @pl.when(jnp.logical_and(is_tail, r >= 1))
        def _():
            merge_teacher(r - 1)

        @pl.loop(
            jnp.where(live, jnp.maximum(r - lag, 0), GROUPS),
            jnp.where(r < final, jnp.maximum(r - lag + 1, 0), GROUPS),
        )
        def _(g):
            chain(g)

        @pl.when(jnp.logical_and(feeds, r + LEAD < GROUPS))
        def _():
            key_own(r + LEAD, down).start()

        @pl.when(r == 0)
        def _():
            key_side(1 - core).wait_recv()
            loads[7].wait()

            @pl.when(jnp.logical_not(is_tail))
            def _():
                loads[2].wait()

        @pl.when(live)
        def _():
            @pl.when(jnp.logical_not(jnp.logical_or(is_tail, is_helper)))
            def _():
                transpose_queries(r)

            @pl.when(is_helper)
            def _():
                if chips > 2:
                    key_spread_all(r, 1 - core).wait_recv()
                query_up(r).wait_recv()

                attend_tail(r)
                transpose_queries(r)

            @pl.when(jnp.logical_not(is_helper))
            def _():
                attend_own(r)

            @pl.when(jnp.logical_not(has_up))
            def _():
                @pl.when(jnp.logical_not(is_helper))
                def _():
                    finish_teacher(r)

        @pl.when(is_helper)
        def _():
            @pl.loop(jnp.where(live, jnp.maximum(r - OWN_LAG, 0), GROUPS - OWN_LAG), jnp.where(live, jnp.maximum(r - OWN_LAG + 1, 0), GROUPS))
            def _(g):
                attend_all(g)

    if skips:

        @pl.when(chip == 0)
        def _():
            for g in range(skips):
                key_lazy(g).start()

    @pl.when(relays)
    def _():
        for g in range(skips):
            take_keys(g, False)

        @pl.loop(0, GROUPS)
        def _(g):
            attend_rest(g)

    sent(kv_ref.at[:, core, chip], send_sem.at[2], sibling)
    sent(cum_ref, send_sem.at[3], sibling)
    sent(send_ref, send_sem.at[6], sibling)
    sent(lout_ref, send_sem.at[7], sibling)

    @pl.when(has_down)
    def _():
        sent(out_ref, send_sem.at[5], down)

    @pl.when(feeds)
    def _():
        sent(kv_ref.at[:, core, chip], send_sem.at[0], down)

    if skips:

        @pl.when(chip == 0)
        def _():
            sent(kv_ref.at[0:skips, core, chip], send_sem.at[1], down)

    @pl.when(relays)
    def _():
        @pl.loop(0, chip)
        def _(j):
            sent(kv_ref.at[skips:, core, j], relay_send.at[j], down)
            sent(kv_ref.at[:, core, j], spread_send.at[j], sibling)

    @pl.when(is_helper)
    def _():
        if chips > 2:
            sent(kv_ref.at[:, core, 0 : chips - 2], spread_send.at[0], sibling)
        sent(part_ref, send_sem.at[4], down)

    @pl.when(is_tail)
    def _():
        sent(qt_ref, send_sem.at[4], up)


def store(s_ref, t_ref, s_out, t_out, sem):
    copies = [
        pltpu.make_async_copy(s_ref, s_out, sem.at[0]),
        pltpu.make_async_copy(t_ref, t_out, sem.at[1]),
    ]
    for copy in copies:
        copy.start()
    for copy in copies:
        copy.wait()


def on_device(
    student_x, student_z, student_b, student_c, step_size, decay_rate, norm_gain,
    teacher_q, teacher_k, teacher_v,
):
    n = lax.axis_size("seq")
    tokens, width = student_x.shape
    heads = step_size.shape[0]
    assert tokens == BLOCK and n % 2 == 0 and n >= 4
    gw = width // GROUPS
    state_dim = student_b.shape[1] // GROUPS
    kv_count = teacher_k.shape[1] // HEAD_SIZE
    assert kv_count == GROUPS
    qw = teacher_q.shape[1] // kv_count
    hbm = pl.BlockSpec(memory_space=pl.ANY)
    vmem = pl.BlockSpec(memory_space=pltpu.VMEM)
    dma = pltpu.SemaphoreType.DMA
    states = pltpu.VMEM((GROUPS, state_dim, gw // HALVES), BF16)
    queries = pltpu.VMEM((kv_count, HEAD_SIZE, qw), BF16)
    results = pl.pallas_call(
        functools.partial(kernel, n),
        out_shape=(
            pltpu.VMEM(student_x.shape, BF16),
            pltpu.VMEM(teacher_q.shape, BF16),
        ),
        in_specs=[hbm] * 10,
        out_specs=(vmem, vmem),
        scratch_shapes=[
            pltpu.VMEM(student_x.shape, BF16),
            pltpu.VMEM(student_z.shape, BF16),
            pltpu.VMEM(student_b.shape, BF16),
            pltpu.VMEM(student_c.shape, BF16),
            pltpu.VMEM(step_size.shape, F32),
            pltpu.VMEM((1, heads), F32),
            pltpu.VMEM((1, width), F32),
            pltpu.VMEM(teacher_q.shape, BF16),
            pltpu.VMEM((kv_count, 2, n // 2, 2, tokens, HEAD_SIZE), BF16),
            pltpu.VMEM(step_size.shape, F32),
            pltpu.VMEM(step_size.shape, F32),
            pltpu.VMEM((GROUPS, tokens, gw), F32),
            pltpu.VMEM((GROUPS, tokens, gw), F32),
            pltpu.VMEM((GROUPS, state_dim, gw), F32),
            states,
            states,
            states,
            pltpu.VMEM((GROUPS, HALVES, state_dim, gw // HALVES), BF16),
            states,
            states,
            queries,
            queries,
            pltpu.VMEM((kv_count, HEAD_SIZE, qw), F32),
            pltpu.VMEM((kv_count, 1, qw), F32),
            pltpu.VMEM((kv_count, 1, qw), F32),
            pltpu.VMEM((kv_count, qw + rows_for(qw // HEAD_SIZE), HEAD_SIZE), BF16),
            pltpu.VMEM((2, qw), F32),
            pltpu.VMEM((HEAD_SIZE, qw), F32),
            dma((9,)),
            dma((8,)),
            dma((max(n // 2 - 3, 1),)),
            dma((max(n // 2 - 3, 1),)),
            dma((kv_count, max(n // 2 - 2, 1))),
            dma((kv_count, max(n // 2 - 3, 1))),
        ]
        + [dma((GROUPS,))] * 4
        + [dma((2,))],
        compiler_params=pltpu.CompilerParams(
            collective_id=0, has_side_effects=True, vmem_limit_bytes=56 * 1024 * 1024
        ),
    )(
        student_x, student_z, student_b, student_c, step_size, decay_rate[None, :],
        norm_gain[None, :], teacher_q, teacher_k, teacher_v,
    )
    results = [pltpu.with_memory_space_constraint(r, pltpu.VMEM) for r in results]
    return pl.pallas_call(
        store,
        out_shape=(
            jax.ShapeDtypeStruct(student_x.shape, BF16),
            jax.ShapeDtypeStruct(teacher_q.shape, BF16),
        ),
        in_specs=[vmem, vmem],
        out_specs=(hbm, hbm),
        scratch_shapes=[dma((2,))],
    )(*results)


def solution(mesh):
    return jax.shard_map(
        on_device,
        mesh=mesh,
        in_specs=(
            P(("dp", "seq"), None),
            P(("dp", "seq"), None),
            P(("dp", "seq"), None),
            P(("dp", "seq"), None),
            P(None, ("dp", "seq")),
            P(),
            P(),
            P(("dp", "seq"), None),
            P(("dp", "seq"), None),
            P(("dp", "seq"), None),
        ),
        out_specs=(P(("dp", "seq"), None), P(("dp", "seq"), None)),
        check_vma=False,
    )
```

```python
import functools
import math

import jax
import jax.numpy as jnp
from jax import lax
from jax.experimental import pallas as pl
from jax.experimental.pallas import tpu as pltpu
from jax.sharding import PartitionSpec as P

GROUPS = 8
HEAD_SIZE = 128
BLOCK = 128
HALVES = 2
LEAD = 2
LAG = 1
OWN_LAG = 2
PIECES = 3
CUTS = 2
SKIPPED = 1

epsilon_norm = 1e-05
masked_score = -1e30
F32 = jnp.float32
BF16 = jnp.bfloat16
MESH = pl.DeviceIdType.MESH


def dot(a, b, ca=1, cb=0):
    return lax.dot_general(a, b, (((ca,), (cb,)), ((), ())), preferred_element_type=F32)


def rows_for(heads):
    return -(-heads * PIECES // 16) * 16


def kernel(
    n,
    x_hbm, z_hbm, b_hbm, c_hbm, step_hbm, rate_hbm, gain_hbm, q_hbm, k_hbm, v_hbm,
    so_ref, to_ref,
    x_ref, z_ref, b_ref, c_ref, step_ref, rate_ref, gain_ref, q_ref, kv_ref,
    cum_ref, csib_ref, ssm_ref, reach_ref, stl_ref, lout_ref, lsib_ref,
    raw_ref, st_ref, send_ref, out_ref,
    qt_ref, qtail_ref, acc_ref, max_ref, sum_ref, part_ref, stat_ref, tacc_ref,
    in_sem, send_sem, relay_send, spread_send, keys_recv, spread_recv, back_recv,
    state_recv, start_recv, local_recv, once_recv,
):
    me = lax.axis_index("seq")
    core = lax.rem(me, 2)
    chip = me // 2
    chips = n // 2
    sibling = me + 1 - 2 * core
    up = me - 2
    down = me + 2
    has_up = chip > 0
    has_down = chip < chips - 1
    is_tail = chip == chips - 1
    is_helper = chip == chips - 2
    feeds = chip < chips - 2
    relays = jnp.logical_and(has_up, feeds)
    skips = SKIPPED if chips == 4 else 0
    helper = 2 * (chips - 2) + core
    lag = jnp.where(feeds, 0, LAG)

    tokens, width = x_ref.shape
    heads = step_ref.shape[0]
    per_group = heads // GROUPS
    head_width = width // heads
    gw = width // GROUPS
    half_width = gw // HALVES
    state_dim = b_ref.shape[1] // GROUPS
    kv_count = kv_ref.shape[0]
    qw = q_ref.shape[1] // kv_count
    ratio = qw // HEAD_SIZE
    lanes = 128
    pack = lanes // head_width
    pairs = per_group // pack
    half_pairs = pairs // HALVES
    scale = math.log2(math.e) / math.sqrt(HEAD_SIZE)

    def span(g, size):
        return pl.ds(pl.multiple_of(g * size, 128), size)

    def to_seq(device):
        return dict(device_id={"seq": device}, device_id_type=MESH)

    key_loads = []
    for g in range(kv_count):
        for i, source in enumerate((k_hbm, v_hbm)):
            key_loads.append(
                pltpu.make_async_copy(
                    source.at[:, g * HEAD_SIZE : (g + 1) * HEAD_SIZE],
                    kv_ref.at[g, core, chip, i],
                    in_sem.at[0],
                )
            )
    own_keys = kv_ref.at[:, core, chip]
    all_keys = pltpu.make_async_copy(own_keys, own_keys, in_sem.at[0])
    loads = [
        pltpu.make_async_copy(src, dst, in_sem.at[i + 1])
        for i, (src, dst) in enumerate(
            (
                (step_hbm, step_ref), (rate_hbm, rate_ref), (q_hbm, q_ref),
                (b_hbm, b_ref), (c_hbm, c_ref), (x_hbm, x_ref), (z_hbm, z_ref), (gain_hbm, gain_ref),
            )
        )
    ]
    skip_pairs = ((0, helper), (chips - 2, core)) if skips else ()

    barrier = pltpu.get_barrier_semaphore()
    pl.semaphore_signal(barrier, inc=1, **to_seq(sibling))

    @pl.when(has_up)
    def _():
        pl.semaphore_signal(barrier, inc=1, **to_seq(up))

    @pl.when(has_down)
    def _():
        pl.semaphore_signal(barrier, inc=1, **to_seq(down))

    for source, target in skip_pairs:

        @pl.when(chip == source)
        def _():
            pl.semaphore_signal(barrier, inc=1, **to_seq(target))

    loads[0].start()
    loads[1].start()
    for load in key_loads:
        load.start()

    @pl.when(is_tail)
    def _():
        loads[2].start()

    for load in loads[3:]:
        load.start()

    @pl.when(jnp.logical_not(is_tail))
    def _():
        loads[2].start()

    def remote(source, target, sent, got, device):
        return pltpu.make_async_remote_copy(
            src_ref=source, dst_ref=target, send_sem=sent, recv_sem=got, **to_seq(device)
        )

    def key_own(g, device):
        block = kv_ref.at[g, core, chip]
        return remote(block, block, send_sem.at[0], keys_recv.at[g, chip], device)

    def key_relay(g, j):
        block = kv_ref.at[g, core, j]
        return remote(block, block, relay_send.at[j], keys_recv.at[g, j], down)

    def key_lazy(g):
        block = kv_ref.at[g, core, chip]
        return remote(block, block, send_sem.at[1], keys_recv.at[g, chip], down)

    def key_side(parity):
        block = kv_ref.at[:, parity, chip]
        return remote(block, block, send_sem.at[2], once_recv.at[0], sibling)

    def key_spread(g, j, parity):
        block = kv_ref.at[g, parity, j]
        return remote(block, block, spread_send.at[j], spread_recv.at[g, j], sibling)

    def key_spread_all(g, parity):
        blocks = kv_ref.at[g, parity, 0 : chips - 2]
        return remote(blocks, blocks, spread_send.at[0], spread_recv.at[g, 0], sibling)

    def cum_side():
        return remote(cum_ref, csib_ref, send_sem.at[3], once_recv.at[1], sibling)

    def query_up(g):
        return remote(qt_ref.at[g], qtail_ref.at[g], send_sem.at[4], back_recv.at[g], up)

    def part_down(g, start, stop):
        block = part_ref.at[g, start:stop]
        return remote(block, block, send_sem.at[4], back_recv.at[g], down)

    def state_down(g):
        return remote(out_ref.at[g], raw_ref.at[g], send_sem.at[5], state_recv.at[g], down)

    def state_side(g, half):
        return remote(send_ref.at[g], st_ref.at[g, half], send_sem.at[6], start_recv.at[g], sibling)

    def local_side(g):
        return remote(lout_ref.at[g], lsib_ref.at[g], send_sem.at[7], local_recv.at[g], sibling)

    def sent(block, semaphore, device):
        remote(block, block, semaphore, once_recv.at[0], device).wait_send()

    all_keys.wait()
    partners = 1 + has_up.astype(jnp.int32) + has_down.astype(jnp.int32)
    for source, _ in skip_pairs:
        partners = partners + (chip == source).astype(jnp.int32)
    pl.semaphore_wait(barrier, partners)

    @pl.when(feeds)
    def _():
        for g in range(LEAD):
            if g < skips:

                @pl.when(chip == 0)
                def _():
                    key_own(g, helper).start()

                @pl.when(has_up)
                def _():
                    key_own(g, down).start()
            else:
                key_own(g, down).start()

    key_side(core).start()
    loads[0].wait()
    loads[1].wait()
    eye = lax.broadcasted_iota(jnp.int32, (heads, heads), 0) == lax.broadcasted_iota(
        jnp.int32, (heads, heads), 1
    )
    rate = jnp.sum(jnp.where(eye, rate_ref[...], 0.0), axis=1, keepdims=True)
    running = -step_ref[...] * rate
    position = lax.broadcasted_iota(jnp.int32, (heads, tokens), 1)
    shift = 1
    while shift < tokens:
        running = running + jnp.where(position >= shift, pltpu.roll(running, shift, 1), 0.0)
        shift *= 2
    cum_ref[...] = running

    cum_side().start()

    def transpose_queries(g):
        for h in range(ratio):
            piece = q_ref[:, pl.ds(pl.multiple_of(g * qw + h * HEAD_SIZE, 128), HEAD_SIZE)]
            qt_ref[g, :, h * HEAD_SIZE : (h + 1) * HEAD_SIZE] = piece.T

    @pl.when(is_tail)
    def _():
        loads[2].wait()

        @pl.loop(0, kv_count)
        def _(g):
            transpose_queries(g)
            query_up(g).start()

    @pl.when(jnp.logical_not(has_up))
    def _():
        raw_ref[...] = jnp.zeros_like(raw_ref)

    for load in loads[3:7]:
        load.wait()

    key_at = lax.broadcasted_iota(jnp.int32, (tokens, tokens), 0)
    query_at = lax.broadcasted_iota(jnp.int32, (tokens, tokens), 1)
    lower = query_at <= key_at
    half = lax.broadcasted_iota(jnp.int32, (tokens, lanes), 1) // head_width
    row_half = lax.broadcasted_iota(jnp.int32, (1, lanes), 1) // head_width
    visible = lax.broadcasted_iota(jnp.int32, (2 * tokens, tokens), 0) <= (
        lax.broadcasted_iota(jnp.int32, (2 * tokens, tokens), 1) + core * tokens
    )

    def mask_last(scores):
        rows = scores.shape[0] // 2
        parts = []
        for parity in range(2):
            seen = visible[parity * tokens : (parity + 1) * tokens]
            part = scores[parity * rows : (parity + 1) * rows]
            parts += [part[: rows - tokens]] if rows > tokens else []
            parts.append(jnp.where(seen, part[rows - tokens :], masked_score))
        return jnp.concatenate(parts, axis=0)

    def columns_of(g, p):
        return pl.ds(pl.multiple_of(g * gw + p * lanes, 128), lanes)

    def student_local(g):
        cum = cum_ref[pl.ds(pl.multiple_of(g * per_group, 8), per_group), :]
        cum_t = cum.T
        tail = jnp.exp(cum[:, tokens - 1 : tokens] - cum)
        b = b_ref[:, span(g, state_dim)]
        b_t = b.T.astype(F32)
        products = dot(c_ref[:, span(g, state_dim)], b, 1, 1)
        for p in range(pairs):
            x = x_ref[:, columns_of(g, p)].astype(F32)
            mixes = []
            adds = []
            sources = []
            reach = None
            for j in range(pack):
                h = p * pack + j
                column = jnp.broadcast_to(cum_t[:, h : h + 1], (tokens, lanes))
                difference = jnp.where(lower, column - cum[h : h + 1, :], masked_score)
                mixes.append((products * jnp.exp(difference)).astype(BF16))
                adds.append((b_t * tail[h : h + 1, :]).astype(BF16))
                sources.append(jnp.where(half == j, x, 0.0).astype(BF16))
                reach = column if j == 0 else jnp.where(half == j, column, reach)
            z = z_ref[:, columns_of(g, p)].astype(F32)
            gate = z / (1.0 + jnp.exp(-z))
            at = slice(p * lanes, (p + 1) * lanes)
            source = jnp.concatenate(sources, axis=0)
            ssm_ref[g, :, at] = gate * dot(jnp.concatenate(mixes, axis=1), source)
            reach_ref[g, :, at] = gate * jnp.exp(reach)
            stl_ref[g, :, at] = dot(jnp.concatenate(adds, axis=1), source)
        lout_ref[g] = stl_ref[g, :, span(1 - core, half_width)].astype(BF16)
        local_side(g).start()

    def chain(g):
        local_side(g).wait_recv()

        @pl.when(has_up)
        def _():
            state_down(g).wait_recv()

        rows = pl.ds(pl.multiple_of(g * per_group, 8), per_group)
        total_own = jnp.exp(cum_ref[rows, tokens - 1 : tokens])
        total_sib = jnp.exp(csib_ref[rows, tokens - 1 : tokens])

        def decay_of(total, p):
            decay = total[p * pack : p * pack + 1, :]
            for j in range(1, pack):
                decay = jnp.where(row_half == j, total[p * pack + j : p * pack + j + 1, :], decay)
            return decay

        for part in range(HALVES):

            @pl.when(core == part)
            def _():
                for i in range(half_pairs):
                    p = part * half_pairs + i
                    at = slice(i * lanes, (i + 1) * lanes)
                    own = (decay_of(total_own, p), stl_ref[g, :, p * lanes : (p + 1) * lanes])
                    other = (decay_of(total_sib, p), lsib_ref[g, :, at].astype(F32))
                    first, second = (own, other) if part == 0 else (other, own)
                    raw = raw_ref[g, :, at]
                    middle = raw.astype(F32) * first[0] + first[1]
                    out_ref[g, :, at] = (middle * second[0] + second[1]).astype(BF16)
                    middle = middle.astype(BF16)
                    st_ref[g, part, :, at] = raw if part == 0 else middle
                    send_ref[g, :, at] = middle if part == 0 else raw

        @pl.when(has_down)
        def _():
            state_down(g).start()

        state_side(g, core).start()

    mean_of = jnp.where(
        lax.broadcasted_iota(jnp.int32, (lanes, lanes), 0) // head_width
        == lax.broadcasted_iota(jnp.int32, (lanes, lanes), 1) // head_width,
        1.0 / head_width,
        0.0,
    ).astype(BF16)

    def student_finish(g):
        state_side(g, 1 - core).wait_recv()
        c = c_ref[:, span(g, state_dim)]
        for part in range(HALVES):
            carried = dot(c, st_ref[g, part])
            for i in range(half_pairs):
                p = part * half_pairs + i
                at = slice(p * lanes, (p + 1) * lanes)
                gated = ssm_ref[g, :, at] + reach_ref[g, :, at] * carried[:, i * lanes : (i + 1) * lanes]
                mean = dot((gated * gated).astype(BF16), mean_of)
                so_ref[:, columns_of(g, p)] = (
                    gated * lax.rsqrt(mean + epsilon_norm) * gain_ref[:, columns_of(g, p)]
                ).astype(BF16)

    def head_at(h):
        return slice(h * HEAD_SIZE, (h + 1) * HEAD_SIZE)

    def pass_over(keys, values, queries, mask=None):
        scores = dot(keys, queries)
        if mask is not None:
            scores = mask(scores)
        top = jnp.max(scores, axis=0, keepdims=True)
        weight = jnp.exp2((scores - top) * scale)
        return top, jnp.sum(weight, axis=0, keepdims=True), dot(values, weight.astype(BF16), 0, 0)

    def join(first, second):
        top = jnp.maximum(first[0], second[0])
        one = jnp.exp2((first[0] - top) * scale)
        two = jnp.exp2((second[0] - top) * scale)
        return top, first[1] * one + second[1] * two, first[2] * one + second[2] * two

    def rows_of(g, kind, start, count):
        taken = kv_ref[g, :, pl.ds(start, count), kind]
        return taken.reshape(2 * count * tokens, HEAD_SIZE)

    def attend_own(g):
        keys = rows_of(g, 0, chip, 1)
        values = rows_of(g, 1, chip, 1)
        for h in range(ratio):
            at = head_at(h)
            max_ref[g, :, at], sum_ref[g, :, at], acc_ref[g, :, at] = pass_over(
                keys, values, qt_ref[g, :, at], mask_last
            )

    def attend_earlier(g):
        @pl.loop(0, chip)
        def _(j):
            keys = rows_of(g, 0, j, 1)
            values = rows_of(g, 1, j, 1)
            for h in range(ratio):
                at = head_at(h)
                held = (max_ref[g, :, at], sum_ref[g, :, at], acc_ref[g, :, at])
                max_ref[g, :, at], sum_ref[g, :, at], acc_ref[g, :, at] = join(
                    held, pass_over(keys, values, qt_ref[g, :, at])
                )

    chunk = max(k for k in range(1, 4) if (chips - 1) % k == 0)
    chunks = (chips - 1) // chunk
    log_rows = rows_for(ratio)

    def attend_tail(g):
        def keep(h, result):
            top, total, acc = result
            part_ref[g, h * HEAD_SIZE : (h + 1) * HEAD_SIZE] = (acc * (1.0 / total)).astype(BF16)
            rest = top * scale + jnp.log2(total)
            pieces = []
            for _ in range(PIECES):
                pieces.append(rest.astype(BF16))
                rest = rest - pieces[-1].astype(F32)
            return pieces

        def send(logs, heads_from, heads_to):
            if heads_to == ratio:
                rows = [piece for pieces in logs for piece in pieces]
                blank = jnp.zeros((log_rows - len(rows), HEAD_SIZE), BF16)
                part_ref[g, ratio * HEAD_SIZE :] = jnp.concatenate(rows + [blank], axis=0)
            part_down(g, heads_from * HEAD_SIZE, heads_to * HEAD_SIZE + (log_rows if heads_to == ratio else 0)).start()

        keys = rows_of(g, 0, 0, chunk)
        values = rows_of(g, 1, 0, chunk)
        logs = []
        for h in range(ratio):
            at = head_at(h)
            result = pass_over(keys, values, qtail_ref[g, :, at])
            if chunks == 1:
                logs.append(keep(h, result))
                if (h + 1) % (ratio // CUTS) == 0:
                    send(logs, h + 1 - ratio // CUTS, h + 1)
            else:
                stat_ref[0:1, at], stat_ref[1:2, at], tacc_ref[:, at] = result
        if chunks > 1:

            @pl.loop(1, chunks)
            def _(k):
                keys = rows_of(g, 0, k * chunk, chunk)
                values = rows_of(g, 1, k * chunk, chunk)
                for h in range(ratio):
                    at = head_at(h)
                    held = (stat_ref[0:1, at], stat_ref[1:2, at], tacc_ref[:, at])
                    stat_ref[0:1, at], stat_ref[1:2, at], tacc_ref[:, at] = join(
                        held, pass_over(keys, values, qtail_ref[g, :, at])
                    )

            for h in range(ratio):
                at = head_at(h)
                logs.append(keep(h, (stat_ref[0:1, at], stat_ref[1:2, at], tacc_ref[:, at])))
            send(logs, 0, ratio)

    def attend_all(g):
        if chunks > 1:
            attend_own(g)
            attend_earlier(g)
            finish_teacher(g)
        else:
            keys = rows_of(g, 0, 0, chunk)
            values = rows_of(g, 1, 0, chunk)
            for h in range(ratio):
                _, total, acc = pass_over(keys, values, qt_ref[g, :, head_at(h)], mask_last)
                write_teacher(g, h, acc * (1.0 / total))

    def write_teacher(g, h, result):
        to_ref[:, pl.ds(pl.multiple_of(g * qw + h * HEAD_SIZE, 128), HEAD_SIZE)] = result.astype(BF16).T

    def finish_teacher(g):
        for h in range(ratio):
            at = head_at(h)
            write_teacher(g, h, acc_ref[g, :, at] * (1.0 / sum_ref[g, :, at]))

    def merge_teacher(g):
        part_down(g, 0, ratio * HEAD_SIZE + log_rows).wait_recv()
        logs = part_ref[g, ratio * HEAD_SIZE :].astype(F32)
        for h in range(ratio):
            at = head_at(h)
            total = sum_ref[g, :, at]
            near = max_ref[g, :, at] * scale + jnp.log2(total)
            far = logs[h * PIECES : h * PIECES + 1]
            for i in range(1, PIECES):
                far = far + logs[h * PIECES + i : h * PIECES + i + 1]
            top = jnp.maximum(near, far)
            one = jnp.exp2(near - top)
            two = jnp.exp2(far - top)
            inverse = 1.0 / (one + two)
            part = part_ref[g, h * HEAD_SIZE : (h + 1) * HEAD_SIZE].astype(F32)
            write_teacher(g, h, acc_ref[g, :, at] * (one * inverse / total) + part * (two * inverse))

    def take_keys(g, onward):
        @pl.loop(0, chip)
        def _(i):
            j = chip - 1 - i
            key_relay(g, j).wait_recv()
            if onward:
                key_relay(g, j).start()
            key_spread(g, j, core).start()

    def attend_rest(g):
        @pl.loop(0, chip)
        def _(i):
            key_spread(g, chip - 1 - i, 1 - core).wait_recv()

        attend_earlier(g)
        finish_teacher(g)

    final = GROUPS - 1

    student_local(0)
    cum_side().wait_recv()

    @pl.loop(0, GROUPS + 1)
    def _(r):
        live = r < GROUPS

        @pl.when(relays)
        def _():
            @pl.loop(jnp.where(r == 0, skips, r + 1), jnp.minimum(r + 2, GROUPS))
            def _(g):
                take_keys(g, True)

        @pl.when(jnp.logical_and(live, is_helper))
        def _():
            @pl.loop(0, chip)
            def _(i):
                key_relay(r, chip - 1 - i).wait_recv()

            if chips > 2:
                key_spread_all(r, core).start()

        @pl.when(r < final)
        def _():
            student_local(r + 1)

        @pl.loop(jnp.where(feeds, GROUPS, jnp.maximum(r - lag - 1, 0)), jnp.where(live, jnp.maximum(r - lag, 0), GROUPS))
        def _(g):
            student_finish(g)

        @pl.when(jnp.logical_and(is_tail, r >= 1))
        def _():
            merge_teacher(r - 1)

        @pl.loop(
            jnp.where(live, jnp.maximum(r - lag, 0), GROUPS),
            jnp.where(r < final, jnp.maximum(r - lag + 1, 0), GROUPS),
        )
        def _(g):
            chain(g)

        @pl.loop(jnp.where(feeds, jnp.maximum(r - lag - 1, 0), GROUPS), jnp.where(live, jnp.maximum(r - lag, 0), GROUPS))
        def _(g):
            student_finish(g)

        @pl.when(jnp.logical_and(feeds, r + LEAD < GROUPS))
        def _():
            key_own(r + LEAD, down).start()

        @pl.when(r == 0)
        def _():
            key_side(1 - core).wait_recv()
            loads[7].wait()

            @pl.when(jnp.logical_not(is_tail))
            def _():
                loads[2].wait()

        @pl.when(live)
        def _():
            @pl.when(jnp.logical_not(jnp.logical_or(is_tail, is_helper)))
            def _():
                transpose_queries(r)

            @pl.when(is_helper)
            def _():
                if chips > 2:
                    key_spread_all(r, 1 - core).wait_recv()
                query_up(r).wait_recv()

                attend_tail(r)
                transpose_queries(r)

            @pl.when(jnp.logical_not(is_helper))
            def _():
                attend_own(r)

            @pl.when(jnp.logical_not(has_up))
            def _():
                @pl.when(jnp.logical_not(is_helper))
                def _():
                    finish_teacher(r)

        @pl.when(is_helper)
        def _():
            @pl.loop(jnp.where(live, jnp.maximum(r - OWN_LAG, 0), GROUPS - OWN_LAG), jnp.where(live, jnp.maximum(r - OWN_LAG + 1, 0), GROUPS))
            def _(g):
                attend_all(g)

    if skips:

        @pl.when(chip == 0)
        def _():
            for g in range(skips):
                key_lazy(g).start()

    @pl.when(relays)
    def _():
        for g in range(skips):
            take_keys(g, False)

        @pl.loop(0, GROUPS)
        def _(g):
            attend_rest(g)

    sent(kv_ref.at[:, core, chip], send_sem.at[2], sibling)
    sent(cum_ref, send_sem.at[3], sibling)
    sent(send_ref, send_sem.at[6], sibling)
    sent(lout_ref, send_sem.at[7], sibling)

    @pl.when(has_down)
    def _():
        sent(out_ref, send_sem.at[5], down)

    @pl.when(feeds)
    def _():
        sent(kv_ref.at[:, core, chip], send_sem.at[0], down)

    if skips:

        @pl.when(chip == 0)
        def _():
            sent(kv_ref.at[0:skips, core, chip], send_sem.at[1], down)

    @pl.when(relays)
    def _():
        @pl.loop(0, chip)
        def _(j):
            sent(kv_ref.at[skips:, core, j], relay_send.at[j], down)
            sent(kv_ref.at[:, core, j], spread_send.at[j], sibling)

    @pl.when(is_helper)
    def _():
        if chips > 2:
            sent(kv_ref.at[:, core, 0 : chips - 2], spread_send.at[0], sibling)
        sent(part_ref, send_sem.at[4], down)

    @pl.when(is_tail)
    def _():
        sent(qt_ref, send_sem.at[4], up)


def store(s_ref, t_ref, s_out, t_out, sem):
    copies = [
        pltpu.make_async_copy(s_ref, s_out, sem.at[0]),
        pltpu.make_async_copy(t_ref, t_out, sem.at[1]),
    ]
    for copy in copies:
        copy.start()
    for copy in copies:
        copy.wait()


def on_device(
    student_x, student_z, student_b, student_c, step_size, decay_rate, norm_gain,
    teacher_q, teacher_k, teacher_v,
):
    n = lax.axis_size("seq")
    tokens, width = student_x.shape
    heads = step_size.shape[0]
    assert tokens == BLOCK and n % 2 == 0 and n >= 4
    gw = width // GROUPS
    state_dim = student_b.shape[1] // GROUPS
    kv_count = teacher_k.shape[1] // HEAD_SIZE
    assert kv_count == GROUPS
    qw = teacher_q.shape[1] // kv_count
    hbm = pl.BlockSpec(memory_space=pl.ANY)
    vmem = pl.BlockSpec(memory_space=pltpu.VMEM)
    dma = pltpu.SemaphoreType.DMA
    states = pltpu.VMEM((GROUPS, state_dim, gw // HALVES), BF16)
    queries = pltpu.VMEM((kv_count, HEAD_SIZE, qw), BF16)
    results = pl.pallas_call(
        functools.partial(kernel, n),
        out_shape=(
            pltpu.VMEM(student_x.shape, BF16),
            pltpu.VMEM(teacher_q.shape, BF16),
        ),
        in_specs=[hbm] * 10,
        out_specs=(vmem, vmem),
        scratch_shapes=[
            pltpu.VMEM(student_x.shape, BF16),
            pltpu.VMEM(student_z.shape, BF16),
            pltpu.VMEM(student_b.shape, BF16),
            pltpu.VMEM(student_c.shape, BF16),
            pltpu.VMEM(step_size.shape, F32),
            pltpu.VMEM((1, heads), F32),
            pltpu.VMEM((1, width), F32),
            pltpu.VMEM(teacher_q.shape, BF16),
            pltpu.VMEM((kv_count, 2, n // 2, 2, tokens, HEAD_SIZE), BF16),
            pltpu.VMEM(step_size.shape, F32),
            pltpu.VMEM(step_size.shape, F32),
            pltpu.VMEM((GROUPS, tokens, gw), F32),
            pltpu.VMEM((GROUPS, tokens, gw), F32),
            pltpu.VMEM((GROUPS, state_dim, gw), F32),
            states,
            states,
            states,
            pltpu.VMEM((GROUPS, HALVES, state_dim, gw // HALVES), BF16),
            states,
            states,
            queries,
            queries,
            pltpu.VMEM((kv_count, HEAD_SIZE, qw), F32),
            pltpu.VMEM((kv_count, 1, qw), F32),
            pltpu.VMEM((kv_count, 1, qw), F32),
            pltpu.VMEM((kv_count, qw + rows_for(qw // HEAD_SIZE), HEAD_SIZE), BF16),
            pltpu.VMEM((2, qw), F32),
            pltpu.VMEM((HEAD_SIZE, qw), F32),
            dma((9,)),
            dma((8,)),
            dma((max(n // 2 - 3, 1),)),
            dma((max(n // 2 - 3, 1),)),
            dma((kv_count, max(n // 2 - 2, 1))),
            dma((kv_count, max(n // 2 - 3, 1))),
        ]
        + [dma((GROUPS,))] * 4
        + [dma((2,))],
        compiler_params=pltpu.CompilerParams(
            collective_id=0, has_side_effects=True, vmem_limit_bytes=56 * 1024 * 1024
        ),
    )(
        student_x, student_z, student_b, student_c, step_size, decay_rate[None, :],
        norm_gain[None, :], teacher_q, teacher_k, teacher_v,
    )
    results = [pltpu.with_memory_space_constraint(r, pltpu.VMEM) for r in results]
    return pl.pallas_call(
        store,
        out_shape=(
            jax.ShapeDtypeStruct(student_x.shape, BF16),
            jax.ShapeDtypeStruct(teacher_q.shape, BF16),
        ),
        in_specs=[vmem, vmem],
        out_specs=(hbm, hbm),
        scratch_shapes=[dma((2,))],
    )(*results)


def solution(mesh):
    return jax.shard_map(
        on_device,
        mesh=mesh,
        in_specs=(
            P(("dp", "seq"), None),
            P(("dp", "seq"), None),
            P(("dp", "seq"), None),
            P(("dp", "seq"), None),
            P(None, ("dp", "seq")),
            P(),
            P(),
            P(("dp", "seq"), None),
            P(("dp", "seq"), None),
            P(("dp", "seq"), None),
        ),
        out_specs=(P(("dp", "seq"), None), P(("dp", "seq"), None)),
        check_vma=False,
    )
```

```python
import functools
import math

import jax
import jax.numpy as jnp
from jax import lax
from jax.experimental import pallas as pl
from jax.experimental.pallas import tpu as pltpu
from jax.sharding import PartitionSpec as P

GROUPS = 8
HEAD_SIZE = 128
BLOCK = 128
HALVES = 2
LEAD = 2
LAG = 1
OWN_LAG = 2
PIECES = 3
CUTS = 2
SKIPPED = 1

epsilon_norm = 1e-05
masked_score = -1e30
F32 = jnp.float32
BF16 = jnp.bfloat16
MESH = pl.DeviceIdType.MESH


def dot(a, b, ca=1, cb=0):
    return lax.dot_general(a, b, (((ca,), (cb,)), ((), ())), preferred_element_type=F32)


def rows_for(heads):
    return -(-heads * PIECES // 16) * 16


def kernel(
    n,
    x_hbm, z_hbm, b_hbm, c_hbm, step_hbm, rate_hbm, gain_hbm, q_hbm, k_hbm, v_hbm,
    so_ref, to_ref,
    x_ref, z_ref, b_ref, c_ref, step_ref, rate_ref, gain_ref, q_ref, kv_ref,
    cum_ref, csib_ref, ssm_ref, reach_ref, stl_ref, lout_ref, lsib_ref,
    raw_ref, st_ref, send_ref, out_ref,
    qt_ref, qtail_ref, acc_ref, max_ref, sum_ref, part_ref, stat_ref, tacc_ref,
    in_sem, send_sem, relay_send, spread_send, keys_recv, spread_recv, back_recv,
    state_recv, start_recv, local_recv, once_recv,
):
    me = lax.axis_index("seq")
    core = lax.rem(me, 2)
    chip = me // 2
    chips = n // 2
    sibling = me + 1 - 2 * core
    up = me - 2
    down = me + 2
    has_up = chip > 0
    relay_count = max(chips - 3, 1)
    key_slots = keys_recv.shape[1]
    has_down = chip < chips - 1
    is_tail = chip == chips - 1
    is_helper = chip == chips - 2
    feeds = chip < chips - 2
    relays = jnp.logical_and(has_up, feeds)
    skips = SKIPPED if chips == 4 else 0
    helper = 2 * (chips - 2) + core
    lag = jnp.where(feeds, 0, LAG)

    tokens, width = x_ref.shape
    heads = step_ref.shape[0]
    per_group = heads // GROUPS
    head_width = width // heads
    gw = width // GROUPS
    half_width = gw // HALVES
    state_dim = b_ref.shape[1] // GROUPS
    kv_count = kv_ref.shape[0]
    qw = q_ref.shape[1] // kv_count
    ratio = qw // HEAD_SIZE
    lanes = 128
    pack = lanes // head_width
    pairs = per_group // pack
    half_pairs = pairs // HALVES
    scale = math.log2(math.e) / math.sqrt(HEAD_SIZE)

    def span(g, size):
        return pl.ds(pl.multiple_of(g * size, 128), size)

    def to_seq(device):
        return dict(device_id={"seq": device}, device_id_type=MESH)

    key_loads = []
    for g in range(kv_count):
        for i, source in enumerate((k_hbm, v_hbm)):
            key_loads.append(
                pltpu.make_async_copy(
                    source.at[:, g * HEAD_SIZE : (g + 1) * HEAD_SIZE],
                    kv_ref.at[g, core, chip, i],
                    in_sem.at[0],
                )
            )
    own_keys = kv_ref.at[:, core, chip]
    all_keys = pltpu.make_async_copy(own_keys, own_keys, in_sem.at[0])
    loads = [
        pltpu.make_async_copy(src, dst, in_sem.at[i + 1])
        for i, (src, dst) in enumerate(
            (
                (step_hbm, step_ref), (rate_hbm, rate_ref), (q_hbm, q_ref),
                (b_hbm, b_ref), (c_hbm, c_ref), (x_hbm, x_ref), (z_hbm, z_ref), (gain_hbm, gain_ref),
            )
        )
    ]
    skip_pairs = ((0, helper), (chips - 2, core)) if skips else ()

    barrier = pltpu.get_barrier_semaphore()
    pl.semaphore_signal(barrier, inc=1, **to_seq(sibling))

    @pl.when(has_up)
    def _():
        pl.semaphore_signal(barrier, inc=1, **to_seq(up))

    @pl.when(has_down)
    def _():
        pl.semaphore_signal(barrier, inc=1, **to_seq(down))

    for source, target in skip_pairs:

        @pl.when(chip == source)
        def _():
            pl.semaphore_signal(barrier, inc=1, **to_seq(target))

    loads[0].start()
    loads[1].start()
    for load in key_loads:
        load.start()

    @pl.when(is_tail)
    def _():
        loads[2].start()

    for load in loads[3:]:
        load.start()

    @pl.when(jnp.logical_not(is_tail))
    def _():
        loads[2].start()

    def remote(source, target, sent, got, device):
        return pltpu.make_async_remote_copy(
            src_ref=source, dst_ref=target, send_sem=sent, recv_sem=got, **to_seq(device)
        )

    def key_own(g, device):
        block = kv_ref.at[g, core, chip]
        return remote(block, block, send_sem.at[0], keys_recv.at[g, jnp.minimum(chip, key_slots - 1)], device)

    def key_relay(g, j):
        block = kv_ref.at[g, core, j]
        return remote(block, block, relay_send.at[jnp.minimum(j, relay_count - 1)], keys_recv.at[g, jnp.minimum(j, key_slots - 1)], down)

    def key_all(g):
        blocks = kv_ref.at[g, core, 0 : chips - 2]
        return remote(blocks, blocks, send_sem.at[0], keys_recv.at[g, 0], down)

    def key_lazy(g):
        block = kv_ref.at[g, core, chip]
        return remote(block, block, send_sem.at[1], keys_recv.at[g, jnp.minimum(chip, key_slots - 1)], down)

    def key_side(parity):
        block = kv_ref.at[:, parity, chip]
        return remote(block, block, send_sem.at[2], once_recv.at[0], sibling)

    def key_spread(g, j, parity):
        block = kv_ref.at[g, parity, j]
        return remote(block, block, spread_send.at[j], spread_recv.at[g, j], sibling)

    def key_spread_all(g, parity):
        blocks = kv_ref.at[g, parity, 0 : chips - 2]
        return remote(blocks, blocks, spread_send.at[0], spread_recv.at[g, 0], sibling)

    def cum_side():
        return remote(cum_ref, csib_ref, send_sem.at[3], once_recv.at[1], sibling)

    def query_up(g):
        return remote(qt_ref.at[g], qtail_ref.at[g], send_sem.at[4], back_recv.at[g], up)

    def part_down(g, start, stop):
        block = part_ref.at[g, start:stop]
        return remote(block, block, send_sem.at[4], back_recv.at[g], down)

    def state_down(g):
        return remote(out_ref.at[g], raw_ref.at[g], send_sem.at[5], state_recv.at[g], down)

    def state_side(g, half):
        return remote(send_ref.at[g], st_ref.at[g, half], send_sem.at[6], start_recv.at[g], sibling)

    def local_side(g):
        return remote(lout_ref.at[g], lsib_ref.at[g], send_sem.at[7], local_recv.at[g], sibling)

    def sent(block, semaphore, device):
        remote(block, block, semaphore, once_recv.at[0], device).wait_send()

    all_keys.wait()
    partners = 1 + has_up.astype(jnp.int32) + has_down.astype(jnp.int32)
    for source, _ in skip_pairs:
        partners = partners + (chip == source).astype(jnp.int32)
    pl.semaphore_wait(barrier, partners)

    @pl.when(feeds)
    def _():
        for g in range(LEAD):
            if g < skips:

                @pl.when(chip == 0)
                def _():
                    key_own(g, helper).start()

                @pl.when(has_up)
                def _():
                    key_own(g, down).start()
            else:
                key_own(g, down).start()

    key_side(core).start()
    loads[0].wait()
    loads[1].wait()
    eye = lax.broadcasted_iota(jnp.int32, (heads, heads), 0) == lax.broadcasted_iota(
        jnp.int32, (heads, heads), 1
    )
    rate = jnp.sum(jnp.where(eye, rate_ref[...], 0.0), axis=1, keepdims=True)
    running = -step_ref[...] * rate
    position = lax.broadcasted_iota(jnp.int32, (heads, tokens), 1)
    shift = 1
    while shift < tokens:
        running = running + jnp.where(position >= shift, pltpu.roll(running, shift, 1), 0.0)
        shift *= 2
    cum_ref[...] = running

    cum_side().start()

    def transpose_queries(g):
        for h in range(ratio):
            piece = q_ref[:, pl.ds(pl.multiple_of(g * qw + h * HEAD_SIZE, 128), HEAD_SIZE)]
            qt_ref[g, :, h * HEAD_SIZE : (h + 1) * HEAD_SIZE] = piece.T

    @pl.when(is_tail)
    def _():
        loads[2].wait()

        @pl.loop(0, kv_count)
        def _(g):
            transpose_queries(g)
            query_up(g).start()

    @pl.when(jnp.logical_not(has_up))
    def _():
        raw_ref[...] = jnp.zeros_like(raw_ref)

    for load in loads[3:7]:
        load.wait()

    key_at = lax.broadcasted_iota(jnp.int32, (tokens, tokens), 0)
    query_at = lax.broadcasted_iota(jnp.int32, (tokens, tokens), 1)
    lower = query_at <= key_at
    half = lax.broadcasted_iota(jnp.int32, (tokens, lanes), 1) // head_width
    row_half = lax.broadcasted_iota(jnp.int32, (1, lanes), 1) // head_width
    visible = lax.broadcasted_iota(jnp.int32, (2 * tokens, tokens), 0) <= (
        lax.broadcasted_iota(jnp.int32, (2 * tokens, tokens), 1) + core * tokens
    )

    def mask_last(scores):
        rows = scores.shape[0] // 2
        parts = []
        for parity in range(2):
            seen = visible[parity * tokens : (parity + 1) * tokens]
            part = scores[parity * rows : (parity + 1) * rows]
            parts += [part[: rows - tokens]] if rows > tokens else []
            parts.append(jnp.where(seen, part[rows - tokens :], masked_score))
        return jnp.concatenate(parts, axis=0)

    def columns_of(g, p):
        return pl.ds(pl.multiple_of(g * gw + p * lanes, 128), lanes)

    def student_local(g):
        cum = cum_ref[pl.ds(pl.multiple_of(g * per_group, 8), per_group), :]
        cum_t = cum.T
        tail = jnp.exp(cum[:, tokens - 1 : tokens] - cum)
        b = b_ref[:, span(g, state_dim)]
        b_t = b.T.astype(F32)
        products = dot(c_ref[:, span(g, state_dim)], b, 1, 1)
        for p in range(pairs):
            x = x_ref[:, columns_of(g, p)].astype(F32)
            mixes = []
            adds = []
            sources = []
            reach = None
            for j in range(pack):
                h = p * pack + j
                column = jnp.broadcast_to(cum_t[:, h : h + 1], (tokens, lanes))
                difference = jnp.where(lower, column - cum[h : h + 1, :], masked_score)
                mixes.append((products * jnp.exp(difference)).astype(BF16))
                adds.append((b_t * tail[h : h + 1, :]).astype(BF16))
                sources.append(jnp.where(half == j, x, 0.0).astype(BF16))
                reach = column if j == 0 else jnp.where(half == j, column, reach)
            z = z_ref[:, columns_of(g, p)].astype(F32)
            gate = z / (1.0 + jnp.exp(-z))
            at = slice(p * lanes, (p + 1) * lanes)
            source = jnp.concatenate(sources, axis=0)
            ssm_ref[g, :, at] = gate * dot(jnp.concatenate(mixes, axis=1), source)
            reach_ref[g, :, at] = gate * jnp.exp(reach)
            stl_ref[g, :, at] = dot(jnp.concatenate(adds, axis=1), source)
        lout_ref[g] = stl_ref[g, :, span(1 - core, half_width)].astype(BF16)
        local_side(g).start()

    def chain(g):
        local_side(g).wait_recv()

        @pl.when(has_up)
        def _():
            state_down(g).wait_recv()

        rows = pl.ds(pl.multiple_of(g * per_group, 8), per_group)
        total_own = jnp.exp(cum_ref[rows, tokens - 1 : tokens])
        total_sib = jnp.exp(csib_ref[rows, tokens - 1 : tokens])

        def decay_of(total, p):
            decay = total[p * pack : p * pack + 1, :]
            for j in range(1, pack):
                decay = jnp.where(row_half == j, total[p * pack + j : p * pack + j + 1, :], decay)
            return decay

        for part in range(HALVES):

            @pl.when(core == part)
            def _():
                for i in range(half_pairs):
                    p = part * half_pairs + i
                    at = slice(i * lanes, (i + 1) * lanes)
                    own = (decay_of(total_own, p), stl_ref[g, :, p * lanes : (p + 1) * lanes])
                    other = (decay_of(total_sib, p), lsib_ref[g, :, at].astype(F32))
                    first, second = (own, other) if part == 0 else (other, own)
                    raw = raw_ref[g, :, at]
                    middle = raw.astype(F32) * first[0] + first[1]
                    out_ref[g, :, at] = (middle * second[0] + second[1]).astype(BF16)
                    middle = middle.astype(BF16)
                    st_ref[g, part, :, at] = raw if part == 0 else middle
                    send_ref[g, :, at] = middle if part == 0 else raw

        @pl.when(has_down)
        def _():
            state_down(g).start()

        state_side(g, core).start()

    mean_of = jnp.where(
        lax.broadcasted_iota(jnp.int32, (lanes, lanes), 0) // head_width
        == lax.broadcasted_iota(jnp.int32, (lanes, lanes), 1) // head_width,
        1.0 / head_width,
        0.0,
    ).astype(BF16)

    def student_finish(g):
        state_side(g, 1 - core).wait_recv()
        c = c_ref[:, span(g, state_dim)]
        for part in range(HALVES):
            carried = dot(c, st_ref[g, part])
            for i in range(half_pairs):
                p = part * half_pairs + i
                at = slice(p * lanes, (p + 1) * lanes)
                gated = ssm_ref[g, :, at] + reach_ref[g, :, at] * carried[:, i * lanes : (i + 1) * lanes]
                mean = dot((gated * gated).astype(BF16), mean_of)
                so_ref[:, columns_of(g, p)] = (
                    gated * lax.rsqrt(mean + epsilon_norm) * gain_ref[:, columns_of(g, p)]
                ).astype(BF16)

    def head_at(h):
        return slice(h * HEAD_SIZE, (h + 1) * HEAD_SIZE)

    def pass_over(keys, values, queries, mask=None):
        scores = dot(keys, queries)
        if mask is not None:
            scores = mask(scores)
        top = jnp.max(scores, axis=0, keepdims=True)
        weight = jnp.exp2((scores - top) * scale)
        return top, jnp.sum(weight, axis=0, keepdims=True), dot(values, weight.astype(BF16), 0, 0)

    def join(first, second):
        top = jnp.maximum(first[0], second[0])
        one = jnp.exp2((first[0] - top) * scale)
        two = jnp.exp2((second[0] - top) * scale)
        return top, first[1] * one + second[1] * two, first[2] * one + second[2] * two

    def rows_of(g, kind, start, count):
        taken = kv_ref[g, :, pl.ds(start, count), kind]
        return taken.reshape(2 * count * tokens, HEAD_SIZE)

    def attend_own(g):
        keys = rows_of(g, 0, chip, 1)
        values = rows_of(g, 1, chip, 1)
        for h in range(ratio):
            at = head_at(h)
            max_ref[g, :, at], sum_ref[g, :, at], acc_ref[g, :, at] = pass_over(
                keys, values, qt_ref[g, :, at], mask_last
            )

    def attend_earlier(g):
        @pl.loop(0, chip)
        def _(j):
            keys = rows_of(g, 0, j, 1)
            values = rows_of(g, 1, j, 1)
            for h in range(ratio):
                at = head_at(h)
                held = (max_ref[g, :, at], sum_ref[g, :, at], acc_ref[g, :, at])
                max_ref[g, :, at], sum_ref[g, :, at], acc_ref[g, :, at] = join(
                    held, pass_over(keys, values, qt_ref[g, :, at])
                )

    chunk = max(k for k in range(1, 4) if (chips - 1) % k == 0)
    chunks = (chips - 1) // chunk
    log_rows = rows_for(ratio)

    def attend_tail(g):
        def keep(h, result):
            top, total, acc = result
            part_ref[g, h * HEAD_SIZE : (h + 1) * HEAD_SIZE] = (acc * (1.0 / total)).astype(BF16)
            rest = top * scale + jnp.log2(total)
            pieces = []
            for _ in range(PIECES):
                pieces.append(rest.astype(BF16))
                rest = rest - pieces[-1].astype(F32)
            return pieces

        def send(logs, heads_from, heads_to):
            if heads_to == ratio:
                rows = [piece for pieces in logs for piece in pieces]
                blank = jnp.zeros((log_rows - len(rows), HEAD_SIZE), BF16)
                part_ref[g, ratio * HEAD_SIZE :] = jnp.concatenate(rows + [blank], axis=0)
            part_down(g, heads_from * HEAD_SIZE, heads_to * HEAD_SIZE + (log_rows if heads_to == ratio else 0)).start()

        keys = rows_of(g, 0, 0, chunk)
        values = rows_of(g, 1, 0, chunk)
        logs = []
        for h in range(ratio):
            at = head_at(h)
            result = pass_over(keys, values, qtail_ref[g, :, at])
            if chunks == 1:
                logs.append(keep(h, result))
                if (h + 1) % (ratio // CUTS) == 0:
                    send(logs, h + 1 - ratio // CUTS, h + 1)
            else:
                stat_ref[0:1, at], stat_ref[1:2, at], tacc_ref[:, at] = result
        if chunks > 1:

            @pl.loop(1, chunks)
            def _(k):
                keys = rows_of(g, 0, k * chunk, chunk)
                values = rows_of(g, 1, k * chunk, chunk)
                for h in range(ratio):
                    at = head_at(h)
                    held = (stat_ref[0:1, at], stat_ref[1:2, at], tacc_ref[:, at])
                    stat_ref[0:1, at], stat_ref[1:2, at], tacc_ref[:, at] = join(
                        held, pass_over(keys, values, qtail_ref[g, :, at])
                    )

            for h in range(ratio):
                at = head_at(h)
                logs.append(keep(h, (stat_ref[0:1, at], stat_ref[1:2, at], tacc_ref[:, at])))
            send(logs, 0, ratio)

    def attend_all(g):
        if chunks > 1:
            attend_own(g)
            attend_earlier(g)
            finish_teacher(g)
        else:
            keys = rows_of(g, 0, 0, chunk)
            values = rows_of(g, 1, 0, chunk)
            for h in range(ratio):
                _, total, acc = pass_over(keys, values, qt_ref[g, :, head_at(h)], mask_last)
                write_teacher(g, h, acc * (1.0 / total))

    def write_teacher(g, h, result):
        to_ref[:, pl.ds(pl.multiple_of(g * qw + h * HEAD_SIZE, 128), HEAD_SIZE)] = result.astype(BF16).T

    def finish_teacher(g):
        for h in range(ratio):
            at = head_at(h)
            write_teacher(g, h, acc_ref[g, :, at] * (1.0 / sum_ref[g, :, at]))

    def merge_teacher(g):
        part_down(g, 0, ratio * HEAD_SIZE + log_rows).wait_recv()
        logs = part_ref[g, ratio * HEAD_SIZE :].astype(F32)
        for h in range(ratio):
            at = head_at(h)
            total = sum_ref[g, :, at]
            near = max_ref[g, :, at] * scale + jnp.log2(total)
            far = logs[h * PIECES : h * PIECES + 1]
            for i in range(1, PIECES):
                far = far + logs[h * PIECES + i : h * PIECES + i + 1]
            top = jnp.maximum(near, far)
            one = jnp.exp2(near - top)
            two = jnp.exp2(far - top)
            inverse = 1.0 / (one + two)
            part = part_ref[g, h * HEAD_SIZE : (h + 1) * HEAD_SIZE].astype(F32)
            write_teacher(g, h, acc_ref[g, :, at] * (one * inverse / total) + part * (two * inverse))

    def take_keys(g, onward):
        @pl.loop(0, chip)
        def _(i):
            j = chip - 1 - i
            key_relay(g, j).wait_recv()
            if onward:
                key_relay(g, j).start()
            key_spread(g, j, core).start()

    def attend_rest(g):
        @pl.loop(0, chip)
        def _(i):
            key_spread(g, chip - 1 - i, 1 - core).wait_recv()

        attend_earlier(g)
        finish_teacher(g)

    final = GROUPS - 1

    student_local(0)
    cum_side().wait_recv()

    @pl.loop(0, GROUPS + 1)
    def _(r):
        live = r < GROUPS

        @pl.when(relays)
        def _():
            @pl.loop(jnp.where(r == 0, skips, r + 1), jnp.minimum(r + 2, GROUPS))
            def _(g):
                take_keys(g, True)

        @pl.when(jnp.logical_and(live, is_helper))
        def _():
            if key_slots < chips - 2:
                key_all(r).wait_recv()
            else:

                @pl.loop(0, chip)
                def _(i):
                    key_relay(r, chip - 1 - i).wait_recv()

            if chips > 2:
                key_spread_all(r, core).start()

        @pl.when(r < final)
        def _():
            student_local(r + 1)

        @pl.loop(jnp.where(feeds, GROUPS, jnp.maximum(r - lag - 1, 0)), jnp.where(live, jnp.maximum(r - lag, 0), GROUPS))
        def _(g):
            student_finish(g)

        @pl.when(jnp.logical_and(is_tail, r >= 1))
        def _():
            merge_teacher(r - 1)

        @pl.loop(
            jnp.where(live, jnp.maximum(r - lag, 0), GROUPS),
            jnp.where(r < final, jnp.maximum(r - lag + 1, 0), GROUPS),
        )
        def _(g):
            chain(g)

        @pl.loop(jnp.where(feeds, jnp.maximum(r - lag - 1, 0), GROUPS), jnp.where(live, jnp.maximum(r - lag, 0), GROUPS))
        def _(g):
            student_finish(g)

        @pl.when(jnp.logical_and(feeds, r + LEAD < GROUPS))
        def _():
            key_own(r + LEAD, down).start()

        @pl.when(r == 0)
        def _():
            key_side(1 - core).wait_recv()
            loads[7].wait()

            @pl.when(jnp.logical_not(is_tail))
            def _():
                loads[2].wait()

        @pl.when(live)
        def _():
            @pl.when(jnp.logical_not(jnp.logical_or(is_tail, is_helper)))
            def _():
                transpose_queries(r)

            @pl.when(is_helper)
            def _():
                if chips > 2:
                    key_spread_all(r, 1 - core).wait_recv()
                query_up(r).wait_recv()

                attend_tail(r)
                transpose_queries(r)

            @pl.when(jnp.logical_not(is_helper))
            def _():
                attend_own(r)

            @pl.when(jnp.logical_not(has_up))
            def _():
                @pl.when(jnp.logical_not(is_helper))
                def _():
                    finish_teacher(r)

        @pl.when(is_helper)
        def _():
            @pl.loop(jnp.where(live, jnp.maximum(r - OWN_LAG, 0), GROUPS - OWN_LAG), jnp.where(live, jnp.maximum(r - OWN_LAG + 1, 0), GROUPS))
            def _(g):
                attend_all(g)

    if skips:

        @pl.when(chip == 0)
        def _():
            for g in range(skips):
                key_lazy(g).start()

    @pl.when(relays)
    def _():
        for g in range(skips):
            take_keys(g, False)

        @pl.loop(0, GROUPS)
        def _(g):
            attend_rest(g)

    sent(kv_ref.at[:, core, chip], send_sem.at[2], sibling)
    sent(cum_ref, send_sem.at[3], sibling)
    sent(send_ref, send_sem.at[6], sibling)
    sent(lout_ref, send_sem.at[7], sibling)

    @pl.when(has_down)
    def _():
        sent(out_ref, send_sem.at[5], down)

    @pl.when(feeds)
    def _():
        sent(kv_ref.at[:, core, chip], send_sem.at[0], down)

    if skips:

        @pl.when(chip == 0)
        def _():
            sent(kv_ref.at[0:skips, core, chip], send_sem.at[1], down)

    @pl.when(relays)
    def _():
        @pl.loop(0, chip)
        def _(j):
            sent(kv_ref.at[skips:, core, j], relay_send.at[j], down)
            sent(kv_ref.at[:, core, j], spread_send.at[j], sibling)

    @pl.when(is_helper)
    def _():
        if chips > 2:
            sent(kv_ref.at[:, core, 0 : chips - 2], spread_send.at[0], sibling)
        sent(part_ref, send_sem.at[4], down)

    @pl.when(is_tail)
    def _():
        sent(qt_ref, send_sem.at[4], up)


def store(s_ref, t_ref, s_out, t_out, sem):
    copies = [
        pltpu.make_async_copy(s_ref, s_out, sem.at[0]),
        pltpu.make_async_copy(t_ref, t_out, sem.at[1]),
    ]
    for copy in copies:
        copy.start()
    for copy in copies:
        copy.wait()


def on_device(
    student_x, student_z, student_b, student_c, step_size, decay_rate, norm_gain,
    teacher_q, teacher_k, teacher_v,
):
    n = lax.axis_size("seq")
    tokens, width = student_x.shape
    heads = step_size.shape[0]
    assert tokens == BLOCK and n % 2 == 0 and n >= 4
    gw = width // GROUPS
    state_dim = student_b.shape[1] // GROUPS
    kv_count = teacher_k.shape[1] // HEAD_SIZE
    assert kv_count == GROUPS
    qw = teacher_q.shape[1] // kv_count
    hbm = pl.BlockSpec(memory_space=pl.ANY)
    vmem = pl.BlockSpec(memory_space=pltpu.VMEM)
    dma = pltpu.SemaphoreType.DMA
    states = pltpu.VMEM((GROUPS, state_dim, gw // HALVES), BF16)
    queries = pltpu.VMEM((kv_count, HEAD_SIZE, qw), BF16)
    results = pl.pallas_call(
        functools.partial(kernel, n),
        out_shape=(
            pltpu.VMEM(student_x.shape, BF16),
            pltpu.VMEM(teacher_q.shape, BF16),
        ),
        in_specs=[hbm] * 10,
        out_specs=(vmem, vmem),
        scratch_shapes=[
            pltpu.VMEM(student_x.shape, BF16),
            pltpu.VMEM(student_z.shape, BF16),
            pltpu.VMEM(student_b.shape, BF16),
            pltpu.VMEM(student_c.shape, BF16),
            pltpu.VMEM(step_size.shape, F32),
            pltpu.VMEM((1, heads), F32),
            pltpu.VMEM((1, width), F32),
            pltpu.VMEM(teacher_q.shape, BF16),
            pltpu.VMEM((kv_count, 2, n // 2, 2, tokens, HEAD_SIZE), BF16),
            pltpu.VMEM(step_size.shape, F32),
            pltpu.VMEM(step_size.shape, F32),
            pltpu.VMEM((GROUPS, tokens, gw), F32),
            pltpu.VMEM((GROUPS, tokens, gw), F32),
            pltpu.VMEM((GROUPS, state_dim, gw), F32),
            states,
            states,
            states,
            pltpu.VMEM((GROUPS, HALVES, state_dim, gw // HALVES), BF16),
            states,
            states,
            queries,
            queries,
            pltpu.VMEM((kv_count, HEAD_SIZE, qw), F32),
            pltpu.VMEM((kv_count, 1, qw), F32),
            pltpu.VMEM((kv_count, 1, qw), F32),
            pltpu.VMEM((kv_count, qw + rows_for(qw // HEAD_SIZE), HEAD_SIZE), BF16),
            pltpu.VMEM((2, qw), F32),
            pltpu.VMEM((HEAD_SIZE, qw), F32),
            dma((9,)),
            dma((8,)),
            dma((max(n // 2 - 3, 1),)),
            dma((max(n // 2 - 3, 1),)),
            dma((kv_count, 1 if n == 8 else max(n // 2 - 2, 1))),
            dma((kv_count, max(n // 2 - 3, 1))),
        ]
        + [dma((GROUPS,))] * 4
        + [dma((2,))],
        compiler_params=pltpu.CompilerParams(
            collective_id=0, has_side_effects=True, vmem_limit_bytes=56 * 1024 * 1024
        ),
    )(
        student_x, student_z, student_b, student_c, step_size, decay_rate[None, :],
        norm_gain[None, :], teacher_q, teacher_k, teacher_v,
    )
    results = [pltpu.with_memory_space_constraint(r, pltpu.VMEM) for r in results]
    return pl.pallas_call(
        store,
        out_shape=(
            jax.ShapeDtypeStruct(student_x.shape, BF16),
            jax.ShapeDtypeStruct(teacher_q.shape, BF16),
        ),
        in_specs=[vmem, vmem],
        out_specs=(hbm, hbm),
        scratch_shapes=[dma((2,))],
    )(*results)


def solution(mesh):
    return jax.shard_map(
        on_device,
        mesh=mesh,
        in_specs=(
            P(("dp", "seq"), None),
            P(("dp", "seq"), None),
            P(("dp", "seq"), None),
            P(("dp", "seq"), None),
            P(None, ("dp", "seq")),
            P(),
            P(),
            P(("dp", "seq"), None),
            P(("dp", "seq"), None),
            P(("dp", "seq"), None),
        ),
        out_specs=(P(("dp", "seq"), None), P(("dp", "seq"), None)),
        check_vma=False,
    )
```

```python
import functools
import math

import jax
import jax.numpy as jnp
from jax import lax
from jax.experimental import pallas as pl
from jax.experimental.pallas import tpu as pltpu
from jax.sharding import PartitionSpec as P

GROUPS = 8
HEAD_SIZE = 128
BLOCK = 128
HALVES = 2
LEAD = 2
LAG = 1
OWN_LAG = 2
PIECES = 3
CUTS = 2
SKIPPED = 1

epsilon_norm = 1e-05
masked_score = -1e30
F32 = jnp.float32
BF16 = jnp.bfloat16
MESH = pl.DeviceIdType.MESH


def dot(a, b, ca=1, cb=0):
    return lax.dot_general(a, b, (((ca,), (cb,)), ((), ())), preferred_element_type=F32)


def rows_for(heads):
    return -(-heads * PIECES // 16) * 16


def kernel(
    n,
    x_hbm, z_hbm, b_hbm, c_hbm, step_hbm, rate_hbm, gain_hbm, q_hbm, k_hbm, v_hbm,
    so_ref, to_ref,
    x_ref, z_ref, b_ref, c_ref, step_ref, rate_ref, gain_ref, q_ref, kv_ref,
    cum_ref, csib_ref, ssm_ref, reach_ref, stl_ref, lout_ref, lsib_ref,
    raw_ref, st_ref, send_ref, out_ref,
    qt_ref, qtail_ref, acc_ref, max_ref, sum_ref, part_ref, stat_ref, tacc_ref,
    in_sem, send_sem, relay_send, spread_send, keys_recv, spread_recv, back_recv,
    state_recv, start_recv, local_recv, once_recv,
):
    me = lax.axis_index("seq")
    core = lax.rem(me, 2)
    chip = me // 2
    chips = n // 2
    sibling = me + 1 - 2 * core
    up = me - 2
    down = me + 2
    has_up = chip > 0
    relay_count = max(chips - 3, 1)
    key_slots = keys_recv.shape[1]
    has_down = chip < chips - 1
    is_tail = chip == chips - 1
    is_helper = chip == chips - 2
    feeds = chip < chips - 2
    relays = jnp.logical_and(has_up, feeds)
    skips = SKIPPED if chips == 4 else 0
    helper = 2 * (chips - 2) + core
    lag = jnp.where(feeds, 0, LAG)

    tokens, width = x_ref.shape
    heads = step_ref.shape[0]
    per_group = heads // GROUPS
    head_width = width // heads
    gw = width // GROUPS
    half_width = gw // HALVES
    state_dim = b_ref.shape[1] // GROUPS
    kv_count = kv_ref.shape[0]
    qw = q_ref.shape[1] // kv_count
    ratio = qw // HEAD_SIZE
    lanes = 128
    pack = lanes // head_width
    pairs = per_group // pack
    half_pairs = pairs // HALVES
    scale = math.log2(math.e) / math.sqrt(HEAD_SIZE)

    def span(g, size):
        return pl.ds(pl.multiple_of(g * size, 128), size)

    def to_seq(device):
        return dict(device_id={"seq": device}, device_id_type=MESH)

    key_loads = []
    for g in range(kv_count):
        for i, source in enumerate((k_hbm, v_hbm)):
            key_loads.append(
                pltpu.make_async_copy(
                    source.at[:, g * HEAD_SIZE : (g + 1) * HEAD_SIZE],
                    kv_ref.at[g, core, chip, i],
                    in_sem.at[0],
                )
            )
    own_keys = kv_ref.at[:, core, chip]
    all_keys = pltpu.make_async_copy(own_keys, own_keys, in_sem.at[0])
    loads = [
        pltpu.make_async_copy(src, dst, in_sem.at[i + 1])
        for i, (src, dst) in enumerate(
            (
                (step_hbm, step_ref), (rate_hbm, rate_ref), (q_hbm, q_ref),
                (b_hbm, b_ref), (c_hbm, c_ref), (x_hbm, x_ref), (z_hbm, z_ref), (gain_hbm, gain_ref),
            )
        )
    ]
    skip_pairs = ((0, helper), (chips - 2, core)) if skips else ()

    barrier = pltpu.get_barrier_semaphore()
    pl.semaphore_signal(barrier, inc=1, **to_seq(sibling))

    @pl.when(has_up)
    def _():
        pl.semaphore_signal(barrier, inc=1, **to_seq(up))

    @pl.when(has_down)
    def _():
        pl.semaphore_signal(barrier, inc=1, **to_seq(down))

    for source, target in skip_pairs:

        @pl.when(chip == source)
        def _():
            pl.semaphore_signal(barrier, inc=1, **to_seq(target))

    loads[0].start()
    loads[1].start()
    for load in key_loads:
        load.start()

    @pl.when(is_tail)
    def _():
        loads[2].start()

    for load in loads[3:]:
        load.start()

    @pl.when(jnp.logical_not(is_tail))
    def _():
        loads[2].start()

    def remote(source, target, sent, got, device):
        return pltpu.make_async_remote_copy(
            src_ref=source, dst_ref=target, send_sem=sent, recv_sem=got, **to_seq(device)
        )

    def key_own(g, device):
        block = kv_ref.at[g, core, chip]
        return remote(block, block, send_sem.at[0], keys_recv.at[g, jnp.minimum(chip, key_slots - 1)], device)

    def key_relay(g, j):
        block = kv_ref.at[g, core, j]
        return remote(block, block, relay_send.at[jnp.minimum(j, relay_count - 1)], keys_recv.at[g, jnp.minimum(j, key_slots - 1)], down)

    def key_all(g):
        blocks = kv_ref.at[g, core, 0 : chips - 2]
        return remote(blocks, blocks, send_sem.at[0], keys_recv.at[g, 0], down)

    def key_lazy(g):
        block = kv_ref.at[g, core, chip]
        return remote(block, block, send_sem.at[1], keys_recv.at[g, jnp.minimum(chip, key_slots - 1)], down)

    def key_side(parity):
        block = kv_ref.at[:, parity, chip]
        return remote(block, block, send_sem.at[2], once_recv.at[0], sibling)

    def key_spread(g, j, parity):
        block = kv_ref.at[g, parity, j]
        return remote(block, block, spread_send.at[j], spread_recv.at[g, j], sibling)

    def key_spread_all(g, parity):
        blocks = kv_ref.at[g, parity, 0 : chips - 2]
        return remote(blocks, blocks, spread_send.at[0], spread_recv.at[g, 0], sibling)

    def cum_side():
        return remote(cum_ref, csib_ref, send_sem.at[3], once_recv.at[1], sibling)

    def query_up(g):
        return remote(qt_ref.at[g], qtail_ref.at[g], send_sem.at[4], back_recv.at[g], up)

    def part_down(g, start, stop):
        block = part_ref.at[g, start:stop]
        return remote(block, block, send_sem.at[4], back_recv.at[g], down)

    def state_down(g):
        return remote(out_ref.at[g], raw_ref.at[g], send_sem.at[5], state_recv.at[g], down)

    def state_side(g, half):
        return remote(send_ref.at[g], st_ref.at[g, half], send_sem.at[6], start_recv.at[g], sibling)

    def local_side(g):
        return remote(lout_ref.at[g], lsib_ref.at[g], send_sem.at[7], local_recv.at[g], sibling)

    def sent(block, semaphore, device):
        remote(block, block, semaphore, once_recv.at[0], device).wait_send()

    all_keys.wait()
    partners = 1 + has_up.astype(jnp.int32) + has_down.astype(jnp.int32)
    for source, _ in skip_pairs:
        partners = partners + (chip == source).astype(jnp.int32)
    pl.semaphore_wait(barrier, partners)

    @pl.when(feeds)
    def _():
        for g in range(LEAD):
            if g < skips:

                @pl.when(chip == 0)
                def _():
                    key_own(g, helper).start()

                @pl.when(has_up)
                def _():
                    key_own(g, down).start()
            else:
                key_own(g, down).start()

    key_side(core).start()
    loads[0].wait()
    loads[1].wait()
    eye = lax.broadcasted_iota(jnp.int32, (heads, heads), 0) == lax.broadcasted_iota(
        jnp.int32, (heads, heads), 1
    )
    rate = jnp.sum(jnp.where(eye, rate_ref[...], 0.0), axis=1, keepdims=True)
    running = -step_ref[...] * rate
    position = lax.broadcasted_iota(jnp.int32, (heads, tokens), 1)
    shift = 1
    while shift < tokens:
        running = running + jnp.where(position >= shift, pltpu.roll(running, shift, 1), 0.0)
        shift *= 2
    cum_ref[...] = running

    cum_side().start()

    def transpose_queries(g):
        for h in range(ratio):
            piece = q_ref[:, pl.ds(pl.multiple_of(g * qw + h * HEAD_SIZE, 128), HEAD_SIZE)]
            qt_ref[g, :, h * HEAD_SIZE : (h + 1) * HEAD_SIZE] = piece.T

    @pl.when(is_tail)
    def _():
        loads[2].wait()

        @pl.loop(0, kv_count)
        def _(g):
            transpose_queries(g)
            query_up(g).start()

    @pl.when(jnp.logical_not(has_up))
    def _():
        raw_ref[...] = jnp.zeros_like(raw_ref)

    for load in loads[3:7]:
        load.wait()

    key_at = lax.broadcasted_iota(jnp.int32, (tokens, tokens), 0)
    query_at = lax.broadcasted_iota(jnp.int32, (tokens, tokens), 1)
    lower = query_at <= key_at
    half = lax.broadcasted_iota(jnp.int32, (tokens, lanes), 1) // head_width
    row_half = lax.broadcasted_iota(jnp.int32, (1, lanes), 1) // head_width
    visible = lax.broadcasted_iota(jnp.int32, (2 * tokens, tokens), 0) <= (
        lax.broadcasted_iota(jnp.int32, (2 * tokens, tokens), 1) + core * tokens
    )

    def mask_last(scores):
        rows = scores.shape[0] // 2
        parts = []
        for parity in range(2):
            seen = visible[parity * tokens : (parity + 1) * tokens]
            part = scores[parity * rows : (parity + 1) * rows]
            parts += [part[: rows - tokens]] if rows > tokens else []
            parts.append(jnp.where(seen, part[rows - tokens :], masked_score))
        return jnp.concatenate(parts, axis=0)

    def columns_of(g, p):
        return pl.ds(pl.multiple_of(g * gw + p * lanes, 128), lanes)

    def student_local(g):
        cum = cum_ref[pl.ds(pl.multiple_of(g * per_group, 8), per_group), :]
        cum_t = cum.T
        tail = jnp.exp(cum[:, tokens - 1 : tokens] - cum)
        b = b_ref[:, span(g, state_dim)]
        b_t = b.T.astype(F32)
        products = dot(c_ref[:, span(g, state_dim)], b, 1, 1)
        for p in range(pairs):
            x = x_ref[:, columns_of(g, p)].astype(F32)
            mixes = []
            adds = []
            sources = []
            reach = None
            for j in range(pack):
                h = p * pack + j
                column = jnp.broadcast_to(cum_t[:, h : h + 1], (tokens, lanes))
                difference = jnp.where(lower, column - cum[h : h + 1, :], masked_score)
                mixes.append((products * jnp.exp(difference)).astype(BF16))
                adds.append((b_t * tail[h : h + 1, :]).astype(BF16))
                sources.append(jnp.where(half == j, x, 0.0).astype(BF16))
                reach = column if j == 0 else jnp.where(half == j, column, reach)
            z = z_ref[:, columns_of(g, p)].astype(F32)
            gate = z / (1.0 + jnp.exp(-z))
            at = slice(p * lanes, (p + 1) * lanes)
            source = jnp.concatenate(sources, axis=0)
            ssm_ref[g, :, at] = gate * dot(jnp.concatenate(mixes, axis=1), source)
            reach_ref[g, :, at] = gate * jnp.exp(reach)
            stl_ref[g, :, at] = dot(jnp.concatenate(adds, axis=1), source)
        lout_ref[g] = stl_ref[g, :, span(1 - core, half_width)].astype(BF16)
        local_side(g).start()

    def chain(g):
        local_side(g).wait_recv()

        @pl.when(has_up)
        def _():
            state_down(g).wait_recv()

        rows = pl.ds(pl.multiple_of(g * per_group, 8), per_group)
        total_own = jnp.exp(cum_ref[rows, tokens - 1 : tokens])
        total_sib = jnp.exp(csib_ref[rows, tokens - 1 : tokens])

        def decay_of(total, p):
            decay = total[p * pack : p * pack + 1, :]
            for j in range(1, pack):
                decay = jnp.where(row_half == j, total[p * pack + j : p * pack + j + 1, :], decay)
            return decay

        for part in range(HALVES):

            @pl.when(core == part)
            def _():
                for i in range(half_pairs):
                    p = part * half_pairs + i
                    at = slice(i * lanes, (i + 1) * lanes)
                    own = (decay_of(total_own, p), stl_ref[g, :, p * lanes : (p + 1) * lanes])
                    other = (decay_of(total_sib, p), lsib_ref[g, :, at].astype(F32))
                    first, second = (own, other) if part == 0 else (other, own)
                    raw = raw_ref[g, :, at]
                    middle = raw.astype(F32) * first[0] + first[1]
                    out_ref[g, :, at] = (middle * second[0] + second[1]).astype(BF16)
                    middle = middle.astype(BF16)
                    st_ref[g, part, :, at] = raw if part == 0 else middle
                    send_ref[g, :, at] = middle if part == 0 else raw

        @pl.when(has_down)
        def _():
            state_down(g).start()

        state_side(g, core).start()

    mean_of = jnp.where(
        lax.broadcasted_iota(jnp.int32, (lanes, lanes), 0) // head_width
        == lax.broadcasted_iota(jnp.int32, (lanes, lanes), 1) // head_width,
        1.0 / head_width,
        0.0,
    ).astype(BF16)

    def student_finish(g):
        state_side(g, 1 - core).wait_recv()
        c = c_ref[:, span(g, state_dim)]
        for part in range(HALVES):
            carried = dot(c, st_ref[g, part])
            for i in range(half_pairs):
                p = part * half_pairs + i
                at = slice(p * lanes, (p + 1) * lanes)
                gated = ssm_ref[g, :, at] + reach_ref[g, :, at] * carried[:, i * lanes : (i + 1) * lanes]
                mean = dot((gated * gated).astype(BF16), mean_of)
                so_ref[:, columns_of(g, p)] = (
                    gated * lax.rsqrt(mean + epsilon_norm) * gain_ref[:, columns_of(g, p)]
                ).astype(BF16)

    def head_at(h):
        return slice(h * HEAD_SIZE, (h + 1) * HEAD_SIZE)

    def pass_over(keys, values, queries, mask=None):
        scores = dot(keys, queries)
        if mask is not None:
            scores = mask(scores)
        top = jnp.max(scores, axis=0, keepdims=True)
        weight = jnp.exp2((scores - top) * scale)
        return top, jnp.sum(weight, axis=0, keepdims=True), dot(values, weight.astype(BF16), 0, 0)

    def join(first, second):
        top = jnp.maximum(first[0], second[0])
        one = jnp.exp2((first[0] - top) * scale)
        two = jnp.exp2((second[0] - top) * scale)
        return top, first[1] * one + second[1] * two, first[2] * one + second[2] * two

    def rows_of(g, kind, start, count):
        taken = kv_ref[g, :, pl.ds(start, count), kind]
        return taken.reshape(2 * count * tokens, HEAD_SIZE)

    def attend_own(g):
        keys = rows_of(g, 0, chip, 1)
        values = rows_of(g, 1, chip, 1)
        for h in range(ratio):
            at = head_at(h)
            max_ref[g, :, at], sum_ref[g, :, at], acc_ref[g, :, at] = pass_over(
                keys, values, qt_ref[g, :, at], mask_last
            )

    def attend_earlier(g):
        @pl.loop(0, chip)
        def _(j):
            keys = rows_of(g, 0, j, 1)
            values = rows_of(g, 1, j, 1)
            for h in range(ratio):
                at = head_at(h)
                held = (max_ref[g, :, at], sum_ref[g, :, at], acc_ref[g, :, at])
                max_ref[g, :, at], sum_ref[g, :, at], acc_ref[g, :, at] = join(
                    held, pass_over(keys, values, qt_ref[g, :, at])
                )

    chunk = max(k for k in range(1, 4) if (chips - 1) % k == 0)
    chunks = (chips - 1) // chunk
    log_rows = rows_for(ratio)

    def attend_tail(g):
        def keep(h, result):
            top, total, acc = result
            part_ref[g, h * HEAD_SIZE : (h + 1) * HEAD_SIZE] = (acc * (1.0 / total)).astype(BF16)
            rest = top * scale + jnp.log2(total)
            pieces = []
            for _ in range(PIECES):
                pieces.append(rest.astype(BF16))
                rest = rest - pieces[-1].astype(F32)
            return pieces

        def send(logs, heads_from, heads_to):
            if heads_to == ratio:
                rows = [piece for pieces in logs for piece in pieces]
                blank = jnp.zeros((log_rows - len(rows), HEAD_SIZE), BF16)
                part_ref[g, ratio * HEAD_SIZE :] = jnp.concatenate(rows + [blank], axis=0)
            part_down(g, heads_from * HEAD_SIZE, heads_to * HEAD_SIZE + (log_rows if heads_to == ratio else 0)).start()

        keys = rows_of(g, 0, 0, chunk)
        values = rows_of(g, 1, 0, chunk)
        logs = []
        for h in range(ratio):
            at = head_at(h)
            result = pass_over(keys, values, qtail_ref[g, :, at])
            if chunks == 1:
                logs.append(keep(h, result))
                if (h + 1) % (ratio // CUTS) == 0:
                    send(logs, h + 1 - ratio // CUTS, h + 1)
            else:
                stat_ref[0:1, at], stat_ref[1:2, at], tacc_ref[:, at] = result
        if chunks > 1:

            @pl.loop(1, chunks)
            def _(k):
                keys = rows_of(g, 0, k * chunk, chunk)
                values = rows_of(g, 1, k * chunk, chunk)
                for h in range(ratio):
                    at = head_at(h)
                    held = (stat_ref[0:1, at], stat_ref[1:2, at], tacc_ref[:, at])
                    stat_ref[0:1, at], stat_ref[1:2, at], tacc_ref[:, at] = join(
                        held, pass_over(keys, values, qtail_ref[g, :, at])
                    )

            for h in range(ratio):
                at = head_at(h)
                logs.append(keep(h, (stat_ref[0:1, at], stat_ref[1:2, at], tacc_ref[:, at])))
            send(logs, 0, ratio)

    def attend_all(g):
        if chunks > 1:
            attend_own(g)
            attend_earlier(g)
            finish_teacher(g)
        else:
            keys = rows_of(g, 0, 0, chunk)
            values = rows_of(g, 1, 0, chunk)
            for h in range(ratio):
                _, total, acc = pass_over(keys, values, qt_ref[g, :, head_at(h)], mask_last)
                write_teacher(g, h, acc * (1.0 / total))

    def write_teacher(g, h, result):
        to_ref[:, pl.ds(pl.multiple_of(g * qw + h * HEAD_SIZE, 128), HEAD_SIZE)] = result.astype(BF16).T

    def finish_teacher(g):
        for h in range(ratio):
            at = head_at(h)
            write_teacher(g, h, acc_ref[g, :, at] * (1.0 / sum_ref[g, :, at]))

    def merge_teacher(g):
        part_down(g, 0, ratio * HEAD_SIZE + log_rows).wait_recv()
        logs = part_ref[g, ratio * HEAD_SIZE :].astype(F32)
        for h in range(ratio):
            at = head_at(h)
            near = max_ref[g, :, at]
            far = logs[h * PIECES : h * PIECES + 1]
            for i in range(1, PIECES):
                far = far + logs[h * PIECES + i : h * PIECES + i + 1]
            top = jnp.maximum(near, far)
            one = jnp.exp2(near - top)
            two = jnp.exp2(far - top)
            inverse = 1.0 / (one + two)
            part = part_ref[g, h * HEAD_SIZE : (h + 1) * HEAD_SIZE].astype(F32)
            write_teacher(g, h, acc_ref[g, :, at] * (one * inverse) + part * (two * inverse))

    def take_keys(g, onward):
        @pl.loop(0, chip)
        def _(i):
            j = chip - 1 - i
            key_relay(g, j).wait_recv()
            if onward:
                key_relay(g, j).start()
            key_spread(g, j, core).start()

    def attend_rest(g):
        @pl.loop(0, chip)
        def _(i):
            key_spread(g, chip - 1 - i, 1 - core).wait_recv()

        attend_earlier(g)
        finish_teacher(g)

    final = GROUPS - 1

    student_local(0)
    cum_side().wait_recv()

    @pl.loop(0, GROUPS + 1)
    def _(r):
        live = r < GROUPS

        @pl.when(relays)
        def _():
            @pl.loop(jnp.where(r == 0, skips, r + 1), jnp.minimum(r + 2, GROUPS))
            def _(g):
                take_keys(g, True)

        @pl.when(jnp.logical_and(live, is_helper))
        def _():
            if key_slots < chips - 2:
                key_all(r).wait_recv()
            else:

                @pl.loop(0, chip)
                def _(i):
                    key_relay(r, chip - 1 - i).wait_recv()

            if chips > 2:
                key_spread_all(r, core).start()

        @pl.when(r < final)
        def _():
            student_local(r + 1)

        @pl.loop(jnp.where(feeds, GROUPS, jnp.maximum(r - lag - 1, 0)), jnp.where(live, jnp.maximum(r - lag, 0), GROUPS))
        def _(g):
            student_finish(g)

        @pl.when(jnp.logical_and(is_tail, r >= 1))
        def _():
            merge_teacher(r - 1)

        @pl.loop(
            jnp.where(live, jnp.maximum(r - lag, 0), GROUPS),
            jnp.where(r < final, jnp.maximum(r - lag + 1, 0), GROUPS),
        )
        def _(g):
            chain(g)

        @pl.loop(jnp.where(feeds, jnp.maximum(r - lag - 1, 0), GROUPS), jnp.where(live, jnp.maximum(r - lag, 0), GROUPS))
        def _(g):
            student_finish(g)

        @pl.when(jnp.logical_and(feeds, r + LEAD < GROUPS))
        def _():
            key_own(r + LEAD, down).start()

        @pl.when(r == 0)
        def _():
            key_side(1 - core).wait_recv()
            loads[7].wait()

            @pl.when(jnp.logical_not(is_tail))
            def _():
                loads[2].wait()

        @pl.when(live)
        def _():
            @pl.when(jnp.logical_not(jnp.logical_or(is_tail, is_helper)))
            def _():
                transpose_queries(r)

            @pl.when(is_helper)
            def _():
                if chips > 2:
                    key_spread_all(r, 1 - core).wait_recv()
                query_up(r).wait_recv()

                attend_tail(r)
                transpose_queries(r)

            @pl.when(jnp.logical_not(is_helper))
            def _():
                attend_own(r)

            @pl.when(is_tail)
            def _():
                for h in range(ratio):
                    at = head_at(h)
                    total = sum_ref[r, :, at]
                    max_ref[r, :, at] = max_ref[r, :, at] * scale + jnp.log2(total)
                    acc_ref[r, :, at] = acc_ref[r, :, at] * (1.0 / total)


            @pl.when(jnp.logical_not(has_up))
            def _():
                @pl.when(jnp.logical_not(is_helper))
                def _():
                    finish_teacher(r)

        @pl.when(is_helper)
        def _():
            @pl.loop(jnp.where(live, jnp.maximum(r - OWN_LAG, 0), GROUPS - OWN_LAG), jnp.where(live, jnp.maximum(r - OWN_LAG + 1, 0), GROUPS))
            def _(g):
                attend_all(g)

    if skips:

        @pl.when(chip == 0)
        def _():
            for g in range(skips):
                key_lazy(g).start()

    @pl.when(relays)
    def _():
        for g in range(skips):
            take_keys(g, False)

        @pl.loop(0, GROUPS)
        def _(g):
            attend_rest(g)

    sent(kv_ref.at[:, core, chip], send_sem.at[2], sibling)
    sent(cum_ref, send_sem.at[3], sibling)
    sent(send_ref, send_sem.at[6], sibling)
    sent(lout_ref, send_sem.at[7], sibling)

    @pl.when(has_down)
    def _():
        sent(out_ref, send_sem.at[5], down)

    @pl.when(feeds)
    def _():
        sent(kv_ref.at[:, core, chip], send_sem.at[0], down)

    if skips:

        @pl.when(chip == 0)
        def _():
            sent(kv_ref.at[0:skips, core, chip], send_sem.at[1], down)

    @pl.when(relays)
    def _():
        @pl.loop(0, chip)
        def _(j):
            sent(kv_ref.at[skips:, core, j], relay_send.at[j], down)
            sent(kv_ref.at[:, core, j], spread_send.at[j], sibling)

    @pl.when(is_helper)
    def _():
        if chips > 2:
            sent(kv_ref.at[:, core, 0 : chips - 2], spread_send.at[0], sibling)
        sent(part_ref, send_sem.at[4], down)

    @pl.when(is_tail)
    def _():
        sent(qt_ref, send_sem.at[4], up)


def store(s_ref, t_ref, s_out, t_out, sem):
    copies = [
        pltpu.make_async_copy(s_ref, s_out, sem.at[0]),
        pltpu.make_async_copy(t_ref, t_out, sem.at[1]),
    ]
    for copy in copies:
        copy.start()
    for copy in copies:
        copy.wait()


def on_device(
    student_x, student_z, student_b, student_c, step_size, decay_rate, norm_gain,
    teacher_q, teacher_k, teacher_v,
):
    n = lax.axis_size("seq")
    tokens, width = student_x.shape
    heads = step_size.shape[0]
    assert tokens == BLOCK and n % 2 == 0 and n >= 4
    gw = width // GROUPS
    state_dim = student_b.shape[1] // GROUPS
    kv_count = teacher_k.shape[1] // HEAD_SIZE
    assert kv_count == GROUPS
    qw = teacher_q.shape[1] // kv_count
    hbm = pl.BlockSpec(memory_space=pl.ANY)
    vmem = pl.BlockSpec(memory_space=pltpu.VMEM)
    dma = pltpu.SemaphoreType.DMA
    states = pltpu.VMEM((GROUPS, state_dim, gw // HALVES), BF16)
    queries = pltpu.VMEM((kv_count, HEAD_SIZE, qw), BF16)
    results = pl.pallas_call(
        functools.partial(kernel, n),
        out_shape=(
            pltpu.VMEM(student_x.shape, BF16),
            pltpu.VMEM(teacher_q.shape, BF16),
        ),
        in_specs=[hbm] * 10,
        out_specs=(vmem, vmem),
        scratch_shapes=[
            pltpu.VMEM(student_x.shape, BF16),
            pltpu.VMEM(student_z.shape, BF16),
            pltpu.VMEM(student_b.shape, BF16),
            pltpu.VMEM(student_c.shape, BF16),
            pltpu.VMEM(step_size.shape, F32),
            pltpu.VMEM((1, heads), F32),
            pltpu.VMEM((1, width), F32),
            pltpu.VMEM(teacher_q.shape, BF16),
            pltpu.VMEM((kv_count, 2, n // 2, 2, tokens, HEAD_SIZE), BF16),
            pltpu.VMEM(step_size.shape, F32),
            pltpu.VMEM(step_size.shape, F32),
            pltpu.VMEM((GROUPS, tokens, gw), F32),
            pltpu.VMEM((GROUPS, tokens, gw), F32),
            pltpu.VMEM((GROUPS, state_dim, gw), F32),
            states,
            states,
            states,
            pltpu.VMEM((GROUPS, HALVES, state_dim, gw // HALVES), BF16),
            states,
            states,
            queries,
            queries,
            pltpu.VMEM((kv_count, HEAD_SIZE, qw), F32),
            pltpu.VMEM((kv_count, 1, qw), F32),
            pltpu.VMEM((kv_count, 1, qw), F32),
            pltpu.VMEM((kv_count, qw + rows_for(qw // HEAD_SIZE), HEAD_SIZE), BF16),
            pltpu.VMEM((2, qw), F32),
            pltpu.VMEM((HEAD_SIZE, qw), F32),
            dma((9,)),
            dma((8,)),
            dma((max(n // 2 - 3, 1),)),
            dma((max(n // 2 - 3, 1),)),
            dma((kv_count, 1 if n == 8 else max(n // 2 - 2, 1))),
            dma((kv_count, max(n // 2 - 3, 1))),
        ]
        + [dma((GROUPS,))] * 4
        + [dma((2,))],
        compiler_params=pltpu.CompilerParams(
            collective_id=0, has_side_effects=True, vmem_limit_bytes=56 * 1024 * 1024
        ),
    )(
        student_x, student_z, student_b, student_c, step_size, decay_rate[None, :],
        norm_gain[None, :], teacher_q, teacher_k, teacher_v,
    )
    results = [pltpu.with_memory_space_constraint(r, pltpu.VMEM) for r in results]
    return pl.pallas_call(
        store,
        out_shape=(
            jax.ShapeDtypeStruct(student_x.shape, BF16),
            jax.ShapeDtypeStruct(teacher_q.shape, BF16),
        ),
        in_specs=[vmem, vmem],
        out_specs=(hbm, hbm),
        scratch_shapes=[dma((2,))],
    )(*results)


def solution(mesh):
    return jax.shard_map(
        on_device,
        mesh=mesh,
        in_specs=(
            P(("dp", "seq"), None),
            P(("dp", "seq"), None),
            P(("dp", "seq"), None),
            P(("dp", "seq"), None),
            P(None, ("dp", "seq")),
            P(),
            P(),
            P(("dp", "seq"), None),
            P(("dp", "seq"), None),
            P(("dp", "seq"), None),
        ),
        out_specs=(P(("dp", "seq"), None), P(("dp", "seq"), None)),
        check_vma=False,
    )
```
